32 devices in a mesh: seq: 8 (over z, x), head: 4 (over y, core).
Axes of the slice: x: 2, y: 2, z: 4, core: 2. Of those that a mesh axis runs over, the one named last changes fastest.
Arguments:
- media: bfloat16 [32768, 1536], P(('seq', 'head')), may hold values from -6 to 6
- media_ids: int32 [32768], P('seq'), may hold values from -1 to 127, as said below
- image_seq: int32 [128], P('seq'), may hold values from 0 to 31, as said below
- image_valid: int32 [128], P('seq'), may hold values from 0 to 1, as said below
- latents: bfloat16 [8192, 1536], P(('seq', 'head')), may hold values from -6 to 6
- w_query: bfloat16 [1536, 1536], P(None, 'head'), may hold values from -0.3125 to 0.3125
- w_key: bfloat16 [1536, 1536], P(None, 'head'), may hold values from -0.15625 to 0.15625
- w_value: bfloat16 [1536, 1536], P(None, 'head'), may hold values from -0.15625 to 0.15625
- w_out: bfloat16 [1536, 1536], P('head'), may hold values from -0.625 to 0.625
- w_up: bfloat16 [1536, 6144], P(None, 'head'), may hold values from -0.15625 to 0.15625
- w_down: bfloat16 [6144, 1536], P('head'), may hold values from -0.078125 to 0.078125
- media_gain: float32 [1536], replicated, may hold values from 0.5 to 1.5
- media_bias: float32 [1536], replicated, may hold values from -1 to 1
- latent_gain: float32 [1536], replicated, may hold values from 0.5 to 1.5
- latent_bias: float32 [1536], replicated, may hold values from -1 to 1
- ffn_gain: float32 [1536], replicated, may hold values from 0.5 to 1.5
- ffn_bias: float32 [1536], replicated, may hold values from -1 to 1
- cotangent: bfloat16 [8192, 1536], P(('seq', 'head')), may hold values from -6 to 6
Outputs:
- latents_out: bfloat16 [8192, 1536], P(('seq', 'head'))
- penalty: float32 [], replicated
- media_grad: bfloat16 [32768, 1536], P(('seq', 'head'))
- latents_grad: bfloat16 [8192, 1536], P(('seq', 'head'))
- w_query_grad: float32 [1536, 1536], P(None, 'head')
- w_key_grad: float32 [1536, 1536], P(None, 'head')
- w_value_grad: float32 [1536, 1536], P(None, 'head')
- w_out_grad: float32 [1536, 1536], P('head')
- w_up_grad: float32 [1536, 6144], P(None, 'head')
- w_down_grad: float32 [6144, 1536], P('head')
- media_gain_grad: float32 [1536], replicated
- media_bias_grad: float32 [1536], replicated
- latent_gain_grad: float32 [1536], replicated
- latent_bias_grad: float32 [1536], replicated
- ffn_gain_grad: float32 [1536], replicated
- ffn_bias_grad: float32 [1536], replicated
The draws below stay inside these ranges and needn't reach their ends.
Inputs may be any that keep to these rules, and one draw needn't show every extreme that they name: `image_seq`: image g goes to one of the 4 sequences of its block: g // 16 * 4 up to that plus 4 - 1. `image_valid`: the first slot of every block of 16 slots is in use. `media_ids`: a row's id is -1 or a slot in use that goes to the row's sequence; every slot in use has one run of one or more rows in its sequence, runs in increasing slot order, pad rows at the end of the sequence; slots not in use have no rows.
All inputs are finite; a program needn't handle non-finite values.
Results may differ from the reference program's by a relative error of at most 0.019.
Values may be sent and summed in bfloat16 or wider, within the bound.
No kernel may reach another device: no remote copies, remote signals or barrier semaphores. Data moves between devices by JAX's collectives and lax.ppermute only.
A program may use at most 320 MiB of HBM per device.

```python
import jax
import jax.numpy as jnp
from jax import lax

D = 1536
HEADS = 16
HEAD_DIM = 96
FF = 6144
LATENTS = 64
LEN = 1024
SEQ_DEV = 4
IMG_DEV = 16
SEQS = 32
ROWS = 32768
IMAGES = 128


def layout(key):
    blocks = IMAGES // IMG_DEV
    slots = jnp.arange(IMAGES, dtype=jnp.int32)
    block_of = slots // IMG_DEV
    within = slots % IMG_DEV
    local_seq = jax.random.randint(jax.random.fold_in(key, 101), (IMAGES,), 0, SEQ_DEV, dtype=jnp.int32)
    local_seq = jnp.where(within == 0, 0, local_seq)
    threshold = 300 + 650 * block_of // max(blocks - 1, 1)
    ticket = jax.random.randint(jax.random.fold_in(key, 102), (IMAGES,), 0, 1000, dtype=jnp.int32)
    valid = jnp.logical_or(ticket < threshold, within == 0).astype(jnp.int32)
    return (local_seq, block_of, valid)


def draw_image_seq(key, part):
    local_seq, block_of, valid = layout(key)
    return (block_of * SEQ_DEV + local_seq).astype(jnp.int32)


def draw_image_valid(key, part):
    local_seq, block_of, valid = layout(key)
    return valid


def draw_media_ids(key, part):
    local_seq, block_of, valid = layout(key)
    seq_number = jnp.arange(SEQS, dtype=jnp.int32)
    seq_block = seq_number // SEQ_DEV
    seq_local = seq_number % SEQ_DEV
    slot_seq = local_seq.reshape(IMAGES // IMG_DEV, IMG_DEV)[seq_block]
    slot_valid = valid.reshape(IMAGES // IMG_DEV, IMG_DEV)[seq_block]
    chosen = jnp.logical_and(slot_seq == seq_local[:, None], slot_valid == 1).astype(jnp.int32)
    lengths = jax.random.randint(jax.random.fold_in(key, 103), (SEQS, IMG_DEV), 1, 8, dtype=jnp.int32) * chosen
    bounds = jnp.cumsum(lengths, axis=1)
    filled = bounds[:, -1]
    padding = jax.random.randint(jax.random.fold_in(key, 104), (SEQS,), 1, 3, dtype=jnp.int32)
    overall = filled + padding
    ticks = jnp.arange(LEN, dtype=jnp.int32)[None, :] * overall[:, None] // LEN
    which = jnp.sum((bounds[:, None, :] <= ticks[:, :, None]).astype(jnp.int32), axis=-1)
    labels = jnp.where(ticks < filled[:, None], seq_block[:, None] * IMG_DEV + which, -1)
    return labels.reshape(SEQS * LEN).astype(jnp.int32)


def block_levels(stream_key, extent, split, least, top_value):
    def one(position, shards_of):
        draws = jax.random.uniform(jax.random.fold_in(jax.random.fold_in(stream_key, 6), position), (shards_of,), jnp.float32, least / len(split), top_value / len(split))
        return jnp.repeat(jnp.exp(draws), extent[position] // shards_of).reshape((-1,) + (1,) * (len(extent) - position - 1))

    level = one(*split[0])
    for cut in split[1:]:
        level = level * one(*cut)
    return level


def normal_values(rng, shape, spread, limit, shards=(), kind=jnp.bfloat16):
    loudness = block_levels(rng, shape, shards, -0.22, 0.18) if shards else 1.0
    values = jax.random.normal(rng, shape, jnp.float32) * spread * loudness
    return jnp.minimum(jnp.maximum(values, -limit), limit).astype(kind)


def setup_inputs(seed: int = 0) -> dict:
    key_list = jax.random.split(jax.random.key(seed), 19)
    return {
        "media": normal_values(key_list[0], (ROWS, D), 1.0, 6.0, ((0, 32),)),
        "media_ids": draw_media_ids(jax.random.fold_in(key_list[18], 71), 0),
        "image_seq": draw_image_seq(jax.random.fold_in(key_list[18], 71), 0),
        "image_valid": draw_image_valid(jax.random.fold_in(key_list[18], 71), 0),
        "latents": normal_values(key_list[4], (IMAGES * LATENTS, D), 1.0, 6.0, ((0, 32),)),
        "w_query": normal_values(key_list[5], (D, HEADS * HEAD_DIM), (D // 4) ** -0.5, 0.3125, ((1, 4),)),
        "w_key": normal_values(key_list[6], (D, HEADS * HEAD_DIM), D ** -0.5, 0.15625, ((1, 4),)),
        "w_value": normal_values(key_list[7], (D, HEADS * HEAD_DIM), D ** -0.5, 0.15625, ((1, 4),)),
        "w_out": normal_values(key_list[8], (HEADS * HEAD_DIM, D), (D // 16) ** -0.5, 0.625, ((0, 4),)),
        "w_up": normal_values(key_list[9], (D, FF), D ** -0.5, 0.15625, ((1, 4),)),
        "w_down": normal_values(key_list[10], (FF, D), FF ** -0.5, 0.078125, ((0, 4),)),
        "media_gain": jnp.clip(1.0 + 0.1 * jax.random.normal(key_list[11], (D,), jnp.float32), 0.5, 1.5),
        "media_bias": normal_values(key_list[12], (D,), 0.2, 1.0, (), jnp.float32),
        "latent_gain": jnp.clip(1.0 + 0.1 * jax.random.normal(key_list[13], (D,), jnp.float32), 0.5, 1.5),
        "latent_bias": normal_values(key_list[14], (D,), 0.2, 1.0, (), jnp.float32),
        "ffn_gain": jnp.clip(1.0 + 0.1 * jax.random.normal(key_list[15], (D,), jnp.float32), 0.5, 1.5),
        "ffn_bias": normal_values(key_list[16], (D,), 0.2, 1.0, (), jnp.float32),
        "cotangent": normal_values(key_list[17], (IMAGES * LATENTS, D), 1.0, 6.0, ((0, 32),)),
    }


epsilon = 1e-05
precise = lax.Precision.HIGHEST

@jax.custom_vjp
def low(v):
    return lax.optimization_barrier(v.astype(jnp.bfloat16)).astype(jnp.float32)

@jax.custom_vjp
def low_back(v):
    return v

def low_keep(v):
    return (low(v), None)

def low_pass(kept, grad):
    return (grad,)

def back_keep(v):
    return (v, None)

def back_low(kept, grad):
    return (low(grad),)
low.defvjp(low_keep, low_pass)
low_back.defvjp(back_keep, back_low)

def layer_norm(row_values, norm_gain, norm_bias):
    row_mean = lax.optimization_barrier(jnp.mean(row_values, axis=-1, keepdims=True))
    centred = row_values - row_mean
    variance = lax.optimization_barrier(jnp.mean(centred * centred, axis=-1, keepdims=True))
    return centred * lax.rsqrt(variance + epsilon) * norm_gain + norm_bias

def matmul(left_side, right_side):
    return jnp.dot(left_side, right_side, precision=precise, preferred_element_type=jnp.float32)

def project(row_values, matrix):
    return low_back(low(matmul(row_values, matrix)))

def block_forward(weights, media_block, latent_block, ids_block, seq_block, valid_block, block_index, pen_scale):
    w_query, w_key, w_value, w_out, w_up, w_down, media_gain, media_bias, latent_gain, latent_bias, ffn_gain, ffn_bias = weights
    media_norm = low(layer_norm(media_block, media_gain, media_bias))
    latent_norm = low(layer_norm(latent_block, latent_gain, latent_bias))
    queries = project(latent_norm, w_query).reshape(IMG_DEV, LATENTS, HEADS, HEAD_DIM)
    key_media = project(media_norm, w_key).reshape(SEQ_DEV, LEN, HEADS, HEAD_DIM)
    value_media = project(media_norm, w_value).reshape(SEQ_DEV, LEN, HEADS, HEAD_DIM)
    key_latent = project(latent_norm, w_key).reshape(IMG_DEV, LATENTS, HEADS, HEAD_DIM)
    value_latent = project(latent_norm, w_value).reshape(IMG_DEV, LATENTS, HEADS, HEAD_DIM)
    local_seq = (seq_block - block_index * SEQ_DEV).astype(jnp.int32)
    key_image = jnp.take(key_media, local_seq, axis=0)
    value_image = jnp.take(value_media, local_seq, axis=0)
    owners = (block_index * IMG_DEV + jnp.arange(IMG_DEV, dtype=jnp.int32)).astype(jnp.int32)
    allowed = jnp.take(ids_block.reshape(SEQ_DEV, LEN), local_seq, axis=0) == owners[:, None]
    score_scale = HEAD_DIM ** (-0.5)
    media_part = low_back(jnp.einsum('gqhe,gkhe->ghqk', queries, key_image, precision=precise) * score_scale)
    latent_part = low_back(jnp.einsum('gqhe,gkhe->ghqk', queries, key_latent, precision=precise) * score_scale)
    media_part = jnp.where(allowed[:, None, None, :], media_part, -1e+30)
    scores = jnp.concatenate([media_part, latent_part], axis=-1)
    log_prob = scores - jax.nn.logsumexp(scores, axis=-1, keepdims=True)
    attn_prob = jnp.exp(log_prob)
    entropy = -lax.optimization_barrier(jnp.sum(attn_prob * log_prob, axis=-1))
    prob_low = low(attn_prob)
    attended = jnp.einsum('ghqk,gkhe->gqhe', prob_low[..., :LEN], value_image, precision=precise)
    attended = attended + jnp.einsum('ghqk,gkhe->gqhe', prob_low[..., LEN:], value_latent, precision=precise)
    attended = low_back(low(attended)).reshape(IMG_DEV * LATENTS, HEADS * HEAD_DIM)
    middle = latent_block + low_back(matmul(attended, w_out))
    ffn_norm = low(layer_norm(middle, ffn_gain, ffn_bias))
    before_gelu = low_back(matmul(ffn_norm, w_up))
    hidden = low(jax.nn.gelu(before_gelu, approximate=False))
    result = middle + low_back(matmul(hidden, w_down))
    weighted = jnp.sum(entropy * valid_block.astype(jnp.float32)[:, None, None])
    return (result, weighted * pen_scale)

def reference(media, media_ids, image_seq, image_valid, latents, w_query, w_key, w_value, w_out, w_up, w_down, media_gain, media_bias, latent_gain, latent_bias, ffn_gain, ffn_bias, cotangent):
    valid_count = jnp.sum(image_valid).astype(jnp.float32)
    pen_scale = 1.0 / (HEADS * LATENTS * valid_count)
    blocks = IMAGES // IMG_DEV
    ids_blocks = media_ids.reshape(blocks, SEQ_DEV * LEN)
    seq_blocks = image_seq.reshape(blocks, IMG_DEV)
    valid_blocks = image_valid.reshape(blocks, IMG_DEV)
    indices = jnp.arange(blocks, dtype=jnp.int32)
    step_function = jax.checkpoint(block_forward)
    penalty_weight = 4.0 * HEADS * LATENTS * IMAGES

    def forward(weights, media_float, latent_float):

        def advance(entropy_sum, inputs):
            media_block, latent_block, ids_block, seq_block, valid_block, block_index = inputs
            result, block_pen = step_function(weights, media_block, latent_block, ids_block, seq_block, valid_block, block_index, pen_scale)
            return (entropy_sum + block_pen, result)
        stacked = (media_float.reshape(blocks, SEQ_DEV * LEN, D), latent_float.reshape(blocks, IMG_DEV * LATENTS, D), ids_blocks, seq_blocks, valid_blocks, indices)
        entropy_sum, results = lax.scan(advance, jnp.zeros((), jnp.float32), stacked)
        return (results.reshape(IMAGES * LATENTS, D), entropy_sum)
    weights = (w_query.astype(jnp.float32), w_key.astype(jnp.float32), w_value.astype(jnp.float32), w_out.astype(jnp.float32), w_up.astype(jnp.float32), w_down.astype(jnp.float32), media_gain, media_bias, latent_gain, latent_bias, ffn_gain, ffn_bias)
    outputs, pullback = jax.vjp(forward, weights, media.astype(jnp.float32), latents.astype(jnp.float32))
    result, penalty = outputs
    weight_grads, media_grad, latent_grad = pullback((cotangent.astype(jnp.float32), jnp.full((), penalty_weight, jnp.float32)))
    return (result.astype(jnp.bfloat16), penalty, media_grad.astype(jnp.bfloat16), latent_grad.astype(jnp.bfloat16), weight_grads[0], weight_grads[1], weight_grads[2], weight_grads[3], weight_grads[4], weight_grads[5], weight_grads[6], weight_grads[7], weight_grads[8], weight_grads[9], weight_grads[10], weight_grads[11])
```

```python
import jax
import jax.numpy as jnp
from jax import lax
from jax.experimental import pallas as pl
from jax.experimental.pallas import tpu as pltpu
from jax.sharding import PartitionSpec as P

HEADS = 16
HEAD_DIM = 96
LATENTS = 64
LEN = 1024
KEY_BLOCK = 256

epsilon = 1e-05
BF16 = jnp.bfloat16
F32 = jnp.float32


def normalize(row_values, norm_gain, norm_bias):
    row_mean = jnp.mean(row_values, axis=-1, keepdims=True)
    centred = row_values - row_mean
    variance = jnp.mean(centred * centred, axis=-1, keepdims=True)
    inverse = lax.rsqrt(variance + epsilon)
    scaled = centred * inverse
    return (scaled * norm_gain + norm_bias, scaled, inverse)


def normalize_back(incoming, scaled, inverse, norm_gain):
    weighted = incoming * norm_gain
    first_mean = jnp.mean(weighted, axis=-1, keepdims=True)
    second_mean = jnp.mean(weighted * scaled, axis=-1, keepdims=True)
    outgoing = inverse * (weighted - first_mean - scaled * second_mean)
    return (outgoing, jnp.sum(incoming * scaled, axis=0), jnp.sum(incoming, axis=0))


def product(left_side, right_side):
    return jnp.dot(left_side, right_side, preferred_element_type=F32)


def contract_rows(left_side, right_side):
    return lax.dot_general(
        left_side, right_side, (((0,), (0,)), ((), ())), preferred_element_type=F32
    )


def contract_cols(left_side, right_side):
    return lax.dot_general(
        left_side, right_side, (((1,), (1,)), ((), ())), preferred_element_type=F32
    )


def gelu_parts(inputs):
    normal_cdf = 0.5 * (1.0 + lax.erf(inputs * 0.7071067811865476))
    density = jnp.exp(-0.5 * inputs * inputs) * 0.3989422804014327
    return (inputs * normal_cdf, normal_cdf + inputs * density)


def block_diagonal(rows, heads):
    lane = lax.broadcasted_iota(jnp.int32, rows.shape, 1)
    parts = []
    for head in range(heads):
        inside = (lane >= head * HEAD_DIM) & (lane < (head + 1) * HEAD_DIM)
        parts.append(jnp.where(inside, rows, jnp.zeros_like(rows)))
    return jnp.concatenate(parts, axis=0)


def take_diagonal(wide, heads):
    lane = lax.broadcasted_iota(jnp.int32, (LATENTS, wide.shape[1]), 1)
    out = wide[:LATENTS]
    for head in range(1, heads):
        out = jnp.where(lane >= head * HEAD_DIM, wide[head * LATENTS : (head + 1) * LATENTS], out)
    return out


def load_keys(kv_hbm, kv_vmem, sems):
    copies = [
        pltpu.make_async_copy(ref, kv_vmem.at[pl.ds(i * LEN, LEN), :], sems.at[i])
        for i, ref in enumerate(kv_hbm)
    ]
    for copy in copies:
        copy.start()
    for copy in copies:
        copy.wait()


def attention_forward(slot, low, high, kv_slots, latent_qkv):
    images = slot.shape[0]
    count = len(kv_slots)
    width = latent_qkv.shape[1] // 3
    heads = width // HEAD_DIM
    rows = heads * LATENTS
    scale = HEAD_DIM ** (-0.5)

    def body(slot_ref, low_ref, high_ref, *refs):
        kv_hbm = refs[:count]
        qkv_ref, out_ref, lse_ref, ent_ref, kv_vmem, scores, sems = refs[count:]
        image = pl.program_id(0)

        @pl.when(image == 0)
        def _():
            load_keys(kv_hbm, kv_vmem, sems)

        base = slot_ref[image] * LEN
        lo = low_ref[image]
        hi = high_ref[image]
        first = lo // KEY_BLOCK
        last = (hi + KEY_BLOCK - 1) // KEY_BLOCK
        query = block_diagonal(qkv_ref[:, :width], heads)
        own = contract_cols(qkv_ref[:, width : 2 * width], query) * scale
        peak = jnp.max(own, axis=0, keepdims=True)

        def first_pass(block, peak):
            at = pl.multiple_of(base + block * KEY_BLOCK, KEY_BLOCK)
            part = contract_cols(kv_vmem[pl.ds(at, KEY_BLOCK), :width], query) * scale
            place = block * KEY_BLOCK + lax.broadcasted_iota(jnp.int32, part.shape, 0)
            part = jnp.where((place >= lo) & (place < hi), part, -1e30)
            to = pl.multiple_of((block - first) * KEY_BLOCK, KEY_BLOCK)
            scores[pl.ds(to, KEY_BLOCK), :] = part
            return jnp.maximum(peak, jnp.max(part, axis=0, keepdims=True))

        peak = lax.fori_loop(first, last, first_pass, peak)
        own = own - peak
        own_exp = jnp.exp(own)
        total = jnp.sum(own_exp, axis=0, keepdims=True)
        moment = jnp.sum(own_exp * own, axis=0, keepdims=True)

        def second_pass(block, carry):
            total, moment = carry
            to = pl.multiple_of((block - first) * KEY_BLOCK, KEY_BLOCK)
            part = scores[pl.ds(to, KEY_BLOCK), :] - peak
            part_exp = jnp.exp(part)
            scores[pl.ds(to, KEY_BLOCK), :] = part_exp
            return (
                total + jnp.sum(part_exp, axis=0, keepdims=True),
                moment + jnp.sum(part_exp * part, axis=0, keepdims=True),
            )

        total, moment = lax.fori_loop(first, last, second_pass, (total, moment))
        inverse = 1.0 / total
        log_total = jnp.log(total)
        lse_ref[0] = peak + log_total
        ent_ref[0] = log_total - moment * inverse
        wide = contract_rows((own_exp * inverse).astype(BF16), qkv_ref[:, 2 * width :])

        def third_pass(block, wide):
            to = pl.multiple_of((block - first) * KEY_BLOCK, KEY_BLOCK)
            at = pl.multiple_of(base + block * KEY_BLOCK, KEY_BLOCK)
            low_prob = (scores[pl.ds(to, KEY_BLOCK), :] * inverse).astype(BF16)
            return wide + contract_rows(low_prob, kv_vmem[pl.ds(at, KEY_BLOCK), width:])

        wide = lax.fori_loop(first, last, third_pass, wide)
        out_ref[...] = take_diagonal(wide, heads).astype(BF16)

    any_spec = pl.BlockSpec(memory_space=pl.ANY)
    return pl.pallas_call(
        body,
        out_shape=(
            jax.ShapeDtypeStruct((images * LATENTS, width), BF16),
            jax.ShapeDtypeStruct((images, 1, rows), F32),
            jax.ShapeDtypeStruct((images, 1, rows), F32),
        ),
        grid_spec=pltpu.PrefetchScalarGridSpec(
            num_scalar_prefetch=3,
            grid=(images,),
            in_specs=[any_spec] * count
            + [pl.BlockSpec((LATENTS, 3 * width), lambda i, *_: (i, 0))],
            out_specs=(
                pl.BlockSpec((LATENTS, width), lambda i, *_: (i, 0)),
                pl.BlockSpec((1, 1, rows), lambda i, *_: (i, 0, 0)),
                pl.BlockSpec((1, 1, rows), lambda i, *_: (i, 0, 0)),
            ),
            scratch_shapes=[
                pltpu.VMEM((count * LEN, 2 * width), BF16),
                pltpu.VMEM((LEN, rows), F32),
                pltpu.SemaphoreType.DMA((count,)),
            ],
        ),
        compiler_params=pltpu.CompilerParams(
            dimension_semantics=("arbitrary",), vmem_limit_bytes=48 << 20
        ),
        name="attention_forward",
    )(slot, low, high, *kv_slots, latent_qkv)


def attention_backward(slot, low, high, weight, kv_slots, latent_qkv, grad_out, lse, entropy):
    images = slot.shape[0]
    count = len(kv_slots)
    width = latent_qkv.shape[1] // 3
    heads = width // HEAD_DIM
    rows = heads * LATENTS
    scale = HEAD_DIM ** (-0.5)

    def body(slot_ref, low_ref, high_ref, weight_ref, *refs):
        kv_hbm = refs[:count]
        qkv_ref, grad_ref, lse_ref, ent_ref = refs[count : count + 4]
        own_out = refs[count + 4]
        key_out = refs[count + 5 : 2 * count + 5]
        kv_vmem, probs, slopes, totals, sems = refs[2 * count + 5 :]
        image = pl.program_id(0)

        @pl.when(image == 0)
        def _():
            load_keys(kv_hbm, kv_vmem, sems)
            totals[...] = jnp.zeros_like(totals)

        base = slot_ref[image] * LEN
        lo = low_ref[image]
        hi = high_ref[image]
        pull = weight_ref[image]
        first = lo // KEY_BLOCK
        last = (hi + KEY_BLOCK - 1) // KEY_BLOCK
        query = block_diagonal(qkv_ref[:, :width], heads)
        grad = block_diagonal(grad_ref[...], heads)
        log_total = lse_ref[0]
        ent = ent_ref[0]
        own_key = qkv_ref[:, width : 2 * width]
        own_log = contract_cols(own_key, query) * scale - log_total
        own_prob = jnp.exp(own_log)
        own_slope = contract_cols(qkv_ref[:, 2 * width :], grad)
        centre = jnp.sum(own_prob * own_slope, axis=0, keepdims=True)
        own_slope = own_slope - pull * (own_log + ent)

        def first_pass(block, centre):
            at = pl.multiple_of(base + block * KEY_BLOCK, KEY_BLOCK)
            to = pl.multiple_of((block - first) * KEY_BLOCK, KEY_BLOCK)
            part = contract_cols(kv_vmem[pl.ds(at, KEY_BLOCK), :width], query) * scale
            place = block * KEY_BLOCK + lax.broadcasted_iota(jnp.int32, part.shape, 0)
            part = jnp.where((place >= lo) & (place < hi), part - log_total, -1e30)
            prob = jnp.exp(part)
            slope = contract_cols(kv_vmem[pl.ds(at, KEY_BLOCK), width:], grad)
            probs[pl.ds(to, KEY_BLOCK), :] = prob
            slopes[pl.ds(to, KEY_BLOCK), :] = slope - pull * (part + ent)
            return centre + jnp.sum(prob * slope, axis=0, keepdims=True)

        centre = lax.fori_loop(first, last, first_pass, centre)
        own_low = (own_prob * (own_slope - centre)).astype(BF16)
        grad_query = contract_rows(own_low, own_key)
        own_out[:, width : 2 * width] = (product(own_low, query) * scale).astype(BF16)
        own_out[:, 2 * width :] = product(own_prob.astype(BF16), grad).astype(BF16)

        def second_pass(block, grad_query):
            at = pl.multiple_of(base + block * KEY_BLOCK, KEY_BLOCK)
            to = pl.multiple_of((block - first) * KEY_BLOCK, KEY_BLOCK)
            prob = probs[pl.ds(to, KEY_BLOCK), :]
            low = (prob * (slopes[pl.ds(to, KEY_BLOCK), :] - centre)).astype(BF16)
            totals[pl.ds(at, KEY_BLOCK), :width] += product(low, query) * scale
            totals[pl.ds(at, KEY_BLOCK), width:] += product(prob.astype(BF16), grad)
            return grad_query + contract_rows(low, kv_vmem[pl.ds(at, KEY_BLOCK), :width])

        grad_query = lax.fori_loop(first, last, second_pass, grad_query)
        own_out[:, :width] = (take_diagonal(grad_query, heads) * scale).astype(BF16)

        @pl.when(image == images - 1)
        def _():
            for i in range(count):
                key_out[i][...] = totals[pl.ds(i * LEN, LEN), :].astype(BF16)

    any_spec = pl.BlockSpec(memory_space=pl.ANY)
    row_spec = pl.BlockSpec((1, 1, rows), lambda i, *_: (i, 0, 0))
    return pl.pallas_call(
        body,
        out_shape=(jax.ShapeDtypeStruct((images * LATENTS, 3 * width), BF16),)
        + (jax.ShapeDtypeStruct((LEN, 2 * width), BF16),) * count,
        grid_spec=pltpu.PrefetchScalarGridSpec(
            num_scalar_prefetch=4,
            grid=(images,),
            in_specs=[any_spec] * count
            + [
                pl.BlockSpec((LATENTS, 3 * width), lambda i, *_: (i, 0)),
                pl.BlockSpec((LATENTS, width), lambda i, *_: (i, 0)),
                row_spec,
                row_spec,
            ],
            out_specs=(pl.BlockSpec((LATENTS, 3 * width), lambda i, *_: (i, 0)),)
            + (pl.BlockSpec((LEN, 2 * width), lambda i, *_: (0, 0)),) * count,
            scratch_shapes=[
                pltpu.VMEM((count * LEN, 2 * width), BF16),
                pltpu.VMEM((LEN, rows), F32),
                pltpu.VMEM((LEN, rows), F32),
                pltpu.VMEM((count * LEN, 2 * width), F32),
                pltpu.SemaphoreType.DMA((count,)),
            ],
        ),
        compiler_params=pltpu.CompilerParams(
            dimension_semantics=("arbitrary",), vmem_limit_bytes=56 << 20
        ),
        name="attention_backward",
    )(slot, low, high, weight, *kv_slots, latent_qkv, grad_out, lse, entropy)


def swap_head(value, bit):
    size = lax.axis_size("head")
    return lax.ppermute(value, "head", [(i, i ^ bit) for i in range(size)])


def swap_seq(value, bit):
    size = lax.axis_size("seq")
    return lax.ppermute(value, "seq", [(i, i ^ bit) for i in range(size)])


def sum_seq(value):
    size = lax.axis_size("seq")
    bit = 1
    while bit < size:
        value = value + swap_seq(value, bit)
        bit *= 2
    return value


def sum_head(value):
    size = lax.axis_size("head")
    bit = 1
    while bit < size:
        value = value + swap_head(value, bit)
        bit *= 2
    return value


def gather_slots(value):
    across = swap_head(value, 2)
    near = swap_head(value, 1)
    return [value, near, across, swap_head(across, 1)]


def scatter_slots(parts):
    far = parts[2] + swap_head(parts[3], 1)
    from_across = swap_head(far, 2)
    near = parts[0] + swap_head(parts[1], 1)
    return near.astype(F32) + from_across.astype(F32)


def half_rows(value, which):
    half = value.shape[0] // 2
    return lax.dynamic_slice_in_dim(value, which * half, half, axis=0)


def join_halves(mine, other, which):
    return jnp.where(
        which == 0,
        jnp.concatenate([mine, other], axis=0),
        jnp.concatenate([other, mine], axis=0),
    )


def sum_rows(value):
    core = lax.axis_index("head") % 2
    mine = half_rows(value, core) + swap_head(half_rows(value, 1 - core), 1)
    mine = mine + swap_head(mine, 2)
    return join_halves(mine, swap_head(mine, 1), core)


def scatter_rows(value):
    head = lax.axis_index("head")
    quarter = value.shape[0] // 4

    def rows(which):
        return lax.dynamic_slice_in_dim(value, which * quarter, quarter, axis=0)

    return scatter_slots([rows(head ^ i) for i in range(4)])


def shards(
    media,
    media_ids,
    image_seq,
    image_valid,
    latents,
    w_query,
    w_key,
    w_value,
    w_out,
    w_up,
    w_down,
    media_gain,
    media_bias,
    latent_gain,
    latent_bias,
    ffn_gain,
    ffn_bias,
    cotangent,
):
    seq_index = lax.axis_index("seq")
    head_index = lax.axis_index("head")
    images = image_seq.shape[0]
    sequences = media_ids.shape[0] // LEN
    own_rows = latents.shape[0]
    inner_width = w_query.shape[1]
    quad = lax.axis_size("head") == 4 and media.shape[0] == LEN
    seq_size = lax.axis_size("seq")
    valid_float = image_valid.astype(F32)

    media_norm, media_hat, media_inv = normalize(media.astype(F32), media_gain, media_bias)
    latent_rows = lax.all_gather(latents, "head", axis=0, tiled=True)
    if quad:
        media_slots = gather_slots(media_norm.astype(BF16))
    else:
        media_all = lax.all_gather(media_norm.astype(BF16), "head", axis=0, tiled=True)
        media_slots = [media_all[i * LEN : (i + 1) * LEN] for i in range(sequences)]
    grad_all = lax.all_gather(cotangent, "head", axis=0, tiled=True)
    latent_float = latent_rows.astype(F32)
    latent_norm, latent_hat, latent_inv = normalize(latent_float, latent_gain, latent_bias)
    latent_low = latent_norm.astype(BF16)

    count_all = jnp.sum(valid_float).reshape(1, 1)
    count_all = sum_seq(jnp.broadcast_to(count_all, (8, 128)))[0, 0]
    pen_scale = 1.0 / (HEADS * LATENTS * count_all)
    weighted_scale = 4.0 * images * seq_size / count_all

    owners = seq_index * images + jnp.arange(images, dtype=jnp.int32)
    local_seq = image_seq - seq_index * sequences
    matches = media_ids[None, :] == owners[:, None]
    place = jnp.arange(media_ids.shape[0], dtype=jnp.int32)[None, :]
    run = jnp.sum(matches.astype(jnp.int32), axis=1)
    start = jnp.min(jnp.where(matches, place, media_ids.shape[0]), axis=1)
    low = jnp.where(run > 0, start - local_seq * LEN, 0)
    high = low + run
    slot = local_seq ^ head_index if quad else local_seq

    w_kv = jnp.concatenate([w_key, w_value], axis=1)
    w_qkv = jnp.concatenate([w_query, w_kv], axis=1)
    latent_qkv = product(latent_low, w_qkv).astype(BF16)
    kv_slots = [product(rows, w_kv).astype(BF16) for rows in media_slots]
    attended, lse, entropy = attention_forward(slot, low, high, kv_slots, latent_qkv)

    if quad:
        attended_all = jnp.concatenate(gather_slots(attended), axis=1)
        w_out_all = jnp.concatenate(gather_slots(w_out), axis=0)
        branch = product(attended_all, w_out_all)
    else:
        branch = lax.psum(product(attended, w_out).astype(BF16), "head").astype(F32)
    middle = latent_float + branch
    ffn_norm, ffn_hat, ffn_inv = normalize(middle, ffn_gain, ffn_bias)
    ffn_low = ffn_norm.astype(BF16)
    before_gelu = product(ffn_low, w_up)
    activated, gelu_slope = gelu_parts(before_gelu)
    hidden = activated.astype(BF16)
    grad_before = (contract_cols(grad_all, w_down) * gelu_slope).astype(BF16)
    grad_ffn_part = contract_cols(grad_before, w_up).astype(BF16)
    if quad:
        grad_ffn = sum_rows(grad_ffn_part).astype(F32)
    else:
        grad_ffn = lax.psum(grad_ffn_part, "head").astype(F32)
    down_grad = contract_rows(hidden, grad_all).astype(BF16)
    up_grad = contract_rows(ffn_low, grad_before).astype(BF16)
    up_grad, down_grad = lax.psum((up_grad, down_grad), "seq")

    ffn_branch = product(hidden, w_down).astype(BF16)
    if quad:
        ffn_branch = scatter_rows(ffn_branch)
    else:
        ffn_branch = lax.psum_scatter(ffn_branch, "head", scatter_dimension=0, tiled=True)

    def own(value):
        return lax.dynamic_slice_in_dim(value, head_index * own_rows, own_rows, axis=0)

    result = (own(middle) + ffn_branch.astype(F32)).astype(BF16)

    middle_part, ffn_gain_part, ffn_bias_part = normalize_back(
        grad_ffn, ffn_hat, ffn_inv, ffn_gain
    )
    grad_middle = grad_all.astype(F32) + middle_part
    grad_branch = grad_middle.astype(BF16)
    grad_attended = contract_cols(grad_branch, w_out).astype(BF16)
    out_grad = contract_rows(attended, grad_branch)
    back = attention_backward(
        slot,
        low,
        high,
        valid_float * weighted_scale,
        kv_slots,
        latent_qkv,
        grad_attended,
        lse,
        entropy,
    )
    latent_back, kv_back = back[0], back[1:]

    order = [3, 2, 1, 0] if quad else list(range(len(kv_back)))
    grad_media = {i: contract_cols(kv_back[i], w_kv).astype(BF16) for i in order}
    if quad:
        grad_media_norm = scatter_slots([grad_media[i] for i in range(4)])
    else:
        grad_media_norm = lax.psum_scatter(
            jnp.concatenate([grad_media[i] for i in range(sequences)], axis=0),
            "head",
            scatter_dimension=0,
            tiled=True,
        ).astype(F32)
    grad_latent_part = contract_cols(latent_back, w_qkv).astype(BF16)
    if quad:
        grad_latent_norm = scatter_rows(grad_latent_part)
    else:
        grad_latent_norm = lax.psum_scatter(
            grad_latent_part, "head", scatter_dimension=0, tiled=True
        ).astype(F32)
    latent_grads = contract_rows(latent_low, latent_back)
    kv_grads = latent_grads[:, inner_width:]
    for rows, back_rows in zip(media_slots, kv_back):
        kv_grads = kv_grads + contract_rows(rows, back_rows)
    late = (
        latent_grads[:, :inner_width].astype(BF16),
        kv_grads.astype(BF16),
        out_grad.astype(BF16),
    )
    up_grad, down_grad, *late = lax.optimization_barrier((up_grad, down_grad) + late)
    query_grad, kv_grads, out_grad = lax.psum(tuple(late), "seq")

    media_rows_grad, media_gain_part, media_bias_part = normalize_back(
        grad_media_norm, media_hat, media_inv, media_gain
    )
    latent_part, latent_gain_part, latent_bias_part = normalize_back(
        grad_latent_norm, own(latent_hat), own(latent_inv), latent_gain
    )
    latents_grad = (own(grad_middle) + latent_part).astype(BF16)
    entropy_local = jnp.sum(entropy.reshape(images, -1) * valid_float[:, None])
    share = 1.0 / lax.axis_size("head")
    sums = jnp.stack(
        [
            media_gain_part,
            media_bias_part,
            latent_gain_part,
            latent_bias_part,
            ffn_gain_part * share,
            ffn_bias_part * share,
            jnp.broadcast_to(entropy_local, media_gain.shape),
            jnp.zeros_like(media_gain),
        ]
    )
    sums = sum_seq(sum_head(sums))
    return (
        result,
        sums[6, 0] * pen_scale,
        media_rows_grad.astype(BF16),
        latents_grad,
        query_grad.astype(F32),
        kv_grads[:, :inner_width].astype(F32),
        kv_grads[:, inner_width:].astype(F32),
        out_grad.astype(F32),
        up_grad.astype(F32),
        down_grad.astype(F32),
        sums[0],
        sums[1],
        sums[2],
        sums[3],
        sums[4],
        sums[5],
    )


def solution(mesh):
    rows = P(("seq", "head"), None)
    columns = P(None, "head")
    lines = P("head", None)
    return jax.shard_map(
        shards,
        mesh=mesh,
        in_specs=(
            (rows, P("seq"), P("seq"), P("seq"), rows)
            + (columns, columns, columns, lines, columns, lines)
            + (P(),) * 6
            + (rows,)
        ),
        out_specs=(
            (rows, P(), rows, rows)
            + (columns, columns, columns, lines, columns, lines)
            + (P(),) * 6
        ),
        check_vma=False,
    )
```

```python
import jax
import jax.numpy as jnp
from jax import lax
from jax.experimental import pallas as pl
from jax.experimental.pallas import tpu as pltpu
from jax.sharding import PartitionSpec as P

HEADS = 16
HEAD_DIM = 96
LATENTS = 64
LEN = 1024
KEY_BLOCK = 256

epsilon = 1e-05
BF16 = jnp.bfloat16


def cost(microseconds):
    return pl.CostEstimate(
        flops=int(microseconds * 1.1e9), transcendentals=0, bytes_accessed=int(microseconds * 3e6)
    )


F32 = jnp.float32


def normalize(row_values, norm_gain, norm_bias):
    row_mean = jnp.mean(row_values, axis=-1, keepdims=True)
    centred = row_values - row_mean
    variance = jnp.mean(centred * centred, axis=-1, keepdims=True)
    inverse = lax.rsqrt(variance + epsilon)
    scaled = centred * inverse
    return (scaled * norm_gain + norm_bias, scaled, inverse)


def normalize_back(incoming, scaled, inverse, norm_gain):
    weighted = incoming * norm_gain
    first_mean = jnp.mean(weighted, axis=-1, keepdims=True)
    second_mean = jnp.mean(weighted * scaled, axis=-1, keepdims=True)
    outgoing = inverse * (weighted - first_mean - scaled * second_mean)
    return (outgoing, jnp.sum(incoming * scaled, axis=0), jnp.sum(incoming, axis=0))


def product(left_side, right_side):
    return jnp.dot(left_side, right_side, preferred_element_type=F32)


def contract_rows(left_side, right_side):
    return lax.dot_general(
        left_side, right_side, (((0,), (0,)), ((), ())), preferred_element_type=F32
    )


def contract_cols(left_side, right_side):
    return lax.dot_general(
        left_side, right_side, (((1,), (1,)), ((), ())), preferred_element_type=F32
    )


def gelu_parts(inputs):
    normal_cdf = 0.5 * (1.0 + lax.erf(inputs * 0.7071067811865476))
    density = jnp.exp(-0.5 * inputs * inputs) * 0.3989422804014327
    return (inputs * normal_cdf, normal_cdf + inputs * density)


def block_diagonal(rows, heads):
    lane = lax.broadcasted_iota(jnp.int32, rows.shape, 1)
    parts = []
    for head in range(heads):
        inside = (lane >= head * HEAD_DIM) & (lane < (head + 1) * HEAD_DIM)
        parts.append(jnp.where(inside, rows, jnp.zeros_like(rows)))
    return jnp.concatenate(parts, axis=0)


def take_diagonal(wide, heads):
    lane = lax.broadcasted_iota(jnp.int32, (LATENTS, wide.shape[1]), 1)
    out = wide[:LATENTS]
    for head in range(1, heads):
        out = jnp.where(lane >= head * HEAD_DIM, wide[head * LATENTS : (head + 1) * LATENTS], out)
    return out


def load_keys(kv_hbm, kv_vmem, sems):
    copies = []
    at = 0
    for i, ref in enumerate(kv_hbm):
        size = ref.shape[0]
        copies.append(pltpu.make_async_copy(ref, kv_vmem.at[pl.ds(at, size), :], sems.at[i]))
        at += size
    for copy in copies:
        copy.start()
    for copy in copies:
        copy.wait()


def attention_forward(
    slot, low, high, kv_slots, latent_qkv, offset=0, before=None, time=15.0
):
    images = slot.shape[0]
    count = len(kv_slots)
    keys = sum(kv.shape[0] for kv in kv_slots)
    slots = keys // LEN
    width = latent_qkv.shape[1] // 3
    heads = width // HEAD_DIM
    rows = heads * LATENTS
    scale = HEAD_DIM ** (-0.5)
    given = () if before is None else tuple(before)

    def body(slot_ref, low_ref, high_ref, *refs):
        kv_hbm = refs[:count]
        qkv_ref = refs[count]
        given_refs = refs[count + 1 : count + 1 + len(given)]
        out_ref, lse_ref, ent_ref, kv_vmem, scores, sems = refs[count + 1 + len(given) :]
        image = pl.program_id(0)

        @pl.when(image == 0)
        def _():
            load_keys(kv_hbm, kv_vmem, sems)

        place = slot_ref[image] - offset
        here = (place >= 0) & (place < slots)

        @pl.when(here)
        def _():
            base = place * LEN
            lo = low_ref[image]
            hi = high_ref[image]
            first = lo // KEY_BLOCK
            last = (hi + KEY_BLOCK - 1) // KEY_BLOCK
            query = block_diagonal(qkv_ref[:, :width], heads)
            own = contract_cols(qkv_ref[:, width : 2 * width], query) * scale
            peak = jnp.max(own, axis=0, keepdims=True)

            def first_pass(block, peak):
                at = pl.multiple_of(base + block * KEY_BLOCK, KEY_BLOCK)
                part = contract_cols(kv_vmem[pl.ds(at, KEY_BLOCK), :width], query) * scale
                key = block * KEY_BLOCK + lax.broadcasted_iota(jnp.int32, part.shape, 0)
                part = jnp.where((key >= lo) & (key < hi), part, -1e30)
                to = pl.multiple_of((block - first) * KEY_BLOCK, KEY_BLOCK)
                scores[pl.ds(to, KEY_BLOCK), :] = part
                return jnp.maximum(peak, jnp.max(part, axis=0, keepdims=True))

            peak = lax.fori_loop(first, last, first_pass, peak)
            own = own - peak
            own_exp = jnp.exp(own)
            total = jnp.sum(own_exp, axis=0, keepdims=True)
            moment = jnp.sum(own_exp * own, axis=0, keepdims=True)

            def second_pass(block, carry):
                total, moment = carry
                to = pl.multiple_of((block - first) * KEY_BLOCK, KEY_BLOCK)
                part = scores[pl.ds(to, KEY_BLOCK), :] - peak
                part_exp = jnp.exp(part)
                scores[pl.ds(to, KEY_BLOCK), :] = part_exp
                return (
                    total + jnp.sum(part_exp, axis=0, keepdims=True),
                    moment + jnp.sum(part_exp * part, axis=0, keepdims=True),
                )

            total, moment = lax.fori_loop(first, last, second_pass, (total, moment))
            inverse = 1.0 / total
            log_total = jnp.log(total)
            lse_ref[0] = peak + log_total
            ent_ref[0] = log_total - moment * inverse
            wide = contract_rows((own_exp * inverse).astype(BF16), qkv_ref[:, 2 * width :])

            def third_pass(block, wide):
                to = pl.multiple_of((block - first) * KEY_BLOCK, KEY_BLOCK)
                at = pl.multiple_of(base + block * KEY_BLOCK, KEY_BLOCK)
                low_prob = (scores[pl.ds(to, KEY_BLOCK), :] * inverse).astype(BF16)
                return wide + contract_rows(low_prob, kv_vmem[pl.ds(at, KEY_BLOCK), width:])

            wide = lax.fori_loop(first, last, third_pass, wide)
            out_ref[...] = take_diagonal(wide, heads).astype(BF16)

        @pl.when(jnp.logical_not(here))
        def _():
            if given:
                out_ref[...] = given_refs[0][...]
                lse_ref[...] = given_refs[1][...]
                ent_ref[...] = given_refs[2][...]
            else:
                out_ref[...] = jnp.zeros_like(out_ref)
                lse_ref[...] = jnp.zeros_like(lse_ref)
                ent_ref[...] = jnp.zeros_like(ent_ref)

    any_spec = pl.BlockSpec(memory_space=pl.ANY)
    results = (
        pl.BlockSpec((LATENTS, width), lambda i, *_: (i, 0)),
        pl.BlockSpec((1, 1, rows), lambda i, *_: (i, 0, 0)),
        pl.BlockSpec((1, 1, rows), lambda i, *_: (i, 0, 0)),
    )
    return pl.pallas_call(
        body,
        out_shape=(
            jax.ShapeDtypeStruct((images * LATENTS, width), BF16),
            jax.ShapeDtypeStruct((images, 1, rows), F32),
            jax.ShapeDtypeStruct((images, 1, rows), F32),
        ),
        grid_spec=pltpu.PrefetchScalarGridSpec(
            num_scalar_prefetch=3,
            grid=(images,),
            in_specs=[any_spec] * count
            + [pl.BlockSpec((LATENTS, 3 * width), lambda i, *_: (i, 0))]
            + list(results[: len(given)]),
            out_specs=results,
            scratch_shapes=[
                pltpu.VMEM((keys, 2 * width), BF16),
                pltpu.VMEM((LEN, rows), F32),
                pltpu.SemaphoreType.DMA((count,)),
            ],
        ),
        compiler_params=pltpu.CompilerParams(
            dimension_semantics=("arbitrary",), vmem_limit_bytes=48 << 20
        ),
        cost_estimate=cost(time),
        name="attention_forward",
    )(slot, low, high, *kv_slots, latent_qkv, *given)


def attention_backward(slot, low, high, weight, kv_slots, latent_qkv, grad_out, lse, entropy):
    images = slot.shape[0]
    count = len(kv_slots)
    keys = sum(kv.shape[0] for kv in kv_slots)
    width = latent_qkv.shape[1] // 3
    heads = width // HEAD_DIM
    rows = heads * LATENTS
    scale = HEAD_DIM ** (-0.5)

    def body(slot_ref, low_ref, high_ref, weight_ref, *refs):
        kv_hbm = refs[:count]
        qkv_ref, grad_ref, lse_ref, ent_ref = refs[count : count + 4]
        own_out = refs[count + 4]
        key_out, kv_vmem, probs, slopes, totals, sems = refs[count + 5 :]
        image = pl.program_id(0)

        @pl.when(image == 0)
        def _():
            load_keys(kv_hbm, kv_vmem, sems)
            totals[...] = jnp.zeros_like(totals)

        base = slot_ref[image] * LEN
        lo = low_ref[image]
        hi = high_ref[image]
        pull = weight_ref[image]
        first = lo // KEY_BLOCK
        last = (hi + KEY_BLOCK - 1) // KEY_BLOCK
        query = block_diagonal(qkv_ref[:, :width], heads)
        grad = block_diagonal(grad_ref[...], heads)
        log_total = lse_ref[0]
        ent = ent_ref[0]
        own_key = qkv_ref[:, width : 2 * width]
        own_log = contract_cols(own_key, query) * scale - log_total
        own_prob = jnp.exp(own_log)
        own_slope = contract_cols(qkv_ref[:, 2 * width :], grad)
        centre = jnp.sum(own_prob * own_slope, axis=0, keepdims=True)
        own_slope = own_slope - pull * (own_log + ent)

        def first_pass(block, centre):
            at = pl.multiple_of(base + block * KEY_BLOCK, KEY_BLOCK)
            to = pl.multiple_of((block - first) * KEY_BLOCK, KEY_BLOCK)
            part = contract_cols(kv_vmem[pl.ds(at, KEY_BLOCK), :width], query) * scale
            place = block * KEY_BLOCK + lax.broadcasted_iota(jnp.int32, part.shape, 0)
            part = jnp.where((place >= lo) & (place < hi), part - log_total, -1e30)
            prob = jnp.exp(part)
            slope = contract_cols(kv_vmem[pl.ds(at, KEY_BLOCK), width:], grad)
            probs[pl.ds(to, KEY_BLOCK), :] = prob
            slopes[pl.ds(to, KEY_BLOCK), :] = slope - pull * (part + ent)
            return centre + jnp.sum(prob * slope, axis=0, keepdims=True)

        centre = lax.fori_loop(first, last, first_pass, centre)
        own_low = (own_prob * (own_slope - centre)).astype(BF16)
        grad_query = contract_rows(own_low, own_key)
        own_out[:, width : 2 * width] = (product(own_low, query) * scale).astype(BF16)
        own_out[:, 2 * width :] = product(own_prob.astype(BF16), grad).astype(BF16)

        def second_pass(block, grad_query):
            at = pl.multiple_of(base + block * KEY_BLOCK, KEY_BLOCK)
            to = pl.multiple_of((block - first) * KEY_BLOCK, KEY_BLOCK)
            prob = probs[pl.ds(to, KEY_BLOCK), :]
            low = (prob * (slopes[pl.ds(to, KEY_BLOCK), :] - centre)).astype(BF16)
            totals[pl.ds(at, KEY_BLOCK), :width] += product(low, query) * scale
            totals[pl.ds(at, KEY_BLOCK), width:] += product(prob.astype(BF16), grad)
            return grad_query + contract_rows(low, kv_vmem[pl.ds(at, KEY_BLOCK), :width])

        grad_query = lax.fori_loop(first, last, second_pass, grad_query)
        own_out[:, :width] = (take_diagonal(grad_query, heads) * scale).astype(BF16)

        @pl.when(image == images - 1)
        def _():
            key_out[...] = totals[...].astype(BF16)

    any_spec = pl.BlockSpec(memory_space=pl.ANY)
    row_spec = pl.BlockSpec((1, 1, rows), lambda i, *_: (i, 0, 0))
    return pl.pallas_call(
        body,
        out_shape=(
            jax.ShapeDtypeStruct((images * LATENTS, 3 * width), BF16),
            jax.ShapeDtypeStruct((keys, 2 * width), BF16),
        ),
        grid_spec=pltpu.PrefetchScalarGridSpec(
            num_scalar_prefetch=4,
            grid=(images,),
            in_specs=[any_spec] * count
            + [
                pl.BlockSpec((LATENTS, 3 * width), lambda i, *_: (i, 0)),
                pl.BlockSpec((LATENTS, width), lambda i, *_: (i, 0)),
                row_spec,
                row_spec,
            ],
            out_specs=(
                pl.BlockSpec((LATENTS, 3 * width), lambda i, *_: (i, 0)),
                pl.BlockSpec((keys, 2 * width), lambda i, *_: (0, 0)),
            ),
            scratch_shapes=[
                pltpu.VMEM((keys, 2 * width), BF16),
                pltpu.VMEM((LEN, rows), F32),
                pltpu.VMEM((LEN, rows), F32),
                pltpu.VMEM((keys, 2 * width), F32),
                pltpu.SemaphoreType.DMA((count,)),
            ],
        ),
        compiler_params=pltpu.CompilerParams(
            dimension_semantics=("arbitrary",), vmem_limit_bytes=56 << 20
        ),
        cost_estimate=cost(30.0),
        name="attention_backward",
    )(slot, low, high, weight, *kv_slots, latent_qkv, grad_out, lse, entropy)


ROW_BLOCK = 256


def call(body, grid, inputs, outputs, name, time=5.0, scratch=()):
    return pl.pallas_call(
        body,
        out_shape=tuple(jax.ShapeDtypeStruct(shape, dtype) for shape, dtype, _ in outputs),
        grid=(grid,),
        in_specs=[spec for _, spec in inputs],
        out_specs=tuple(spec for _, _, spec in outputs),
        scratch_shapes=list(scratch),
        compiler_params=pltpu.CompilerParams(
            dimension_semantics=("arbitrary",), vmem_limit_bytes=56 << 20
        ),
        cost_estimate=cost(time),
        name=name,
    )(*[value for value, _ in inputs])


def by_rows(width, move=lambda i: i, size=ROW_BLOCK):
    return pl.BlockSpec((size, width), lambda i: (move(i), 0))


def whole(value):
    return pl.BlockSpec(value.shape, lambda i: (0,) * value.ndim, pipeline_mode=pl.Buffered(1))


def low_half(i):
    return jnp.minimum(i, 1)


def high_half(i):
    return jnp.maximum(i - 2, 0)


def pair_inputs(pair, rest):
    return [(pair, by_rows(pair.shape[1], low_half)), (rest, by_rows(rest.shape[1], high_half))]


def pick(pair_ref, rest_ref):
    return jnp.where(pl.program_id(0) < 2, pair_ref[...], rest_ref[...])


def put_halves(low_ref, high_ref, value):
    @pl.when(pl.program_id(0) < 2)
    def _():
        low_ref[...] = value

    @pl.when(pl.program_id(0) >= 2)
    def _():
        high_ref[...] = value


def half_outputs(width):
    return [
        ((2 * ROW_BLOCK, width), BF16, by_rows(width, low_half)),
        ((2 * ROW_BLOCK, width), BF16, by_rows(width, high_half)),
    ]


def add_up(ref, value):
    total = jnp.sum(value, axis=0, keepdims=True)

    @pl.when(pl.program_id(0) == 0)
    def _():
        ref[...] = total

    @pl.when(pl.program_id(0) > 0)
    def _():
        ref[...] += total


def sum_output(width):
    return ((1, width), F32, pl.BlockSpec((1, width), lambda i: (0, 0)))


def norm_project(rows, gain, bias, weights, time=7.5):
    width, wide = rows[0].shape[1], weights.shape[1]
    count = sum(part.shape[0] for part in rows)

    def body(*refs):
        if len(rows) == 2:
            value = pick(refs[0], refs[1])
        else:
            value = refs[0][...]
        gain_ref, bias_ref, weight_ref, out_ref, norm_ref = refs[len(rows) :]
        norm = normalize(value.astype(F32), gain_ref[...], bias_ref[...])[0].astype(BF16)
        norm_ref[...] = norm
        out_ref[...] = product(norm, weight_ref[...]).astype(BF16)

    first = pair_inputs(*rows) if len(rows) == 2 else [(rows[0], by_rows(width))]
    return call(
        body,
        count // ROW_BLOCK,
        first + [(gain, whole(gain)), (bias, whole(bias)), (weights, whole(weights))],
        [((count, wide), BF16, by_rows(wide)), ((count, width), BF16, by_rows(width))],
        "norm_project",
        time,
    )


def cotangent_down(pair, rest, weights):
    wide = weights.shape[0]

    def body(pair_ref, rest_ref, weight_ref, out_ref):
        out_ref[...] = contract_cols(pick(pair_ref, rest_ref), weight_ref[...])

    return call(
        body,
        4,
        pair_inputs(pair, rest) + [(weights, whole(weights))],
        [((4 * ROW_BLOCK, wide), F32, by_rows(wide))],
        "cotangent_down",
        10.0,
    )[0]


def feed_forward(attended, out_weights, latent_rows, pulled, w_up, gain, bias):
    width = attended[0].shape[1]
    dim = w_up.shape[0]
    wide = w_up.shape[1]

    def body(*refs):
        own, near, across, beyond, first_ref, second_ref, lat_ref, lat_rest, pulled_ref = refs[:9]
        up_ref, gain_ref, bias_ref, middle_ref, ffn_ref, hidden_ref, grad_ref, low_ref, high_ref = (
            refs[9:]
        )
        rows = pick(lat_ref, lat_rest).astype(F32)
        rows = rows + product(jnp.concatenate([own[...], near[...]], axis=1), first_ref[...])
        rows = rows + product(jnp.concatenate([across[...], beyond[...]], axis=1), second_ref[...])
        middle_ref[...] = rows
        norm = normalize(rows, gain_ref[...], bias_ref[...])[0].astype(BF16)
        ffn_ref[...] = norm
        step = wide // 3
        for i in range(3):
            at = slice(i * step, (i + 1) * step)
            activated, slope = gelu_parts(product(norm, up_ref[:, at]))
            hidden_ref[:, at] = activated.astype(BF16)
            grad_ref[:, at] = (pulled_ref[:, at] * slope).astype(BF16)
        back = contract_cols(grad_ref[...], up_ref[...]).astype(BF16)
        put_halves(low_ref, high_ref, back)

    count = 4 * ROW_BLOCK
    return call(
        body,
        4,
        [
            (attended[0], by_rows(width)),
            (attended[1], by_rows(width, lambda i: i ^ 2)),
            (attended[2], by_rows(width, lambda i: i ^ 1)),
            (attended[3], by_rows(width, lambda i: i ^ 3)),
            (out_weights[0], whole(out_weights[0])),
            (out_weights[1], whole(out_weights[1])),
        ]
        + pair_inputs(*latent_rows)
        + [
            (pulled, by_rows(wide)),
            (w_up, whole(w_up)),
            (gain, whole(gain)),
            (bias, whole(bias)),
        ],
        [
            ((count, dim), F32, by_rows(dim)),
            ((count, dim), BF16, by_rows(dim)),
            ((count, wide), BF16, by_rows(wide)),
            ((count, wide), BF16, by_rows(wide)),
        ]
        + half_outputs(dim),
        "feed_forward",
        27.0,
    )


def part(value, rows=None, at=0, columns=slice(None)):
    return (value, value.shape[0] if rows is None else rows, at, columns)


def weight_grad(pairs, start, size, block=256, time=6.0):
    inputs = []
    for left, rights in pairs:
        inputs.append(
            (left, pl.BlockSpec((left.shape[0], block), lambda i: (0, i + start // block)))
        )
        for value, rows, at, _ in rights:
            spec = pl.BlockSpec(
                (rows, value.shape[1]), lambda i, at=at: (at, 0), pipeline_mode=pl.Buffered(1)
            )
            inputs.append((value, spec))
    value, _, _, columns = pairs[0][1][0]
    wide = len(range(*columns.indices(value.shape[1])))

    def body(*refs):
        total = None
        index = 0
        for left, rights in pairs:
            left_ref = refs[index]
            row = 0
            for i, (_, rows, _, columns) in enumerate(rights):
                value = contract_rows(
                    left_ref[row : row + rows, :], refs[index + 1 + i][:, columns]
                )
                row += rows
                total = value if total is None else total + value
            index += 1 + len(rights)
        refs[-1][...] = total.astype(BF16)

    return call(
        body,
        size // block,
        inputs,
        [((size, wide), BF16, by_rows(wide, size=block))],
        "weight_grad",
        time,
    )[0]


def project_halves(rows, weights, transposed, name):
    wide = weights.shape[0] if transposed else weights.shape[1]

    def body(rows_ref, weight_ref, low_ref, high_ref):
        if transposed:
            out = contract_cols(rows_ref[...], weight_ref[...])
        else:
            out = product(rows_ref[...], weight_ref[...])
        put_halves(low_ref, high_ref, out.astype(BF16))

    return call(
        body,
        4,
        [(rows, by_rows(rows.shape[1])), (weights, whole(weights))],
        half_outputs(wide),
        name,
        9.0,
    )


def project_slot(rows, slot, weights, added=None):
    wide = weights.shape[0]
    blocks_in = LEN // ROW_BLOCK
    extra = [] if added is None else [(added, by_rows(wide))]

    def body(rows_ref, weight_ref, *refs):
        out = contract_cols(rows_ref[...], weight_ref[...])
        if extra:
            out = out + refs[0][...].astype(F32)
        refs[-1][...] = out.astype(BF16)

    return call(
        body,
        blocks_in,
        [
            (rows, by_rows(rows.shape[1], lambda i: i + slot * blocks_in)),
            (weights, whole(weights)),
        ]
        + extra,
        [((LEN, wide), BF16, by_rows(wide))],
        "project_slot",
        6.5,
    )[0]


def middle_back(grads, middle, cotangents, gain, bias, w_out):
    dim = middle.shape[1]
    width = w_out.shape[0]

    def body(*refs):
        grad_ref, grad_rest, middle_ref, cot_ref, cot_rest, gain_ref, bias_ref, out_ref = refs[:8]
        branch_ref, own_ref, attended_ref, gain_sum, bias_sum = refs[8:]
        grad = pick(grad_ref, grad_rest).astype(F32)
        _, hat, inv = normalize(middle_ref[...], gain_ref[...], bias_ref[...])
        weighted = grad * gain_ref[...]
        moved = grad * hat
        first_mean = jnp.mean(weighted, axis=-1, keepdims=True)
        second_mean = jnp.mean(weighted * hat, axis=-1, keepdims=True)
        value = pick(cot_ref, cot_rest).astype(F32) + inv * (
            weighted - first_mean - hat * second_mean
        )
        low = value.astype(BF16)
        branch_ref[...] = low
        attended_ref[...] = contract_cols(low, out_ref[...]).astype(BF16)
        add_up(gain_sum, moved)
        add_up(bias_sum, grad)

        @pl.when(pl.program_id(0) == 0)
        def _():
            own_ref[...] = value

    count = 4 * ROW_BLOCK
    return call(
        body,
        4,
        pair_inputs(*grads)
        + [(middle, by_rows(dim))]
        + pair_inputs(*cotangents)
        + [(gain, whole(gain)), (bias, whole(bias)), (w_out, whole(w_out))],
        [
            ((count, dim), BF16, by_rows(dim)),
            ((ROW_BLOCK, dim), F32, by_rows(dim, lambda i: 0)),
            ((count, width), BF16, by_rows(width)),
            sum_output(dim),
            sum_output(dim),
        ],
        "middle_back",
        12.0,
    )


def norm_back(near, far, rows, gain, bias, added=None):
    dim = rows.shape[1]
    extra = [] if added is None else [(added, by_rows(dim))]

    def body(*refs):
        near_ref, far_ref, rows_ref, gain_ref, bias_ref = refs[:5]
        out_ref, gain_sum, bias_sum = refs[-3:]
        grad = near_ref[...].astype(F32) + far_ref[...].astype(F32)
        _, hat, inv = normalize(rows_ref[...].astype(F32), gain_ref[...], bias_ref[...])
        weighted = grad * gain_ref[...]
        first_mean = jnp.mean(weighted, axis=-1, keepdims=True)
        second_mean = jnp.mean(weighted * hat, axis=-1, keepdims=True)
        value = inv * (weighted - first_mean - hat * second_mean)
        if extra:
            value = refs[5][...] + value
        out_ref[...] = value.astype(BF16)
        add_up(gain_sum, grad * hat)
        add_up(bias_sum, grad)

    return call(
        body,
        rows.shape[0] // ROW_BLOCK,
        [(near, by_rows(dim)), (far, by_rows(dim)), (rows, by_rows(dim))]
        + [(gain, whole(gain)), (bias, whole(bias))]
        + extra,
        [(rows.shape, BF16, by_rows(dim)), sum_output(dim), sum_output(dim)],
        "norm_back",
        rows.shape[0] / 120.0,
    )


def swap_head(value, bit):
    size = lax.axis_size("head")
    return lax.ppermute(value, "head", [(i, i ^ bit) for i in range(size)])


def swap_seq(value, bit):
    size = lax.axis_size("seq")
    return lax.ppermute(value, "seq", [(i, i ^ bit) for i in range(size)])


def sum_seq(value):
    size = lax.axis_size("seq")
    bit = 1
    while bit < size:
        value = value + swap_seq(value, bit)
        bit *= 2
    return value


def sum_head(value):
    size = lax.axis_size("head")
    bit = 1
    while bit < size:
        value = value + swap_head(value, bit)
        bit *= 2
    return value


def half_rows(value, which):
    half = value.shape[0] // 2
    return lax.dynamic_slice_in_dim(value, which * half, half, axis=0)


def join_halves(mine, other, which):
    return jnp.where(
        which == 0,
        jnp.concatenate([mine, other], axis=0),
        jnp.concatenate([other, mine], axis=0),
    )


def line_pairs():
    inward = [(x, 2 + x) for x in range(2)] + [(6 + x, 4 + x) for x in range(2)]
    middle = [(2 + x, 4 + x) for x in range(2)] + [(4 + x, 2 + x) for x in range(2)]
    outward = [(2 + x, x) for x in range(2)] + [(4 + x, 6 + x) for x in range(2)]
    return inward, middle, outward


class Order:
    def __init__(self):
        self.last = None

    def __call__(self, step, *values):
        if self.last is not None:
            *values, _ = lax.optimization_barrier((*values, self.last))
        out = step(*values)
        self.last = out[0] if isinstance(out, (tuple, list)) else out
        return out

    def gate(self, value):
        return lax.optimization_barrier((value, self.last))[0]


class SeqSum:
    def __init__(self, order, value):
        self.order = order
        index = lax.axis_index("seq")
        self.x = index % 2
        self.inner = (index // 2 == 1) | (index // 2 == 2)
        self.pairs = line_pairs()
        self.stage = 0
        self.value = value
        self.moving = swap_seq(order(lambda v: half_rows(v, 1 - self.x), value), 1)

    def step(self):
        order, x, inner = self.order, self.x, self.inner
        if self.stage == 0:
            self.value = order(lambda v, r: half_rows(v, x) + r, self.value, self.moving)
        elif self.stage < 3:
            self.value = order(lambda v, r: v + r, self.value, self.moving)
        elif self.stage == 3:
            self.value = order(lambda v, r: jnp.where(inner, v, r), self.value, self.moving)
        if self.stage < 3:
            self.moving = lax.ppermute(self.value, "seq", self.pairs[self.stage])
        else:
            self.moving = swap_seq(self.value, 1)
        self.stage += 1

    def finish(self):
        while self.stage < 4:
            self.step()
        return (self.value, self.moving)


def join_sums(parts, columns=slice(None)):
    x = lax.axis_index("seq") % 2
    rows = []
    for mine, other in parts:
        mine, other = mine[:, columns].astype(F32), other[:, columns].astype(F32)
        rows += [jnp.where(x == 0, mine, other), jnp.where(x == 0, other, mine)]
    return jnp.concatenate(rows, axis=0)


def blocks(value, count):
    size = value.shape[0] // count
    return [value[i * size : (i + 1) * size] for i in range(count)]


def shards_quad(
    media,
    media_ids,
    image_seq,
    image_valid,
    latents,
    w_query,
    w_key,
    w_value,
    w_out,
    w_up,
    w_down,
    media_gain,
    media_bias,
    latent_gain,
    latent_bias,
    ffn_gain,
    ffn_bias,
    cotangent,
):
    seq_index = lax.axis_index("seq")
    head_index = lax.axis_index("head")
    seq_size = lax.axis_size("seq")
    images = image_seq.shape[0]
    sequences = media_ids.shape[0] // LEN
    own_rows = latents.shape[0]
    width = w_query.shape[1]
    dim = media.shape[1]
    order = Order()
    media_gain, media_bias, latent_gain, latent_bias, ffn_gain, ffn_bias = (
        value.reshape(1, dim)
        for value in (media_gain, media_bias, latent_gain, latent_bias, ffn_gain, ffn_bias)
    )

    slots = jnp.array([0, 2, 1, 3], jnp.int32)
    per_device = images // 4
    which = ((slots ^ head_index)[:, None] * per_device + jnp.arange(per_device)[None, :]).reshape(-1)
    owners = seq_index * images + which
    local_seq = jnp.take(image_seq, which) - seq_index * sequences
    valid_float = jnp.take(image_valid, which).astype(F32)
    matches = media_ids[None, :] == owners[:, None]
    place = jnp.arange(media_ids.shape[0], dtype=jnp.int32)[None, :]
    run = jnp.sum(matches.astype(jnp.int32), axis=1)
    start = jnp.min(jnp.where(matches, place, media_ids.shape[0]), axis=1)
    low = jnp.where(run > 0, start - local_seq * LEN, 0)
    high = low + run
    slot = local_seq ^ head_index

    share = width // seq_size
    used = jnp.full((16, dim), jnp.sum(valid_float)).astype(BF16)
    out_piece = jnp.concatenate(
        [lax.dynamic_slice_in_dim(w_out, seq_index * share, share, axis=0), used], axis=0
    )
    latents_across = swap_head(latents, 2)
    raw_near = swap_head(media, 1)
    out_piece = swap_head(out_piece, 2)
    out_near = swap_head(w_out, 1)

    w_kv = jnp.concatenate([w_key, w_value], axis=1)
    w_qkv = jnp.concatenate([w_query, w_kv], axis=1)

    def media_step(rows, weights):
        return norm_project([rows], media_gain, media_bias, weights, 1.0)

    def stack(*values):
        return jnp.concatenate(values, axis=0)

    def add(left, right):
        return left + right

    kv_own, norm_own = order(media_step, media, w_kv)
    raw = order(lambda v: tuple(blocks(v, 2)), media)
    latent_pair = order(stack, latents, latents_across)
    latent_rest = swap_head(latent_pair, 1)
    raw = lax.optimization_barrier((*raw, latent_pair, out_piece))[:2]
    raw_across = [swap_head(piece, 2) for piece in raw]
    kv_near, norm_near = order(media_step, raw_near, w_kv)
    cotangent_across = swap_head(order.gate(cotangent), 2)
    out_far = lax.all_gather(order.gate(out_piece), "seq", axis=0, tiled=True)
    latent_qkv, latent_low = order(
        lambda v, r, w: norm_project([v, r], latent_gain, latent_bias, w, 1.0),
        latent_pair,
        latent_rest,
        w_qkv,
    )
    near_part = order(
        lambda *v: attention_forward(*v[:3], v[3:5], v[5], time=1.0),
        slot,
        low,
        high,
        kv_own,
        kv_near,
        latent_qkv,
    )
    out_first = order(stack, w_out, out_near)
    across, beyond = [], []
    for piece in raw_across:
        piece = order.gate(piece)
        moved = swap_head(piece, 1)
        across.append(order(media_step, piece, w_kv))
        beyond.append(order(media_step, moved, w_kv))
    far = across + beyond
    out_far = order.gate(out_far)
    pieces = blocks(out_far, seq_size)
    count_all = sum(piece[share, 0].astype(F32) for piece in pieces)
    out_far = order(stack, *[piece[:share] for piece in pieces])
    out_beyond = swap_head(out_far, 1)
    pen_scale = 1.0 / (HEADS * LATENTS * count_all)
    weighted_scale = 4.0 * images * seq_size / count_all
    attended, lse, entropy = order(
        lambda *v: attention_forward(*v[:3], v[3:7], v[7], 2, v[8:]),
        slot,
        low,
        high,
        *[kv for kv, _ in far],
        latent_qkv,
        *near_part,
    )
    attended_across = swap_head(attended, 2)
    attended_near = swap_head(attended, 1)
    cotangent_pair = order(stack, cotangent, cotangent_across)
    cotangent_rest = swap_head(cotangent_pair, 1)
    out_second = order(stack, out_far, out_beyond)
    pulled = order(cotangent_down, cotangent_pair, cotangent_rest, w_down)
    attended_across = order.gate(attended_across)
    attended_beyond = swap_head(attended_across, 1)
    middle, ffn_low, hidden, grad_before, lower, upper = order(
        lambda *v: feed_forward(v[:4], v[4:6], v[6:8], v[8], v[9], ffn_gain, ffn_bias),
        attended,
        attended_near,
        attended_across,
        attended_beyond,
        out_first,
        out_second,
        latent_pair,
        latent_rest,
        pulled,
        w_up,
    )
    upper_moved = swap_head(upper, 1)

    def grad_chunk(left, rights, chunk):
        size = left.shape[1] // 2
        return order(
            lambda v, *g: weight_grad([(v, [part(one) for one in g])], chunk * size, size),
            left,
            *rights,
        )

    cotangents = (cotangent_pair, cotangent_rest)
    down0 = SeqSum(order, grad_chunk(hidden, cotangents, 0))
    lower = order(add, lower, upper_moved)
    lower_moved = swap_head(lower, 2)
    down1 = SeqSum(order, grad_chunk(hidden, cotangents, 1))
    up0 = SeqSum(order, grad_chunk(ffn_low, (grad_before,), 0))
    up1 = SeqSum(order, grad_chunk(ffn_low, (grad_before,), 1))
    lower_branch, upper_branch = order(
        lambda v, w: project_halves(v, w, False, "branch"), hidden, w_down
    )
    down0.step()
    grad_pair = order(
        lambda v, r: v + jnp.concatenate(blocks(r, 2)[::-1], axis=0), lower, lower_moved
    )
    grad_rest = swap_head(grad_pair, 1)
    grad_branch, grad_middle, grad_attended, ffn_gain_part, ffn_bias_part = order(
        lambda *v: middle_back(v[:2], v[2], v[3:5], ffn_gain, ffn_bias, v[5]),
        grad_pair,
        grad_rest,
        middle,
        cotangent_pair,
        cotangent_rest,
        w_out,
    )
    down1.step()
    down0.step()
    latent_back, kv_back = order(
        lambda *v: attention_backward(*v[:4], v[4:10], *v[10:]),
        slot,
        low,
        high,
        valid_float * weighted_scale,
        kv_own,
        kv_near,
        *[kv for kv, _ in far],
        latent_qkv,
        grad_attended,
        lse,
        entropy,
    )
    up0.step()
    down1.step()
    down0.step()
    beyond_back = order(lambda v, w: project_slot(v, 3, w), kv_back, w_kv)
    beyond_moved = swap_head(beyond_back, 1)
    up1.step()
    media_far = order(lambda v, w, r: project_slot(v, 2, w, r), kv_back, w_kv, beyond_moved)
    media_far = swap_head(media_far, 2)
    up0.step()
    down0.step()
    down1.step()
    out_grad = order(
        lambda v, g: weight_grad([(v, [part(g)])], 0, width, 128), attended, grad_branch
    )
    query_grad = order(
        lambda v, g: weight_grad([(v, [part(g)])], 0, width, 128), latent_back, latent_low
    )
    late = SeqSum(order, order(stack, query_grad, out_grad))

    def key_grad(start, own, near, first, second, third, fourth, back, latent, latent_part):
        half = LEN // 2
        pairs = [(own, [part(back, LEN, 0)]), (near, [part(back, LEN, 1)])]
        for i, rows in enumerate((first, second, third, fourth)):
            pairs.append((rows, [part(back, half, 4 + i)]))
        pairs.append((latent, [part(latent_part, columns=slice(width, None))]))
        return weight_grad(pairs, start, dim // 2, time=12.0)

    norms = (norm_own, norm_near, *[norm for _, norm in far])

    def key_chunk(chunk):
        return order(
            lambda *v: key_grad(chunk * dim // 2, *v), *norms, kv_back, latent_low, latent_back
        )

    key0 = SeqSum(order, key_chunk(0))
    up1.step()
    up0.step()
    down1.step()
    key1 = SeqSum(order, key_chunk(1))
    late.step()
    up1.step()
    up0.step()
    latent_lower, latent_upper = order(
        lambda v, w: project_halves(v, w, True, "latent_back"), latent_back, w_qkv
    )
    latent_moved = swap_head(latent_upper, 1)
    key0.step()
    near_back = order(lambda v, w: project_slot(v, 1, w), kv_back, w_kv)
    near_moved = swap_head(near_back, 1)
    key1.step()
    late.step()
    up1.step()
    latent_lower = order(add, latent_lower, latent_moved)
    latent_moved = swap_head(latent_lower[own_rows:], 2)
    media_near = order(lambda v, w, r: project_slot(v, 0, w, r), kv_back, w_kv, near_moved)
    key0.step()
    late.step()
    key1.step()
    media_grad, media_gain_part, media_bias_part = order(
        lambda *v: norm_back(*v, media_gain, media_bias), media_near, media_far, media
    )
    down_grad = order(lambda *v: join_sums((v[:2], v[2:])), *down0.finish(), *down1.finish())
    key0.step()
    branch_moved = swap_head(order.gate(upper_branch), 1)
    late.step()
    key1.step()
    latents_grad, latent_gain_part, latent_bias_part = order(
        lambda *v: norm_back(*v[:3], latent_gain, latent_bias, v[3]),
        latent_lower,
        latent_moved,
        latents,
        grad_middle,
    )
    entropy_local = jnp.sum(entropy.reshape(images, -1) * valid_float[:, None])
    share = 1.0 / lax.axis_size("head")
    sums = order(
        stack,
        media_gain_part,
        media_bias_part,
        latent_gain_part,
        latent_bias_part,
        ffn_gain_part * share,
        ffn_bias_part * share,
        jnp.broadcast_to(entropy_local, (2, dim)),
    )
    moved = swap_head(sums, 1)
    branch = order(add, lower_branch, branch_moved)
    branch_moved = swap_head(branch[own_rows:], 2)
    key0.step()
    sums = order(add, sums, moved)
    moved = swap_head(sums, 2)
    key1.step()
    up_grad = order(lambda *v: join_sums((v[:2], v[2:])), *up0.finish(), *up1.finish())
    sums = order(add, sums, moved)
    moved = swap_seq(sums, 1)
    result = order(
        lambda m, b, r: (m[:own_rows] + b[:own_rows].astype(F32) + r.astype(F32)).astype(BF16),
        middle,
        branch,
        branch_moved,
    )
    sums = order(add, sums, moved)
    moved = swap_seq(sums, 2)
    late_grads = order(lambda *v: join_sums((v,)), *late.finish())
    sums = order(add, sums, moved)
    moved = swap_seq(sums, 4)
    key_parts = [half.finish() for half in (key0, key1)]
    key_grads = order(
        lambda *v: join_sums((v[:2], v[2:]), slice(0, width)), *key_parts[0], *key_parts[1]
    )
    value_grads = order(
        lambda *v: join_sums((v[:2], v[2:]), slice(width, None)), *key_parts[0], *key_parts[1]
    )
    sums = order(add, sums, moved)
    return (
        result,
        sums[6, 0] * pen_scale,
        media_grad,
        latents_grad,
        late_grads[:width].T,
        key_grads,
        value_grads,
        late_grads[width:],
        up_grad,
        down_grad,
        sums[0],
        sums[1],
        sums[2],
        sums[3],
        sums[4],
        sums[5],
    )


def shards_any(
    media,
    media_ids,
    image_seq,
    image_valid,
    latents,
    w_query,
    w_key,
    w_value,
    w_out,
    w_up,
    w_down,
    media_gain,
    media_bias,
    latent_gain,
    latent_bias,
    ffn_gain,
    ffn_bias,
    cotangent,
):
    seq_index = lax.axis_index("seq")
    head_index = lax.axis_index("head")
    images = image_seq.shape[0]
    sequences = media_ids.shape[0] // LEN
    own_rows = latents.shape[0]
    inner_width = w_query.shape[1]
    seq_size = lax.axis_size("seq")
    valid_float = image_valid.astype(F32)

    media_norm, media_hat, media_inv = normalize(media.astype(F32), media_gain, media_bias)
    latent_rows = lax.all_gather(latents, "head", axis=0, tiled=True)
    media_all = lax.all_gather(media_norm.astype(BF16), "head", axis=0, tiled=True)
    grad_all = lax.all_gather(cotangent, "head", axis=0, tiled=True)
    latent_float = latent_rows.astype(F32)
    latent_norm, latent_hat, latent_inv = normalize(latent_float, latent_gain, latent_bias)
    latent_low = latent_norm.astype(BF16)

    count_all = jnp.sum(valid_float).reshape(1, 1)
    count_all = sum_seq(jnp.broadcast_to(count_all, (8, 128)))[0, 0]
    pen_scale = 1.0 / (HEADS * LATENTS * count_all)
    weighted_scale = 4.0 * images * seq_size / count_all

    owners = seq_index * images + jnp.arange(images, dtype=jnp.int32)
    local_seq = image_seq - seq_index * sequences
    matches = media_ids[None, :] == owners[:, None]
    place = jnp.arange(media_ids.shape[0], dtype=jnp.int32)[None, :]
    run = jnp.sum(matches.astype(jnp.int32), axis=1)
    start = jnp.min(jnp.where(matches, place, media_ids.shape[0]), axis=1)
    low = jnp.where(run > 0, start - local_seq * LEN, 0)
    high = low + run
    slot = local_seq

    w_kv = jnp.concatenate([w_key, w_value], axis=1)
    w_qkv = jnp.concatenate([w_query, w_kv], axis=1)
    latent_qkv = product(latent_low, w_qkv).astype(BF16)
    kv_slots = [product(media_all, w_kv).astype(BF16)]
    attended, lse, entropy = attention_forward(slot, low, high, kv_slots, latent_qkv)

    branch = lax.psum(product(attended, w_out).astype(BF16), "head").astype(F32)
    middle = latent_float + branch
    ffn_norm, ffn_hat, ffn_inv = normalize(middle, ffn_gain, ffn_bias)
    ffn_low = ffn_norm.astype(BF16)
    before_gelu = product(ffn_low, w_up)
    activated, gelu_slope = gelu_parts(before_gelu)
    hidden = activated.astype(BF16)
    grad_before = (contract_cols(grad_all, w_down) * gelu_slope).astype(BF16)
    grad_ffn_part = contract_cols(grad_before, w_up).astype(BF16)
    grad_ffn = lax.psum(grad_ffn_part, "head").astype(F32)
    down_grad = contract_rows(hidden, grad_all).astype(BF16)
    up_grad = contract_rows(ffn_low, grad_before).astype(BF16)
    up_grad, down_grad = lax.psum((up_grad, down_grad), "seq")

    ffn_branch = product(hidden, w_down).astype(BF16)
    ffn_branch = lax.psum_scatter(ffn_branch, "head", scatter_dimension=0, tiled=True)

    def own(value):
        return lax.dynamic_slice_in_dim(value, head_index * own_rows, own_rows, axis=0)

    result = (own(middle) + ffn_branch.astype(F32)).astype(BF16)

    middle_part, ffn_gain_part, ffn_bias_part = normalize_back(
        grad_ffn, ffn_hat, ffn_inv, ffn_gain
    )
    grad_middle = grad_all.astype(F32) + middle_part
    grad_branch = grad_middle.astype(BF16)
    grad_attended = contract_cols(grad_branch, w_out).astype(BF16)
    out_grad = contract_rows(attended, grad_branch)
    back = attention_backward(
        slot,
        low,
        high,
        valid_float * weighted_scale,
        kv_slots,
        latent_qkv,
        grad_attended,
        lse,
        entropy,
    )
    latent_back, kv_back = back
    grad_media_norm = lax.psum_scatter(
        contract_cols(kv_back, w_kv).astype(BF16), "head", scatter_dimension=0, tiled=True
    ).astype(F32)
    grad_latent_part = contract_cols(latent_back, w_qkv).astype(BF16)
    grad_latent_norm = lax.psum_scatter(
        grad_latent_part, "head", scatter_dimension=0, tiled=True
    ).astype(F32)
    latent_grads = contract_rows(latent_low, latent_back)
    kv_grads = latent_grads[:, inner_width:] + contract_rows(media_all, kv_back)
    late = (
        latent_grads[:, :inner_width].astype(BF16),
        kv_grads.astype(BF16),
        out_grad.astype(BF16),
    )
    up_grad, down_grad, *late = lax.optimization_barrier((up_grad, down_grad) + late)
    query_grad, kv_grads, out_grad = lax.psum(tuple(late), "seq")

    media_rows_grad, media_gain_part, media_bias_part = normalize_back(
        grad_media_norm, media_hat, media_inv, media_gain
    )
    latent_part, latent_gain_part, latent_bias_part = normalize_back(
        grad_latent_norm, own(latent_hat), own(latent_inv), latent_gain
    )
    latents_grad = (own(grad_middle) + latent_part).astype(BF16)
    entropy_local = jnp.sum(entropy.reshape(images, -1) * valid_float[:, None])
    share = 1.0 / lax.axis_size("head")
    sums = jnp.stack(
        [
            media_gain_part,
            media_bias_part,
            latent_gain_part,
            latent_bias_part,
            ffn_gain_part * share,
            ffn_bias_part * share,
            jnp.broadcast_to(entropy_local, media_gain.shape),
            jnp.zeros_like(media_gain),
        ]
    )
    sums = sum_seq(sum_head(sums))
    return (
        result,
        sums[6, 0] * pen_scale,
        media_rows_grad.astype(BF16),
        latents_grad,
        query_grad.astype(F32),
        kv_grads[:, :inner_width].astype(F32),
        kv_grads[:, inner_width:].astype(F32),
        out_grad.astype(F32),
        up_grad.astype(F32),
        down_grad.astype(F32),
        sums[0],
        sums[1],
        sums[2],
        sums[3],
        sums[4],
        sums[5],
    )


def solution(mesh):
    rows = P(("seq", "head"), None)
    columns = P(None, "head")
    lines = P("head", None)
    quad = mesh.shape["head"] == 4 and mesh.shape["seq"] == 8
    return jax.shard_map(
        shards_quad if quad else shards_any,
        mesh=mesh,
        in_specs=(
            (rows, P("seq"), P("seq"), P("seq"), rows)
            + (columns, columns, columns, lines, columns, lines)
            + (P(),) * 6
            + (rows,)
        ),
        out_specs=(
            (rows, P(), rows, rows)
            + (columns, columns, columns, lines, columns, lines)
            + (P(),) * 6
        ),
        check_vma=False,
    )
```

```python
import jax
import jax.numpy as jnp
from jax import lax
from jax.experimental import pallas as pl
from jax.experimental.pallas import tpu as pltpu
from jax.sharding import PartitionSpec as P

HEADS = 16
HEAD_DIM = 96
LATENTS = 64
LEN = 1024
KEY_BLOCK = 256

epsilon = 1e-05
BF16 = jnp.bfloat16


def cost(microseconds):
    return pl.CostEstimate(
        flops=int(microseconds * 1.1e9), transcendentals=0, bytes_accessed=int(microseconds * 3e6)
    )


F32 = jnp.float32


def normalize(row_values, norm_gain, norm_bias):
    row_mean = jnp.mean(row_values, axis=-1, keepdims=True)
    centred = row_values - row_mean
    variance = jnp.mean(centred * centred, axis=-1, keepdims=True)
    inverse = lax.rsqrt(variance + epsilon)
    scaled = centred * inverse
    return (scaled * norm_gain + norm_bias, scaled, inverse)


def normalize_back(incoming, scaled, inverse, norm_gain):
    weighted = incoming * norm_gain
    first_mean = jnp.mean(weighted, axis=-1, keepdims=True)
    second_mean = jnp.mean(weighted * scaled, axis=-1, keepdims=True)
    outgoing = inverse * (weighted - first_mean - scaled * second_mean)
    return (outgoing, jnp.sum(incoming * scaled, axis=0), jnp.sum(incoming, axis=0))


def product(left_side, right_side):
    return jnp.dot(left_side, right_side, preferred_element_type=F32)


def contract_rows(left_side, right_side):
    return lax.dot_general(
        left_side, right_side, (((0,), (0,)), ((), ())), preferred_element_type=F32
    )


def contract_cols(left_side, right_side):
    return lax.dot_general(
        left_side, right_side, (((1,), (1,)), ((), ())), preferred_element_type=F32
    )


def gelu_parts(inputs):
    normal_cdf = 0.5 * (1.0 + lax.erf(inputs * 0.7071067811865476))
    density = jnp.exp(-0.5 * inputs * inputs) * 0.3989422804014327
    return (inputs * normal_cdf, normal_cdf + inputs * density)


def block_diagonal(rows, heads):
    lane = lax.broadcasted_iota(jnp.int32, rows.shape, 1)
    parts = []
    for head in range(heads):
        inside = (lane >= head * HEAD_DIM) & (lane < (head + 1) * HEAD_DIM)
        parts.append(jnp.where(inside, rows, jnp.zeros_like(rows)))
    return jnp.concatenate(parts, axis=0)


def take_diagonal(wide, heads):
    lane = lax.broadcasted_iota(jnp.int32, (LATENTS, wide.shape[1]), 1)
    out = wide[:LATENTS]
    for head in range(1, heads):
        out = jnp.where(lane >= head * HEAD_DIM, wide[head * LATENTS : (head + 1) * LATENTS], out)
    return out


def load_keys(kv_hbm, kv_vmem, sems):
    copies = []
    at = 0
    for i, ref in enumerate(kv_hbm):
        size = ref.shape[0]
        copies.append(pltpu.make_async_copy(ref, kv_vmem.at[pl.ds(at, size), :], sems.at[i]))
        at += size
    for copy in copies:
        copy.start()
    for copy in copies:
        copy.wait()


def attention_forward(
    slot, low, high, kv_slots, latent_qkv, offset=0, before=None, time=15.0
):
    images = slot.shape[0]
    count = len(kv_slots)
    keys = sum(kv.shape[0] for kv in kv_slots)
    slots = keys // LEN
    width = latent_qkv.shape[1] // 3
    heads = width // HEAD_DIM
    rows = heads * LATENTS
    scale = HEAD_DIM ** (-0.5)
    given = () if before is None else tuple(before)

    def body(slot_ref, low_ref, high_ref, *refs):
        kv_hbm = refs[:count]
        qkv_ref = refs[count]
        given_refs = refs[count + 1 : count + 1 + len(given)]
        out_ref, lse_ref, ent_ref, kv_vmem, scores, sems = refs[count + 1 + len(given) :]
        image = pl.program_id(0)

        @pl.when(image == 0)
        def _():
            load_keys(kv_hbm, kv_vmem, sems)

        place = slot_ref[image] - offset
        here = (place >= 0) & (place < slots)

        @pl.when(here)
        def _():
            base = place * LEN
            lo = low_ref[image]
            hi = high_ref[image]
            first = lo // KEY_BLOCK
            last = (hi + KEY_BLOCK - 1) // KEY_BLOCK
            query = block_diagonal(qkv_ref[:, :width], heads)
            own = contract_cols(qkv_ref[:, width : 2 * width], query) * scale
            peak = jnp.max(own, axis=0, keepdims=True)

            def first_pass(block, peak):
                at = pl.multiple_of(base + block * KEY_BLOCK, KEY_BLOCK)
                part = contract_cols(kv_vmem[pl.ds(at, KEY_BLOCK), :width], query) * scale
                key = block * KEY_BLOCK + lax.broadcasted_iota(jnp.int32, part.shape, 0)
                part = jnp.where((key >= lo) & (key < hi), part, -1e30)
                to = pl.multiple_of((block - first) * KEY_BLOCK, KEY_BLOCK)
                scores[pl.ds(to, KEY_BLOCK), :] = part
                return jnp.maximum(peak, jnp.max(part, axis=0, keepdims=True))

            peak = lax.fori_loop(first, last, first_pass, peak)
            own = own - peak
            own_exp = jnp.exp(own)
            total = jnp.sum(own_exp, axis=0, keepdims=True)
            moment = jnp.sum(own_exp * own, axis=0, keepdims=True)

            def second_pass(block, carry):
                total, moment = carry
                to = pl.multiple_of((block - first) * KEY_BLOCK, KEY_BLOCK)
                part = scores[pl.ds(to, KEY_BLOCK), :] - peak
                part_exp = jnp.exp(part)
                scores[pl.ds(to, KEY_BLOCK), :] = part_exp
                return (
                    total + jnp.sum(part_exp, axis=0, keepdims=True),
                    moment + jnp.sum(part_exp * part, axis=0, keepdims=True),
                )

            total, moment = lax.fori_loop(first, last, second_pass, (total, moment))
            inverse = 1.0 / total
            log_total = jnp.log(total)
            lse_ref[0] = peak + log_total
            ent_ref[0] = log_total - moment * inverse
            wide = contract_rows((own_exp * inverse).astype(BF16), qkv_ref[:, 2 * width :])

            def third_pass(block, wide):
                to = pl.multiple_of((block - first) * KEY_BLOCK, KEY_BLOCK)
                at = pl.multiple_of(base + block * KEY_BLOCK, KEY_BLOCK)
                low_prob = (scores[pl.ds(to, KEY_BLOCK), :] * inverse).astype(BF16)
                return wide + contract_rows(low_prob, kv_vmem[pl.ds(at, KEY_BLOCK), width:])

            wide = lax.fori_loop(first, last, third_pass, wide)
            out_ref[...] = take_diagonal(wide, heads).astype(BF16)

        @pl.when(jnp.logical_not(here))
        def _():
            if given:
                out_ref[...] = given_refs[0][...]
                lse_ref[...] = given_refs[1][...]
                ent_ref[...] = given_refs[2][...]
            else:
                out_ref[...] = jnp.zeros_like(out_ref)
                lse_ref[...] = jnp.zeros_like(lse_ref)
                ent_ref[...] = jnp.zeros_like(ent_ref)

    any_spec = pl.BlockSpec(memory_space=pl.ANY)
    results = (
        pl.BlockSpec((LATENTS, width), lambda i, *_: (i, 0)),
        pl.BlockSpec((1, 1, rows), lambda i, *_: (i, 0, 0)),
        pl.BlockSpec((1, 1, rows), lambda i, *_: (i, 0, 0)),
    )
    return pl.pallas_call(
        body,
        out_shape=(
            jax.ShapeDtypeStruct((images * LATENTS, width), BF16),
            jax.ShapeDtypeStruct((images, 1, rows), F32),
            jax.ShapeDtypeStruct((images, 1, rows), F32),
        ),
        grid_spec=pltpu.PrefetchScalarGridSpec(
            num_scalar_prefetch=3,
            grid=(images,),
            in_specs=[any_spec] * count
            + [pl.BlockSpec((LATENTS, 3 * width), lambda i, *_: (i, 0))]
            + list(results[: len(given)]),
            out_specs=results,
            scratch_shapes=[
                pltpu.VMEM((keys, 2 * width), BF16),
                pltpu.VMEM((LEN, rows), F32),
                pltpu.SemaphoreType.DMA((count,)),
            ],
        ),
        compiler_params=pltpu.CompilerParams(
            dimension_semantics=("arbitrary",), vmem_limit_bytes=48 << 20
        ),
        cost_estimate=cost(time),
        name="attention_forward",
    )(slot, low, high, *kv_slots, latent_qkv, *given)


def attention_backward(slot, low, high, weight, kv_slots, latent_qkv, grad_out, lse, entropy):
    images = slot.shape[0]
    count = len(kv_slots)
    keys = sum(kv.shape[0] for kv in kv_slots)
    width = latent_qkv.shape[1] // 3
    heads = width // HEAD_DIM
    rows = heads * LATENTS
    scale = HEAD_DIM ** (-0.5)

    def body(slot_ref, low_ref, high_ref, weight_ref, *refs):
        kv_hbm = refs[:count]
        qkv_ref, grad_ref, lse_ref, ent_ref = refs[count : count + 4]
        own_out = refs[count + 4]
        key_out, kv_vmem, probs, slopes, totals, sems = refs[count + 5 :]
        image = pl.program_id(0)

        @pl.when(image == 0)
        def _():
            load_keys(kv_hbm, kv_vmem, sems)
            totals[...] = jnp.zeros_like(totals)

        base = slot_ref[image] * LEN
        lo = low_ref[image]
        hi = high_ref[image]
        pull = weight_ref[image]
        first = lo // KEY_BLOCK
        last = (hi + KEY_BLOCK - 1) // KEY_BLOCK
        query = block_diagonal(qkv_ref[:, :width], heads)
        grad = block_diagonal(grad_ref[...], heads)
        log_total = lse_ref[0]
        ent = ent_ref[0]
        own_key = qkv_ref[:, width : 2 * width]
        own_log = contract_cols(own_key, query) * scale - log_total
        own_prob = jnp.exp(own_log)
        own_slope = contract_cols(qkv_ref[:, 2 * width :], grad)
        centre = jnp.sum(own_prob * own_slope, axis=0, keepdims=True)
        own_slope = own_slope - pull * (own_log + ent)

        def first_pass(block, centre):
            at = pl.multiple_of(base + block * KEY_BLOCK, KEY_BLOCK)
            to = pl.multiple_of((block - first) * KEY_BLOCK, KEY_BLOCK)
            part = contract_cols(kv_vmem[pl.ds(at, KEY_BLOCK), :width], query) * scale
            place = block * KEY_BLOCK + lax.broadcasted_iota(jnp.int32, part.shape, 0)
            part = jnp.where((place >= lo) & (place < hi), part - log_total, -1e30)
            prob = jnp.exp(part)
            slope = contract_cols(kv_vmem[pl.ds(at, KEY_BLOCK), width:], grad)
            probs[pl.ds(to, KEY_BLOCK), :] = prob
            slopes[pl.ds(to, KEY_BLOCK), :] = slope - pull * (part + ent)
            return centre + jnp.sum(prob * slope, axis=0, keepdims=True)

        centre = lax.fori_loop(first, last, first_pass, centre)
        own_low = (own_prob * (own_slope - centre)).astype(BF16)
        grad_query = contract_rows(own_low, own_key)
        own_out[:, width : 2 * width] = (product(own_low, query) * scale).astype(BF16)
        own_out[:, 2 * width :] = product(own_prob.astype(BF16), grad).astype(BF16)

        def second_pass(block, grad_query):
            at = pl.multiple_of(base + block * KEY_BLOCK, KEY_BLOCK)
            to = pl.multiple_of((block - first) * KEY_BLOCK, KEY_BLOCK)
            prob = probs[pl.ds(to, KEY_BLOCK), :]
            low = (prob * (slopes[pl.ds(to, KEY_BLOCK), :] - centre)).astype(BF16)
            totals[pl.ds(at, KEY_BLOCK), :width] += product(low, query) * scale
            totals[pl.ds(at, KEY_BLOCK), width:] += product(prob.astype(BF16), grad)
            return grad_query + contract_rows(low, kv_vmem[pl.ds(at, KEY_BLOCK), :width])

        grad_query = lax.fori_loop(first, last, second_pass, grad_query)
        own_out[:, :width] = (take_diagonal(grad_query, heads) * scale).astype(BF16)

        @pl.when(image == images - 1)
        def _():
            key_out[...] = totals[...].astype(BF16)

    any_spec = pl.BlockSpec(memory_space=pl.ANY)
    row_spec = pl.BlockSpec((1, 1, rows), lambda i, *_: (i, 0, 0))
    return pl.pallas_call(
        body,
        out_shape=(
            jax.ShapeDtypeStruct((images * LATENTS, 3 * width), BF16),
            jax.ShapeDtypeStruct((keys, 2 * width), BF16),
        ),
        grid_spec=pltpu.PrefetchScalarGridSpec(
            num_scalar_prefetch=4,
            grid=(images,),
            in_specs=[any_spec] * count
            + [
                pl.BlockSpec((LATENTS, 3 * width), lambda i, *_: (i, 0)),
                pl.BlockSpec((LATENTS, width), lambda i, *_: (i, 0)),
                row_spec,
                row_spec,
            ],
            out_specs=(
                pl.BlockSpec((LATENTS, 3 * width), lambda i, *_: (i, 0)),
                pl.BlockSpec((keys, 2 * width), lambda i, *_: (0, 0)),
            ),
            scratch_shapes=[
                pltpu.VMEM((keys, 2 * width), BF16),
                pltpu.VMEM((LEN, rows), F32),
                pltpu.VMEM((LEN, rows), F32),
                pltpu.VMEM((keys, 2 * width), F32),
                pltpu.SemaphoreType.DMA((count,)),
            ],
        ),
        compiler_params=pltpu.CompilerParams(
            dimension_semantics=("arbitrary",), vmem_limit_bytes=56 << 20
        ),
        cost_estimate=cost(0.5),
        name="attention_backward",
    )(slot, low, high, weight, *kv_slots, latent_qkv, grad_out, lse, entropy)


ROW_BLOCK = 256


def call(body, grid, inputs, outputs, name, time=5.0, scratch=()):
    return pl.pallas_call(
        body,
        out_shape=tuple(jax.ShapeDtypeStruct(shape, dtype) for shape, dtype, _ in outputs),
        grid=(grid,),
        in_specs=[spec for _, spec in inputs],
        out_specs=tuple(spec for _, _, spec in outputs),
        scratch_shapes=list(scratch),
        compiler_params=pltpu.CompilerParams(
            dimension_semantics=("arbitrary",), vmem_limit_bytes=56 << 20
        ),
        cost_estimate=cost(time),
        name=name,
    )(*[value for value, _ in inputs])


def by_rows(width, move=lambda i: i, size=ROW_BLOCK):
    return pl.BlockSpec((size, width), lambda i: (move(i), 0))


def whole(value):
    return pl.BlockSpec(value.shape, lambda i: (0,) * value.ndim, pipeline_mode=pl.Buffered(1))


def stacked(values):
    steps = values[0].shape[0] // ROW_BLOCK
    return [
        (value, by_rows(value.shape[1], lambda i, k=k: jnp.clip(i - k * steps, 0, steps - 1)))
        for k, value in enumerate(values)
    ]


def stacked_rows(refs, values):
    steps = values[0].shape[0] // ROW_BLOCK
    rows = refs[0][...]
    for k in range(1, len(values)):
        rows = jnp.where(pl.program_id(0) >= k * steps, refs[k][...], rows)
    return rows


def low_half(i):
    return jnp.minimum(i, 1)


def high_half(i):
    return jnp.maximum(i - 2, 0)


def pair_inputs(pair, rest):
    return [(pair, by_rows(pair.shape[1], low_half)), (rest, by_rows(rest.shape[1], high_half))]


def pick(pair_ref, rest_ref):
    return jnp.where(pl.program_id(0) < 2, pair_ref[...], rest_ref[...])


def put_halves(low_ref, high_ref, value):
    @pl.when(pl.program_id(0) < 2)
    def _():
        low_ref[...] = value

    @pl.when(pl.program_id(0) >= 2)
    def _():
        high_ref[...] = value


def half_outputs(width):
    return [
        ((2 * ROW_BLOCK, width), BF16, by_rows(width, low_half)),
        ((2 * ROW_BLOCK, width), BF16, by_rows(width, high_half)),
    ]


def add_up(ref, value):
    total = jnp.sum(value, axis=0, keepdims=True)

    @pl.when(pl.program_id(0) == 0)
    def _():
        ref[...] = total

    @pl.when(pl.program_id(0) > 0)
    def _():
        ref[...] += total


def sum_output(width):
    return ((1, width), F32, pl.BlockSpec((1, width), lambda i: (0, 0)))


def norm_project(rows, gain, bias, weights, time=7.5):
    width, wide = rows[0].shape[1], weights.shape[1]
    count = sum(part.shape[0] for part in rows)

    def body(*refs):
        value = stacked_rows(refs, rows)
        gain_ref, bias_ref, weight_ref, out_ref, norm_ref = refs[len(rows) :]
        norm = normalize(value.astype(F32), gain_ref[...], bias_ref[...])[0].astype(BF16)
        norm_ref[...] = norm
        out_ref[...] = product(norm, weight_ref[...]).astype(BF16)

    return call(
        body,
        count // ROW_BLOCK,
        stacked(rows) + [(gain, whole(gain)), (bias, whole(bias)), (weights, whole(weights))],
        [((count, wide), BF16, by_rows(wide)), ((count, width), BF16, by_rows(width))],
        "norm_project",
        time,
    )


def cotangent_down(pair, rest, weights):
    wide = weights.shape[0]

    def body(pair_ref, rest_ref, weight_ref, out_ref):
        out_ref[...] = contract_cols(pick(pair_ref, rest_ref), weight_ref[...])

    return call(
        body,
        4,
        pair_inputs(pair, rest) + [(weights, whole(weights))],
        [((4 * ROW_BLOCK, wide), F32, by_rows(wide))],
        "cotangent_down",
        10.0,
    )[0]


def feed_forward(attended, out_weights, latent_rows, pulled, w_up, gain, bias):
    width = attended[0].shape[1]
    dim = w_up.shape[0]
    wide = w_up.shape[1]

    def body(*refs):
        own, near, across, beyond, first_ref, second_ref, lat_ref, lat_rest, pulled_ref = refs[:9]
        up_ref, gain_ref, bias_ref, middle_ref, ffn_ref, hidden_ref, grad_ref, low_ref, high_ref = (
            refs[9:]
        )
        rows = pick(lat_ref, lat_rest).astype(F32)
        rows = rows + product(jnp.concatenate([own[...], near[...]], axis=1), first_ref[...])
        rows = rows + product(jnp.concatenate([across[...], beyond[...]], axis=1), second_ref[...])
        middle_ref[...] = rows
        norm = normalize(rows, gain_ref[...], bias_ref[...])[0].astype(BF16)
        ffn_ref[...] = norm
        step = wide // 3
        for i in range(3):
            at = slice(i * step, (i + 1) * step)
            activated, slope = gelu_parts(product(norm, up_ref[:, at]))
            hidden_ref[:, at] = activated.astype(BF16)
            grad_ref[:, at] = (pulled_ref[:, at] * slope).astype(BF16)
        back = contract_cols(grad_ref[...], up_ref[...]).astype(BF16)
        put_halves(low_ref, high_ref, back)

    count = 4 * ROW_BLOCK
    return call(
        body,
        4,
        [
            (attended[0], by_rows(width)),
            (attended[1], by_rows(width, lambda i: i ^ 2)),
            (attended[2], by_rows(width, lambda i: i ^ 1)),
            (attended[3], by_rows(width, lambda i: i ^ 3)),
            (out_weights[0], whole(out_weights[0])),
            (out_weights[1], whole(out_weights[1])),
        ]
        + pair_inputs(*latent_rows)
        + [
            (pulled, by_rows(wide)),
            (w_up, whole(w_up)),
            (gain, whole(gain)),
            (bias, whole(bias)),
        ],
        [
            ((count, dim), F32, by_rows(dim)),
            ((count, dim), BF16, by_rows(dim)),
            ((count, wide), BF16, by_rows(wide)),
            ((count, wide), BF16, by_rows(wide)),
        ]
        + half_outputs(dim),
        "feed_forward",
        27.0,
    )


def part(value, rows=None, at=0, columns=slice(None)):
    return (value, value.shape[0] if rows is None else rows, at, columns)


def grad_halves(side, pairs, chunk, name):
    columns_in = pairs[0][0].shape[1] // 2
    half = columns_in // 2
    inputs = []
    for left, rights in pairs:
        inputs.append(
            (
                left,
                pl.BlockSpec(
                    (left.shape[0], half),
                    lambda i, x: (0, 2 * chunk + (i + 1 + x[0]) % 2),
                ),
            )
        )
        for value, rows, at, _ in rights:
            spec = pl.BlockSpec(
                (rows, value.shape[1]), lambda i, x, at=at: (at, 0), pipeline_mode=pl.Buffered(1)
            )
            inputs.append((value, spec))
    value, _, _, columns = pairs[0][1][0]
    wide = len(range(*columns.indices(value.shape[1])))

    def body(x_ref, *refs):
        total = None
        index = 0
        for left, rights in pairs:
            left_ref = refs[index]
            row = 0
            for i, (_, rows, _, columns) in enumerate(rights):
                value = contract_rows(
                    left_ref[row : row + rows, :], refs[index + 1 + i][:, columns]
                )
                row += rows
                total = value if total is None else total + value
            index += 1 + len(rights)
        put_sides(refs[-2], refs[-1], total.astype(BF16))

    return side_call(body, side, inputs, half, wide, name)


def put_sides(other_ref, mine_ref, value):
    @pl.when(pl.program_id(0) == 0)
    def _():
        other_ref[...] = value

    @pl.when(pl.program_id(0) == 1)
    def _():
        mine_ref[...] = value


def side_call(body, side, inputs, half, wide, name):
    out = pl.BlockSpec((half, wide), lambda i, x: (0, 0))
    return pl.pallas_call(
        body,
        out_shape=(jax.ShapeDtypeStruct((half, wide), BF16),) * 2,
        grid_spec=pltpu.PrefetchScalarGridSpec(
            num_scalar_prefetch=1,
            grid=(2,),
            in_specs=[spec for _, spec in inputs],
            out_specs=(out, out),
        ),
        compiler_params=pltpu.CompilerParams(
            dimension_semantics=("arbitrary",), vmem_limit_bytes=56 << 20
        ),
        cost_estimate=cost(0.5),
        name=name,
    )(side, *[value for value, _ in inputs])


def late_grads(side, latent_back, latent_low, attended, grad_branch):
    width = attended.shape[1]
    wide = grad_branch.shape[1]

    def body(x_ref, back_ref, low_ref, attended_ref, branch_ref, other_ref, mine_ref):
        which = (pl.program_id(0) + 1 + x_ref[0]) % 2

        @pl.when(which == 0)
        def _():
            value = contract_rows(back_ref[...], low_ref[...]).astype(BF16)
            put_sides(other_ref, mine_ref, value)

        @pl.when(which == 1)
        def _():
            value = contract_rows(attended_ref[...], branch_ref[...]).astype(BF16)
            put_sides(other_ref, mine_ref, value)

    inputs = [
        (
            value,
            pl.BlockSpec(
                (value.shape[0], min(value.shape[1], size)),
                lambda i, x: (0, 0),
                pipeline_mode=pl.Buffered(1),
            ),
        )
        for value, size in (
            (latent_back, width),
            (latent_low, wide),
            (attended, width),
            (grad_branch, wide),
        )
    ]
    return side_call(body, side, inputs, width, wide, "late_grads")


def join_rows(side, parts, splits):
    half = parts[0].shape[0]
    count = len(parts)

    def body(x_ref, *refs):
        step = pl.program_id(0)
        for i in range(count):

            @pl.when(step == i)
            def _():
                for (first, last), out_ref in zip(splits, refs[count:]):
                    out_ref[...] = refs[i][:, first:last].astype(F32)

    inputs = [
        pl.BlockSpec(value.shape, lambda i, x: (0, 0), pipeline_mode=pl.Buffered(1))
        for value in parts
    ]
    return pl.pallas_call(
        body,
        out_shape=tuple(
            jax.ShapeDtypeStruct((count * half, last - first), F32) for first, last in splits
        ),
        grid_spec=pltpu.PrefetchScalarGridSpec(
            num_scalar_prefetch=1,
            grid=(count,),
            in_specs=inputs,
            out_specs=tuple(
                pl.BlockSpec(
                    (half, last - first),
                    lambda i, x: (i // 2 * 2 + (i + x[0]) % 2, 0),
                )
                for first, last in splits
            ),
        ),
        compiler_params=pltpu.CompilerParams(
            dimension_semantics=("arbitrary",), vmem_limit_bytes=56 << 20
        ),
        cost_estimate=cost(0.5),
        name="join_rows",
    )(side, *parts)


def join_late(side, mine, other):
    wide, dim = mine.shape

    def body(x_ref, mine_ref, other_ref, query_ref, out_ref):
        first = x_ref[0] == 0
        query = jnp.where(first, mine_ref[...], other_ref[...]).astype(F32)
        query_ref[...] = query.T
        out_ref[...] = jnp.where(first, other_ref[...], mine_ref[...]).astype(F32)

    spec = pl.BlockSpec((wide, 384), lambda i, x: (0, i))
    return pl.pallas_call(
        body,
        out_shape=(
            jax.ShapeDtypeStruct((dim, wide), F32),
            jax.ShapeDtypeStruct((wide, dim), F32),
        ),
        grid_spec=pltpu.PrefetchScalarGridSpec(
            num_scalar_prefetch=1,
            grid=(dim // 384,),
            in_specs=[spec, spec],
            out_specs=(pl.BlockSpec((384, wide), lambda i, x: (i, 0)), spec),
        ),
        compiler_params=pltpu.CompilerParams(dimension_semantics=("arbitrary",)),
        cost_estimate=cost(0.5),
        name="join_late",
    )(side, mine, other)


def project_halves(rows, weights, transposed, name):
    wide = weights.shape[0] if transposed else weights.shape[1]

    def body(rows_ref, weight_ref, low_ref, high_ref):
        if transposed:
            out = contract_cols(rows_ref[...], weight_ref[...])
        else:
            out = product(rows_ref[...], weight_ref[...])
        put_halves(low_ref, high_ref, out.astype(BF16))

    return call(
        body,
        4,
        [(rows, by_rows(rows.shape[1])), (weights, whole(weights))],
        half_outputs(wide),
        name,
        0.5,
    )


def project_slot(rows, slot, weights, added=()):
    wide = weights.shape[0]
    blocks_in = LEN // ROW_BLOCK

    def body(rows_ref, weight_ref, *refs):
        out = contract_cols(rows_ref[...], weight_ref[...])
        if added:
            out = out + stacked_rows(refs, added).astype(F32)
        refs[-1][...] = out.astype(BF16)

    return call(
        body,
        blocks_in,
        [
            (rows, by_rows(rows.shape[1], lambda i: i + slot * blocks_in)),
            (weights, whole(weights)),
        ]
        + (stacked(added) if added else []),
        [((LEN, wide), BF16, by_rows(wide))],
        "project_slot",
        0.5,
    )[0]


def middle_back(grads, middle, cotangents, gain, bias, w_out):
    dim = middle.shape[1]
    width = w_out.shape[0]

    def body(*refs):
        grad_ref, *rest_refs, middle_ref, cot_ref, cot_rest, gain_ref, bias_ref, out_ref = refs[:11]
        branch_ref, own_ref, attended_ref, gain_sum, bias_sum = refs[11:]
        step = pl.program_id(0)
        third = jnp.concatenate([ref[...] for ref in rest_refs[:2]], axis=0)
        fourth = jnp.concatenate([ref[...] for ref in rest_refs[2:]], axis=0)
        grad = jnp.where(step == 2, third, fourth)
        grad = jnp.where(step < 2, grad_ref[...], grad).astype(F32)
        _, hat, inv = normalize(middle_ref[...], gain_ref[...], bias_ref[...])
        weighted = grad * gain_ref[...]
        moved = grad * hat
        first_mean = jnp.mean(weighted, axis=-1, keepdims=True)
        second_mean = jnp.mean(weighted * hat, axis=-1, keepdims=True)
        value = pick(cot_ref, cot_rest).astype(F32) + inv * (
            weighted - first_mean - hat * second_mean
        )
        low = value.astype(BF16)
        branch_ref[...] = low
        attended_ref[...] = contract_cols(low, out_ref[...]).astype(BF16)
        add_up(gain_sum, moved)
        add_up(bias_sum, grad)

        @pl.when(pl.program_id(0) == 0)
        def _():
            own_ref[...] = value

    count = 4 * ROW_BLOCK
    return call(
        body,
        4,
        [(grads[0], by_rows(dim, low_half))]
        + [(grad, whole(grad)) for grad in grads[1:]]
        + [(middle, by_rows(dim))]
        + pair_inputs(*cotangents)
        + [(gain, whole(gain)), (bias, whole(bias)), (w_out, whole(w_out))],
        [
            ((count, dim), BF16, by_rows(dim)),
            ((ROW_BLOCK, dim), F32, by_rows(dim, lambda i: 0)),
            ((count, width), BF16, by_rows(width)),
            sum_output(dim),
            sum_output(dim),
        ],
        "middle_back",
        0.5,
    )


def norm_back(near, far, rows, gain, bias, added=None):
    dim = rows.shape[1]
    extra = [] if added is None else [(added, by_rows(dim))]

    def body(*refs):
        near_ref, far_ref, rows_ref, gain_ref, bias_ref = refs[:5]
        out_ref, gain_sum, bias_sum = refs[-3:]
        grad = near_ref[...].astype(F32) + far_ref[...].astype(F32)
        _, hat, inv = normalize(rows_ref[...].astype(F32), gain_ref[...], bias_ref[...])
        weighted = grad * gain_ref[...]
        first_mean = jnp.mean(weighted, axis=-1, keepdims=True)
        second_mean = jnp.mean(weighted * hat, axis=-1, keepdims=True)
        value = inv * (weighted - first_mean - hat * second_mean)
        if extra:
            value = refs[5][...] + value
        out_ref[...] = value.astype(BF16)
        add_up(gain_sum, grad * hat)
        add_up(bias_sum, grad)

    return call(
        body,
        rows.shape[0] // ROW_BLOCK,
        [(near, by_rows(dim)), (far, by_rows(dim)), (rows, by_rows(dim))]
        + [(gain, whole(gain)), (bias, whole(bias))]
        + extra,
        [(rows.shape, BF16, by_rows(dim)), sum_output(dim), sum_output(dim)],
        "norm_back",
        0.5,
    )


def swap_head(value, bit):
    size = lax.axis_size("head")
    return lax.ppermute(value, "head", [(i, i ^ bit) for i in range(size)])


def swap_seq(value, bit):
    size = lax.axis_size("seq")
    return lax.ppermute(value, "seq", [(i, i ^ bit) for i in range(size)])


def sum_seq(value):
    size = lax.axis_size("seq")
    bit = 1
    while bit < size:
        value = value + swap_seq(value, bit)
        bit *= 2
    return value


def sum_head(value):
    size = lax.axis_size("head")
    bit = 1
    while bit < size:
        value = value + swap_head(value, bit)
        bit *= 2
    return value


def line_pairs():
    inward = [(x, 2 + x) for x in range(2)] + [(6 + x, 4 + x) for x in range(2)]
    middle = [(2 + x, 4 + x) for x in range(2)] + [(4 + x, 2 + x) for x in range(2)]
    outward = [(2 + x, x) for x in range(2)] + [(4 + x, 6 + x) for x in range(2)]
    return inward, middle, outward


STEPS = (
    "u0", "lowadd", "d1", "u1", "branch", "u0.1", "gpair", "d0", "mback", "u1.1", "u0.2",
    "attb", "d1.1", "u1.2", "u0.3", "d0.1", "l", "k1", "u1.3", "d1.2", "pb", "u0.4", "l.1",
    "d0.2", "pa", "u1.4", "d1.3", "k1.1", "k0", "l.2", "d0.3", "pn", "lb", "u.5", "d1.4",
    "k1.2", "l.3", "d0.4", "k0.1", "po", "ladd", "k0.2", "k1.3", "nbm", "l.4", "k0.3", "nbl",
    "s0", "d.5", "s1", "bradd", "s2", "k1.4", "k0.4", "s3", "s4", "s5", "l.5", "res", "k.5",
)


class Order:
    def __init__(self):
        self.last = None

    def __call__(self, step, *values):
        if self.last is not None:
            *values, _ = lax.optimization_barrier((*values, self.last))
        out = step(*values)
        self.last = out[0] if isinstance(out, (tuple, list)) else out
        return out

    def gate(self, value):
        return lax.optimization_barrier((value, self.last))[0]


class SeqSum:
    def __init__(self, order, other, mine):
        self.order = order
        index = lax.axis_index("seq")
        self.inner = (index // 2 == 1) | (index // 2 == 2)
        self.pairs = line_pairs()
        self.stage = 0
        self.value = mine
        self.moving = swap_seq(other, 1)

    def step(self):
        order, inner = self.order, self.inner
        if self.stage < 3:
            self.value = order(lambda v, r: v + r, self.value, self.moving)
            self.moving = lax.ppermute(self.value, "seq", self.pairs[self.stage])
        else:
            self.value = order(lambda v, r: jnp.where(inner, v, r), self.value, self.moving)
            self.moving = swap_seq(self.value, 1)
        self.stage += 1


def blocks(value, count):
    size = value.shape[0] // count
    return [value[i * size : (i + 1) * size] for i in range(count)]


def shards_quad(
    media,
    media_ids,
    image_seq,
    image_valid,
    latents,
    w_query,
    w_key,
    w_value,
    w_out,
    w_up,
    w_down,
    media_gain,
    media_bias,
    latent_gain,
    latent_bias,
    ffn_gain,
    ffn_bias,
    cotangent,
):
    seq_index = lax.axis_index("seq")
    head_index = lax.axis_index("head")
    seq_size = lax.axis_size("seq")
    images = image_seq.shape[0]
    sequences = media_ids.shape[0] // LEN
    own_rows = latents.shape[0]
    width = w_query.shape[1]
    dim = media.shape[1]
    order = Order()
    media_gain, media_bias, latent_gain, latent_bias, ffn_gain, ffn_bias = (
        value.reshape(1, dim)
        for value in (media_gain, media_bias, latent_gain, latent_bias, ffn_gain, ffn_bias)
    )

    slots = jnp.array([0, 2, 1, 3], jnp.int32)
    per_device = images // 4
    which = ((slots ^ head_index)[:, None] * per_device + jnp.arange(per_device)[None, :]).reshape(-1)
    owners = seq_index * images + which
    local_seq = jnp.take(image_seq, which) - seq_index * sequences
    valid_float = jnp.take(image_valid, which).astype(F32)
    matches = media_ids[None, :] == owners[:, None]
    place = jnp.arange(media_ids.shape[0], dtype=jnp.int32)[None, :]
    run = jnp.sum(matches.astype(jnp.int32), axis=1)
    start = jnp.min(jnp.where(matches, place, media_ids.shape[0]), axis=1)
    low = jnp.where(run > 0, start - local_seq * LEN, 0)
    high = low + run
    slot = local_seq ^ head_index

    share = width // seq_size
    used = jnp.full((16, dim), jnp.sum(valid_float)).astype(BF16)
    out_piece = jnp.concatenate(
        [lax.dynamic_slice_in_dim(w_out, seq_index * share, share, axis=0), used], axis=0
    )
    latents_across = swap_head(latents, 2)
    raw_near = swap_head(media, 1)
    out_piece = swap_head(out_piece, 2)
    out_near = swap_head(w_out, 1)

    w_kv = jnp.concatenate([w_key, w_value], axis=1)
    w_qkv = jnp.concatenate([w_query, w_kv], axis=1)

    def media_step(rows, weights):
        return norm_project([rows], media_gain, media_bias, weights, 1.0)

    def stack(*values):
        return jnp.concatenate(values, axis=0)

    def add(left, right):
        return left + right

    kv_own, norm_own = order(media_step, media, w_kv)
    raw = order(lambda v: tuple(blocks(v, 2)), media)
    latent_pair = order(stack, latents, latents_across)
    latent_rest = swap_head(latent_pair, 1)
    raw = lax.optimization_barrier((*raw, latent_pair, out_piece))[:2]
    raw_across = [swap_head(piece, 2) for piece in raw]
    kv_near, norm_near = order(media_step, raw_near, w_kv)
    cotangent_across = swap_head(order.gate(cotangent), 2)
    out_far = lax.all_gather(order.gate(out_piece), "seq", axis=0, tiled=True)
    latent_qkv, latent_low = order(
        lambda v, r, w: norm_project([v, r], latent_gain, latent_bias, w, 1.0),
        latent_pair,
        latent_rest,
        w_qkv,
    )
    near_part = order(
        lambda *v: attention_forward(*v[:3], v[3:5], v[5], time=1.0),
        slot,
        low,
        high,
        kv_own,
        kv_near,
        latent_qkv,
    )
    out_first = order(stack, w_out, out_near)
    across, beyond = [], []
    for piece in raw_across:
        piece = order.gate(piece)
        moved = [swap_head(half, 1) for half in blocks(piece, 2)]
        across.append(order(media_step, piece, w_kv))
        beyond.append(
            order(
                lambda v, r, w: norm_project([v, r], media_gain, media_bias, w, 1.0), *moved, w_kv
            )
        )
    far = across + beyond
    out_far = order.gate(out_far)
    pieces = blocks(out_far, seq_size)
    count_all = sum(piece[share, 0].astype(F32) for piece in pieces)
    out_far = order(stack, *[piece[:share] for piece in pieces])
    out_beyond = swap_head(out_far, 1)
    pen_scale = 1.0 / (HEADS * LATENTS * count_all)
    weighted_scale = 4.0 * images * seq_size / count_all
    attended, lse, entropy = order(
        lambda *v: attention_forward(*v[:3], v[3:7], v[7], 2, v[8:]),
        slot,
        low,
        high,
        *[kv for kv, _ in far],
        latent_qkv,
        *near_part,
    )
    attended_across = swap_head(attended, 2)
    attended_near = swap_head(attended, 1)
    cotangent_pair = order(stack, cotangent, cotangent_across)
    cotangent_rest = swap_head(cotangent_pair, 1)
    out_second = order(stack, out_far, out_beyond)
    pulled = order(cotangent_down, cotangent_pair, cotangent_rest, w_down)
    attended_across = order.gate(attended_across)
    attended_beyond = swap_head(attended_across, 1)
    middle, ffn_low, hidden, grad_before, lower, upper = order(
        lambda *v: feed_forward(v[:4], v[4:6], v[6:8], v[8], v[9], ffn_gain, ffn_bias),
        attended,
        attended_near,
        attended_across,
        attended_beyond,
        out_first,
        out_second,
        latent_pair,
        latent_rest,
        pulled,
        w_up,
    )
    side = (seq_index % 2).reshape(1)
    v = {}
    step = {}

    def define(name):
        def keep(function):
            step[name] = function
            return function

        return keep

    v["upper"] = swap_head(upper, 1)

    @define("lowadd")
    def _():
        v["lower"] = order(add, lower, v["upper"])
        v["Y"] = swap_head(v["lower"], 2)

    def sum_steps(name, grads):
        @define(name)
        def _():
            v[name] = SeqSum(order, *grads())

        for i in range(1, 5):

            @define(name + "." + str(i))
            def _():
                v[name].step()

    def down_chunk(chunk):
        return lambda: order(
            lambda x, h, g, r: grad_halves(x, [(h, [part(g), part(r)])], chunk, "down_grad"),
            side,
            hidden,
            cotangent_pair,
            cotangent_rest,
        )

    def up_chunk(chunk):
        return lambda: order(
            lambda x, h, g: grad_halves(x, [(h, [part(g)])], chunk, "up_grad"),
            side,
            ffn_low,
            grad_before,
        )

    half_len = LEN // 2
    norms = (norm_own, norm_near, *[norm for _, norm in far])

    def key_grads(x, chunk, own, near, first, second, third, fourth, back, latent, latent_part):
        pairs = [(own, [part(back, LEN, 0)]), (near, [part(back, LEN, 1)])]
        for i, rows in enumerate((first, second, third, fourth)):
            pairs.append((rows, [part(back, half_len, 4 + i)]))
        pairs.append((latent, [part(latent_part, columns=slice(width, None))]))
        return grad_halves(x, pairs, chunk, "key_grad")

    def key_chunk(chunk):
        return lambda: order(
            lambda x, *a: key_grads(x, chunk, *a),
            side,
            *norms,
            v["kv_back"],
            latent_low,
            v["latent_back"],
        )

    for i in range(2):
        sum_steps("d" + str(i), down_chunk(i))
        sum_steps("u" + str(i), up_chunk(i))
        sum_steps("k" + str(i), key_chunk(i))
    sum_steps(
        "l",
        lambda: order(
            late_grads, side, v["latent_back"], latent_low, attended, v["grad_branch"]
        ),
    )

    @define("branch")
    def _():
        v["branch"], v["branch_upper"] = order(
            lambda h, w: project_halves(h, w, False, "branch"), hidden, w_down
        )
        v["BC"] = swap_head(v["branch_upper"], 1)

    @define("bradd")
    def _():
        v["branch"] = order(add, v["branch"], v["BC"])
        v["BY"] = swap_head(v["branch"][own_rows:], 2)

    @define("res")
    def _():
        v["result"] = order(
            lambda m, b, r: (m[:own_rows] + b[:own_rows].astype(F32) + r.astype(F32)).astype(BF16),
            middle,
            v["branch"],
            v["BY"],
        )

    @define("gpair")
    def _():
        v["pair"] = order(
            lambda a, r: a + jnp.concatenate(blocks(r, 2)[::-1], axis=0), v["lower"], v["Y"]
        )
        v["G"] = [swap_head(piece, 1) for piece in blocks(v["pair"], 4)]

    @define("mback")
    def _():
        out = order(
            lambda *a: middle_back(a[:5], a[5], a[6:8], ffn_gain, ffn_bias, a[8]),
            v["pair"],
            *v["G"],
            middle,
            cotangent_pair,
            cotangent_rest,
            w_out,
        )
        v["grad_branch"], v["grad_middle"], v["grad_attended"] = out[:3]
        v["ffn_sums"] = out[3:]

    @define("attb")
    def _():
        v["latent_back"], v["kv_back"] = order(
            lambda *a: attention_backward(*a[:4], a[4:10], *a[10:]),
            slot,
            low,
            high,
            valid_float * weighted_scale,
            kv_own,
            kv_near,
            *[kv for kv, _ in far],
            latent_qkv,
            v["grad_attended"],
            lse,
            entropy,
        )

    def swap_pieces(value):
        return [swap_head(piece, 1) for piece in blocks(value, 4)]

    @define("pb")
    def _():
        v["K1"] = swap_pieces(order(lambda a, w: project_slot(a, 3, w), v["kv_back"], w_kv))

    @define("pa")
    def _():
        v["MF"] = swap_head(
            order(lambda a, w, *r: project_slot(a, 2, w, r), v["kv_back"], w_kv, *v["K1"]), 2
        )

    @define("pn")
    def _():
        v["K2"] = swap_pieces(order(lambda a, w: project_slot(a, 1, w), v["kv_back"], w_kv))

    @define("po")
    def _():
        v["media_near"] = order(
            lambda a, w, *r: project_slot(a, 0, w, r), v["kv_back"], w_kv, *v["K2"]
        )

    @define("lb")
    def _():
        v["latent_lower"], upper = order(
            lambda a, w: project_halves(a, w, True, "latent_back"), v["latent_back"], w_qkv
        )
        v["LC"] = swap_head(upper, 1)

    @define("ladd")
    def _():
        v["latent_lower"] = order(add, v["latent_lower"], v["LC"])
        v["LY"] = swap_head(v["latent_lower"][own_rows:], 2)

    @define("nbm")
    def _():
        v["media_grad"], *v["media_sums"] = order(
            lambda *a: norm_back(*a, media_gain, media_bias), v["media_near"], v["MF"], media
        )

    @define("nbl")
    def _():
        v["latents_grad"], *v["latent_sums"] = order(
            lambda *a: norm_back(*a[:3], latent_gain, latent_bias, a[3]),
            v["latent_lower"],
            v["LY"],
            latents,
            v["grad_middle"],
        )

    @define("s0")
    def _():
        entropy_local = jnp.sum(entropy.reshape(images, -1) * valid_float[:, None])
        part_of = 1.0 / lax.axis_size("head")
        v["sums"] = order(
            stack,
            *v["media_sums"],
            *v["latent_sums"],
            *[value * part_of for value in v["ffn_sums"]],
            jnp.broadcast_to(entropy_local, (2, dim)),
        )
        v["moved"] = swap_head(v["sums"], 1)

    def sums_step(i):
        @define("s" + str(i))
        def _():
            v["sums"] = order(add, v["sums"], v["moved"])
            if i == 1:
                v["moved"] = swap_head(v["sums"], 2)
            elif i < 5:
                v["moved"] = swap_seq(v["sums"], 2 ** (i - 2))

    for i in range(1, 6):
        sums_step(i)

    def both(*sums):
        return [value for one in sums for value in (one.value, one.moving)]

    @define("d.5")
    def _():
        v["down"] = order(
            lambda x, *a: join_rows(x, a, ((0, dim),))[0], side, *both(v["d0"], v["d1"])
        )

    @define("u.5")
    def _():
        v["up"] = order(
            lambda x, *a: join_rows(x, a, ((0, dim),))[0], side, *both(v["u0"], v["u1"])
        )

    @define("k.5")
    def _():
        v["key"], v["value"] = order(
            lambda x, *a: join_rows(x, a, ((0, width), (width, 2 * width))),
            side,
            *both(v["k0"], v["k1"]),
        )

    @define("l.5")
    def _():
        v["query"], v["out"] = order(join_late, side, *both(v["l"]))

    for name in STEPS:
        step.pop(name)()
    assert not step
    sums = v["sums"]
    return (
        v["result"],
        sums[6, 0] * pen_scale,
        v["media_grad"],
        v["latents_grad"],
        v["query"],
        v["key"],
        v["value"],
        v["out"],
        v["up"],
        v["down"],
        sums[0],
        sums[1],
        sums[2],
        sums[3],
        sums[4],
        sums[5],
    )


def shards_any(
    media,
    media_ids,
    image_seq,
    image_valid,
    latents,
    w_query,
    w_key,
    w_value,
    w_out,
    w_up,
    w_down,
    media_gain,
    media_bias,
    latent_gain,
    latent_bias,
    ffn_gain,
    ffn_bias,
    cotangent,
):
    seq_index = lax.axis_index("seq")
    head_index = lax.axis_index("head")
    images = image_seq.shape[0]
    sequences = media_ids.shape[0] // LEN
    own_rows = latents.shape[0]
    inner_width = w_query.shape[1]
    seq_size = lax.axis_size("seq")
    valid_float = image_valid.astype(F32)

    media_norm, media_hat, media_inv = normalize(media.astype(F32), media_gain, media_bias)
    latent_rows = lax.all_gather(latents, "head", axis=0, tiled=True)
    media_all = lax.all_gather(media_norm.astype(BF16), "head", axis=0, tiled=True)
    grad_all = lax.all_gather(cotangent, "head", axis=0, tiled=True)
    latent_float = latent_rows.astype(F32)
    latent_norm, latent_hat, latent_inv = normalize(latent_float, latent_gain, latent_bias)
    latent_low = latent_norm.astype(BF16)

    count_all = jnp.sum(valid_float).reshape(1, 1)
    count_all = sum_seq(jnp.broadcast_to(count_all, (8, 128)))[0, 0]
    pen_scale = 1.0 / (HEADS * LATENTS * count_all)
    weighted_scale = 4.0 * images * seq_size / count_all

    owners = seq_index * images + jnp.arange(images, dtype=jnp.int32)
    local_seq = image_seq - seq_index * sequences
    matches = media_ids[None, :] == owners[:, None]
    place = jnp.arange(media_ids.shape[0], dtype=jnp.int32)[None, :]
    run = jnp.sum(matches.astype(jnp.int32), axis=1)
    start = jnp.min(jnp.where(matches, place, media_ids.shape[0]), axis=1)
    low = jnp.where(run > 0, start - local_seq * LEN, 0)
    high = low + run
    slot = local_seq

    w_kv = jnp.concatenate([w_key, w_value], axis=1)
    w_qkv = jnp.concatenate([w_query, w_kv], axis=1)
    latent_qkv = product(latent_low, w_qkv).astype(BF16)
    kv_slots = [product(media_all, w_kv).astype(BF16)]
    attended, lse, entropy = attention_forward(slot, low, high, kv_slots, latent_qkv)

    branch = lax.psum(product(attended, w_out).astype(BF16), "head").astype(F32)
    middle = latent_float + branch
    ffn_norm, ffn_hat, ffn_inv = normalize(middle, ffn_gain, ffn_bias)
    ffn_low = ffn_norm.astype(BF16)
    before_gelu = product(ffn_low, w_up)
    activated, gelu_slope = gelu_parts(before_gelu)
    hidden = activated.astype(BF16)
    grad_before = (contract_cols(grad_all, w_down) * gelu_slope).astype(BF16)
    grad_ffn_part = contract_cols(grad_before, w_up).astype(BF16)
    grad_ffn = lax.psum(grad_ffn_part, "head").astype(F32)
    down_grad = contract_rows(hidden, grad_all).astype(BF16)
    up_grad = contract_rows(ffn_low, grad_before).astype(BF16)
    up_grad, down_grad = lax.psum((up_grad, down_grad), "seq")

    ffn_branch = product(hidden, w_down).astype(BF16)
    ffn_branch = lax.psum_scatter(ffn_branch, "head", scatter_dimension=0, tiled=True)

    def own(value):
        return lax.dynamic_slice_in_dim(value, head_index * own_rows, own_rows, axis=0)

    result = (own(middle) + ffn_branch.astype(F32)).astype(BF16)

    middle_part, ffn_gain_part, ffn_bias_part = normalize_back(
        grad_ffn, ffn_hat, ffn_inv, ffn_gain
    )
    grad_middle = grad_all.astype(F32) + middle_part
    grad_branch = grad_middle.astype(BF16)
    grad_attended = contract_cols(grad_branch, w_out).astype(BF16)
    out_grad = contract_rows(attended, grad_branch)
    back = attention_backward(
        slot,
        low,
        high,
        valid_float * weighted_scale,
        kv_slots,
        latent_qkv,
        grad_attended,
        lse,
        entropy,
    )
    latent_back, kv_back = back
    grad_media_norm = lax.psum_scatter(
        contract_cols(kv_back, w_kv).astype(BF16), "head", scatter_dimension=0, tiled=True
    ).astype(F32)
    grad_latent_part = contract_cols(latent_back, w_qkv).astype(BF16)
    grad_latent_norm = lax.psum_scatter(
        grad_latent_part, "head", scatter_dimension=0, tiled=True
    ).astype(F32)
    latent_grads = contract_rows(latent_low, latent_back)
    kv_grads = latent_grads[:, inner_width:] + contract_rows(media_all, kv_back)
    late = (
        latent_grads[:, :inner_width].astype(BF16),
        kv_grads.astype(BF16),
        out_grad.astype(BF16),
    )
    up_grad, down_grad, *late = lax.optimization_barrier((up_grad, down_grad) + late)
    query_grad, kv_grads, out_grad = lax.psum(tuple(late), "seq")

    media_rows_grad, media_gain_part, media_bias_part = normalize_back(
        grad_media_norm, media_hat, media_inv, media_gain
    )
    latent_part, latent_gain_part, latent_bias_part = normalize_back(
        grad_latent_norm, own(latent_hat), own(latent_inv), latent_gain
    )
    latents_grad = (own(grad_middle) + latent_part).astype(BF16)
    entropy_local = jnp.sum(entropy.reshape(images, -1) * valid_float[:, None])
    share = 1.0 / lax.axis_size("head")
    sums = jnp.stack(
        [
            media_gain_part,
            media_bias_part,
            latent_gain_part,
            latent_bias_part,
            ffn_gain_part * share,
            ffn_bias_part * share,
            jnp.broadcast_to(entropy_local, media_gain.shape),
            jnp.zeros_like(media_gain),
        ]
    )
    sums = sum_seq(sum_head(sums))
    return (
        result,
        sums[6, 0] * pen_scale,
        media_rows_grad.astype(BF16),
        latents_grad,
        query_grad.astype(F32),
        kv_grads[:, :inner_width].astype(F32),
        kv_grads[:, inner_width:].astype(F32),
        out_grad.astype(F32),
        up_grad.astype(F32),
        down_grad.astype(F32),
        sums[0],
        sums[1],
        sums[2],
        sums[3],
        sums[4],
        sums[5],
    )


def solution(mesh):
    rows = P(("seq", "head"), None)
    columns = P(None, "head")
    lines = P("head", None)
    quad = mesh.shape["head"] == 4 and mesh.shape["seq"] == 8
    return jax.shard_map(
        shards_quad if quad else shards_any,
        mesh=mesh,
        in_specs=(
            (rows, P("seq"), P("seq"), P("seq"), rows)
            + (columns, columns, columns, lines, columns, lines)
            + (P(),) * 6
            + (rows,)
        ),
        out_specs=(
            (rows, P(), rows, rows)
            + (columns, columns, columns, lines, columns, lines)
            + (P(),) * 6
        ),
        check_vma=False,
    )
```

```python
import jax
import jax.numpy as jnp
from jax import lax
from jax.experimental import pallas as pl
from jax.experimental.pallas import tpu as pltpu
from jax.sharding import PartitionSpec as P

HEADS = 16
HEAD_DIM = 96
LATENTS = 64
LEN = 1024
KEY_BLOCK = 256

epsilon = 1e-05
BF16 = jnp.bfloat16


def cost(microseconds):
    return pl.CostEstimate(
        flops=int(microseconds * 1.1e9), transcendentals=0, bytes_accessed=int(microseconds * 3e6)
    )


F32 = jnp.float32


def normalize(row_values, norm_gain, norm_bias):
    row_mean = jnp.mean(row_values, axis=-1, keepdims=True)
    centred = row_values - row_mean
    variance = jnp.mean(centred * centred, axis=-1, keepdims=True)
    inverse = lax.rsqrt(variance + epsilon)
    scaled = centred * inverse
    return (scaled * norm_gain + norm_bias, scaled, inverse)


def normalize_back(incoming, scaled, inverse, norm_gain):
    weighted = incoming * norm_gain
    first_mean = jnp.mean(weighted, axis=-1, keepdims=True)
    second_mean = jnp.mean(weighted * scaled, axis=-1, keepdims=True)
    outgoing = inverse * (weighted - first_mean - scaled * second_mean)
    return (outgoing, jnp.sum(incoming * scaled, axis=0), jnp.sum(incoming, axis=0))


def product(left_side, right_side):
    return jnp.dot(left_side, right_side, preferred_element_type=F32)


def contract_rows(left_side, right_side):
    return lax.dot_general(
        left_side, right_side, (((0,), (0,)), ((), ())), preferred_element_type=F32
    )


def contract_cols(left_side, right_side):
    return lax.dot_general(
        left_side, right_side, (((1,), (1,)), ((), ())), preferred_element_type=F32
    )


def gelu_parts(inputs):
    normal_cdf = 0.5 * (1.0 + lax.erf(inputs * 0.7071067811865476))
    density = jnp.exp(-0.5 * inputs * inputs) * 0.3989422804014327
    return (inputs * normal_cdf, normal_cdf + inputs * density)


def block_diagonal(rows, heads):
    lane = lax.broadcasted_iota(jnp.int32, rows.shape, 1)
    parts = []
    for head in range(heads):
        inside = (lane >= head * HEAD_DIM) & (lane < (head + 1) * HEAD_DIM)
        parts.append(jnp.where(inside, rows, jnp.zeros_like(rows)))
    return jnp.concatenate(parts, axis=0)


def take_diagonal(wide, heads):
    lane = lax.broadcasted_iota(jnp.int32, (LATENTS, wide.shape[1]), 1)
    out = wide[:LATENTS]
    for head in range(1, heads):
        out = jnp.where(lane >= head * HEAD_DIM, wide[head * LATENTS : (head + 1) * LATENTS], out)
    return out


def start_loads(kv_hbm, kv_vmem, sems):
    copies = []
    at = 0
    for i, ref in enumerate(kv_hbm):
        size = ref.shape[0]
        copies.append(pltpu.make_async_copy(ref, kv_vmem.at[pl.ds(at, size), :], sems.at[i]))
        at += size
    for copy in copies:
        copy.start()
    return copies


WINDOWS = (256, 512)


def image_rows(image):
    return pl.ds(pl.multiple_of(image * LATENTS, LATENTS), LATENTS)


def window_start(lo, size):
    return jnp.minimum(lo // 16 * 16, LEN - size)


def list_images(here, low, high):
    images = here.shape[0]
    kind = len(WINDOWS) - sum(
        (high - window_start(low, size) <= size).astype(jnp.int32) for size in WINDOWS
    )
    kind = jnp.where(here, kind, len(WINDOWS) + 1)
    number = jnp.arange(images, dtype=jnp.int32)
    key = kind * images + number
    rank = jnp.sum((key[None, :] < key[:, None]).astype(jnp.int32), axis=1)
    listed = jnp.sum(jnp.where(rank[None, :] == number[:, None], number[None, :], 0), axis=1)
    ends = [jnp.sum((kind <= i).astype(jnp.int32)).reshape(1) for i in range(len(WINDOWS) + 1)]
    return jnp.concatenate([listed, *ends])


def each_image(listed_ref, images, short, long):
    begin = 0
    for i, size in enumerate(WINDOWS):
        end = listed_ref[images + i]

        def pair(index, _, size=size, begin=begin, end=end):
            at = begin + 2 * index
            short(size, [listed_ref[at], listed_ref[jnp.minimum(at + 1, end - 1)]])
            return 0

        lax.fori_loop(0, (end - begin + 1) // 2, pair, 0)
        begin = end

    def single(index, _):
        long(listed_ref[index])
        return 0

    lax.fori_loop(begin, listed_ref[images + len(WINDOWS)], single, 0)


def attention_forward(
    slot, low, high, kv_slots, latent_qkv, offset=0, before=None, time=15.0
):
    images = slot.shape[0]
    count = len(kv_slots)
    keys = sum(kv.shape[0] for kv in kv_slots)
    width = latent_qkv.shape[1] // 3
    heads = width // HEAD_DIM
    rows = heads * LATENTS
    scale = HEAD_DIM ** (-0.5)
    given = () if before is None else tuple(before)
    here = jnp.logical_and(slot >= offset, slot < offset + keys // LEN)
    listed = list_images(here, low, high)

    def body(listed_ref, slot_ref, low_ref, high_ref, *refs):
        kv_hbm = refs[:count]
        qkv_ref = refs[count]
        given_refs = refs[count + 1 : count + 1 + len(given)]
        out_ref, lse_ref, ent_ref, kv_vmem, scores, sems = refs[count + 1 + len(given) :]
        copies = start_loads(kv_hbm, kv_vmem, sems)
        if given:
            out_ref[...] = given_refs[0][...]
            lse_ref[...] = given_refs[1][...]
            ent_ref[...] = given_refs[2][...]
        for copy in copies:
            copy.wait()

        def short(size, pair):
            for image in pair:
                at = image_rows(image)
                lo = low_ref[image]
                hi = high_ref[image]
                start = window_start(lo, size)
                place = pl.multiple_of((slot_ref[image] - offset) * LEN + start, 16)
                query = block_diagonal(qkv_ref[at, :width], heads)
                own = contract_cols(qkv_ref[at, width : 2 * width], query) * scale
                part = contract_cols(kv_vmem[pl.ds(place, size), :width], query) * scale
                key = start + lax.broadcasted_iota(jnp.int32, part.shape, 0)
                part = jnp.where((key >= lo) & (key < hi), part, -1e30)
                peak = jnp.maximum(
                    jnp.max(own, axis=0, keepdims=True), jnp.max(part, axis=0, keepdims=True)
                )
                own = own - peak
                part = part - peak
                own_exp = jnp.exp(own)
                part_exp = jnp.exp(part)
                total = jnp.sum(own_exp, axis=0, keepdims=True) + jnp.sum(
                    part_exp, axis=0, keepdims=True
                )
                moment = jnp.sum(own_exp * own, axis=0, keepdims=True) + jnp.sum(
                    part_exp * part, axis=0, keepdims=True
                )
                inverse = 1.0 / total
                log_total = jnp.log(total)
                lse_ref[image] = peak + log_total
                ent_ref[image] = log_total - moment * inverse
                wide = contract_rows((own_exp * inverse).astype(BF16), qkv_ref[at, 2 * width :])
                wide = wide + contract_rows(
                    (part_exp * inverse).astype(BF16), kv_vmem[pl.ds(place, size), width:]
                )
                out_ref[at, :] = take_diagonal(wide, heads).astype(BF16)

        def long(image):
            at = image_rows(image)
            base = (slot_ref[image] - offset) * LEN
            lo = low_ref[image]
            hi = high_ref[image]
            first = lo // KEY_BLOCK
            last = (hi + KEY_BLOCK - 1) // KEY_BLOCK
            query = block_diagonal(qkv_ref[at, :width], heads)
            own = contract_cols(qkv_ref[at, width : 2 * width], query) * scale
            peak = jnp.max(own, axis=0, keepdims=True)

            def first_pass(block, peak):
                row = pl.multiple_of(base + block * KEY_BLOCK, KEY_BLOCK)
                part = contract_cols(kv_vmem[pl.ds(row, KEY_BLOCK), :width], query) * scale
                key = block * KEY_BLOCK + lax.broadcasted_iota(jnp.int32, part.shape, 0)
                part = jnp.where((key >= lo) & (key < hi), part, -1e30)
                to = pl.multiple_of((block - first) * KEY_BLOCK, KEY_BLOCK)
                scores[pl.ds(to, KEY_BLOCK), :] = part
                return jnp.maximum(peak, jnp.max(part, axis=0, keepdims=True))

            peak = lax.fori_loop(first, last, first_pass, peak)
            own = own - peak
            own_exp = jnp.exp(own)
            total = jnp.sum(own_exp, axis=0, keepdims=True)
            moment = jnp.sum(own_exp * own, axis=0, keepdims=True)

            def second_pass(block, carry):
                total, moment = carry
                to = pl.multiple_of((block - first) * KEY_BLOCK, KEY_BLOCK)
                part = scores[pl.ds(to, KEY_BLOCK), :] - peak
                part_exp = jnp.exp(part)
                scores[pl.ds(to, KEY_BLOCK), :] = part_exp
                return (
                    total + jnp.sum(part_exp, axis=0, keepdims=True),
                    moment + jnp.sum(part_exp * part, axis=0, keepdims=True),
                )

            total, moment = lax.fori_loop(first, last, second_pass, (total, moment))
            inverse = 1.0 / total
            log_total = jnp.log(total)
            lse_ref[image] = peak + log_total
            ent_ref[image] = log_total - moment * inverse
            wide = contract_rows((own_exp * inverse).astype(BF16), qkv_ref[at, 2 * width :])

            def third_pass(block, wide):
                to = pl.multiple_of((block - first) * KEY_BLOCK, KEY_BLOCK)
                row = pl.multiple_of(base + block * KEY_BLOCK, KEY_BLOCK)
                low_prob = (scores[pl.ds(to, KEY_BLOCK), :] * inverse).astype(BF16)
                return wide + contract_rows(low_prob, kv_vmem[pl.ds(row, KEY_BLOCK), width:])

            wide = lax.fori_loop(first, last, third_pass, wide)
            out_ref[at, :] = take_diagonal(wide, heads).astype(BF16)

        each_image(listed_ref, images, short, long)

    shapes = (
        jax.ShapeDtypeStruct((images * LATENTS, width), BF16),
        jax.ShapeDtypeStruct((images, 1, rows), F32),
        jax.ShapeDtypeStruct((images, 1, rows), F32),
    )
    scalar = pl.BlockSpec(memory_space=pltpu.SMEM)
    vmem = pl.BlockSpec(memory_space=pltpu.VMEM)
    return pl.pallas_call(
        body,
        out_shape=shapes,
        in_specs=[scalar] * 4
        + [pl.BlockSpec(memory_space=pl.ANY)] * count
        + [vmem] * (1 + len(given)),
        out_specs=(vmem,) * 3,
        scratch_shapes=[
            pltpu.VMEM((keys, 2 * width), BF16),
            pltpu.VMEM((LEN, rows), F32),
            pltpu.SemaphoreType.DMA((count,)),
        ],
        compiler_params=pltpu.CompilerParams(vmem_limit_bytes=48 << 20),
        cost_estimate=cost(time),
        name="attention_forward",
    )(listed, slot, low, high, *kv_slots, latent_qkv, *given)


def attention_backward(slot, low, high, weight, kv_slots, latent_qkv, grad_out, lse, entropy):
    images = slot.shape[0]
    count = len(kv_slots)
    keys = sum(kv.shape[0] for kv in kv_slots)
    width = latent_qkv.shape[1] // 3
    heads = width // HEAD_DIM
    rows = heads * LATENTS
    scale = HEAD_DIM ** (-0.5)

    listed = list_images(jnp.full((images,), True), low, high)

    def body(listed_ref, slot_ref, low_ref, high_ref, weight_ref, *refs):
        kv_hbm = refs[:count]
        qkv_ref, grad_ref, lse_ref, ent_ref = refs[count : count + 4]
        own_out, key_out, kv_vmem, probs, slopes, totals, sems = refs[count + 4 :]
        copies = start_loads(kv_hbm, kv_vmem, sems)
        totals[...] = jnp.zeros_like(totals)
        for copy in copies:
            copy.wait()

        def short(size, pair):
            for which, image in enumerate(pair):
                repeated = jnp.logical_and(which == 1, pair[0] == image)
                at = image_rows(image)
                lo = low_ref[image]
                hi = high_ref[image]
                pull = weight_ref[image]
                start = window_start(lo, size)
                place = pl.multiple_of(slot_ref[image] * LEN + start, 16)
                window = pl.ds(place, size)
                query = block_diagonal(qkv_ref[at, :width], heads)
                grad = block_diagonal(grad_ref[at, :], heads)
                log_total = lse_ref[image]
                ent = ent_ref[image]
                own_key = qkv_ref[at, width : 2 * width]
                own_log = contract_cols(own_key, query) * scale - log_total
                own_prob = jnp.exp(own_log)
                own_slope = contract_cols(qkv_ref[at, 2 * width :], grad)
                part = contract_cols(kv_vmem[window, :width], query) * scale
                key = start + lax.broadcasted_iota(jnp.int32, part.shape, 0)
                part = jnp.where((key >= lo) & (key < hi), part - log_total, -1e30)
                prob = jnp.exp(part)
                slope = contract_cols(kv_vmem[window, width:], grad)
                centre = jnp.sum(own_prob * own_slope, axis=0, keepdims=True)
                centre = centre + jnp.sum(prob * slope, axis=0, keepdims=True)
                own_low = own_prob * (own_slope - pull * (own_log + ent) - centre)
                own_low = own_low.astype(BF16)
                low_grad = (prob * (slope - pull * (part + ent) - centre)).astype(BF16)
                grad_query = contract_rows(own_low, own_key)
                grad_query = grad_query + contract_rows(low_grad, kv_vmem[window, :width])
                own_out[at, width : 2 * width] = (product(own_low, query) * scale).astype(BF16)
                own_out[at, 2 * width :] = product(own_prob.astype(BF16), grad).astype(BF16)
                once = jnp.where(repeated, 0.0, 1.0)
                totals[window, :width] += product(low_grad, query) * (scale * once)
                totals[window, width:] += product(prob.astype(BF16), grad) * once
                own_out[at, :width] = (take_diagonal(grad_query, heads) * scale).astype(BF16)

        def long(image):
            at = image_rows(image)
            base = slot_ref[image] * LEN
            lo = low_ref[image]
            hi = high_ref[image]
            pull = weight_ref[image]
            first = lo // KEY_BLOCK
            last = (hi + KEY_BLOCK - 1) // KEY_BLOCK
            query = block_diagonal(qkv_ref[at, :width], heads)
            grad = block_diagonal(grad_ref[at, :], heads)
            log_total = lse_ref[image]
            ent = ent_ref[image]
            own_key = qkv_ref[at, width : 2 * width]
            own_log = contract_cols(own_key, query) * scale - log_total
            own_prob = jnp.exp(own_log)
            own_slope = contract_cols(qkv_ref[at, 2 * width :], grad)
            centre = jnp.sum(own_prob * own_slope, axis=0, keepdims=True)
            own_slope = own_slope - pull * (own_log + ent)

            def first_pass(block, centre):
                row = pl.multiple_of(base + block * KEY_BLOCK, KEY_BLOCK)
                to = pl.multiple_of((block - first) * KEY_BLOCK, KEY_BLOCK)
                part = contract_cols(kv_vmem[pl.ds(row, KEY_BLOCK), :width], query) * scale
                key = block * KEY_BLOCK + lax.broadcasted_iota(jnp.int32, part.shape, 0)
                part = jnp.where((key >= lo) & (key < hi), part - log_total, -1e30)
                prob = jnp.exp(part)
                slope = contract_cols(kv_vmem[pl.ds(row, KEY_BLOCK), width:], grad)
                probs[pl.ds(to, KEY_BLOCK), :] = prob
                slopes[pl.ds(to, KEY_BLOCK), :] = slope - pull * (part + ent)
                return centre + jnp.sum(prob * slope, axis=0, keepdims=True)

            centre = lax.fori_loop(first, last, first_pass, centre)
            own_low = (own_prob * (own_slope - centre)).astype(BF16)
            grad_query = contract_rows(own_low, own_key)
            own_out[at, width : 2 * width] = (product(own_low, query) * scale).astype(BF16)
            own_out[at, 2 * width :] = product(own_prob.astype(BF16), grad).astype(BF16)

            def second_pass(block, grad_query):
                row = pl.multiple_of(base + block * KEY_BLOCK, KEY_BLOCK)
                to = pl.multiple_of((block - first) * KEY_BLOCK, KEY_BLOCK)
                prob = probs[pl.ds(to, KEY_BLOCK), :]
                low_grad = (prob * (slopes[pl.ds(to, KEY_BLOCK), :] - centre)).astype(BF16)
                totals[pl.ds(row, KEY_BLOCK), :width] += product(low_grad, query) * scale
                totals[pl.ds(row, KEY_BLOCK), width:] += product(prob.astype(BF16), grad)
                return grad_query + contract_rows(
                    low_grad, kv_vmem[pl.ds(row, KEY_BLOCK), :width]
                )

            grad_query = lax.fori_loop(first, last, second_pass, grad_query)
            own_out[at, :width] = (take_diagonal(grad_query, heads) * scale).astype(BF16)

        each_image(listed_ref, images, short, long)
        key_out[...] = totals[...].astype(BF16)

    scalar = pl.BlockSpec(memory_space=pltpu.SMEM)
    vmem = pl.BlockSpec(memory_space=pltpu.VMEM)
    return pl.pallas_call(
        body,
        out_shape=(
            jax.ShapeDtypeStruct((images * LATENTS, 3 * width), BF16),
            jax.ShapeDtypeStruct((keys, 2 * width), BF16),
        ),
        in_specs=[scalar] * 5 + [pl.BlockSpec(memory_space=pl.ANY)] * count + [vmem] * 4,
        out_specs=(vmem, vmem),
        scratch_shapes=[
            pltpu.VMEM((keys, 2 * width), BF16),
            pltpu.VMEM((LEN, rows), F32),
            pltpu.VMEM((LEN, rows), F32),
            pltpu.VMEM((keys, 2 * width), F32),
            pltpu.SemaphoreType.DMA((count,)),
        ],
        compiler_params=pltpu.CompilerParams(vmem_limit_bytes=56 << 20),
        cost_estimate=cost(0.5),
        name="attention_backward",
    )(listed, slot, low, high, weight, *kv_slots, latent_qkv, grad_out, lse, entropy)


ROW_BLOCK = 256


def call(body, grid, inputs, outputs, name, time=5.0, scratch=()):
    return pl.pallas_call(
        body,
        out_shape=tuple(jax.ShapeDtypeStruct(shape, dtype) for shape, dtype, _ in outputs),
        grid=(grid,),
        in_specs=[spec for _, spec in inputs],
        out_specs=tuple(spec for _, _, spec in outputs),
        scratch_shapes=list(scratch),
        compiler_params=pltpu.CompilerParams(
            dimension_semantics=("arbitrary",), vmem_limit_bytes=56 << 20
        ),
        cost_estimate=cost(time),
        name=name,
    )(*[value for value, _ in inputs])


def by_rows(width, move=lambda i: i, size=ROW_BLOCK):
    return pl.BlockSpec((size, width), lambda i: (move(i), 0))


def whole(value):
    return pl.BlockSpec(value.shape, lambda i: (0,) * value.ndim, pipeline_mode=pl.Buffered(1))


def stacked(values):
    steps = values[0].shape[0] // ROW_BLOCK
    return [
        (value, by_rows(value.shape[1], lambda i, k=k: jnp.clip(i - k * steps, 0, steps - 1)))
        for k, value in enumerate(values)
    ]


def stacked_rows(refs, values):
    steps = values[0].shape[0] // ROW_BLOCK
    rows = refs[0][...]
    for k in range(1, len(values)):
        rows = jnp.where(pl.program_id(0) >= k * steps, refs[k][...], rows)
    return rows


def low_half(i):
    return jnp.minimum(i, 1)


def high_half(i):
    return jnp.maximum(i - 2, 0)


def pair_inputs(pair, rest):
    return [(pair, by_rows(pair.shape[1], low_half)), (rest, by_rows(rest.shape[1], high_half))]


def pick(pair_ref, rest_ref):
    return jnp.where(pl.program_id(0) < 2, pair_ref[...], rest_ref[...])


def put_halves(low_ref, high_ref, value):
    @pl.when(pl.program_id(0) < 2)
    def _():
        low_ref[...] = value

    @pl.when(pl.program_id(0) >= 2)
    def _():
        high_ref[...] = value


def half_outputs(width):
    return [
        ((2 * ROW_BLOCK, width), BF16, by_rows(width, low_half)),
        ((2 * ROW_BLOCK, width), BF16, by_rows(width, high_half)),
    ]


def add_up(ref, value):
    total = jnp.sum(value, axis=0, keepdims=True)

    @pl.when(pl.program_id(0) == 0)
    def _():
        ref[...] = total

    @pl.when(pl.program_id(0) > 0)
    def _():
        ref[...] += total


def sum_output(width):
    return ((1, width), F32, pl.BlockSpec((1, width), lambda i: (0, 0)))


def norm_project(rows, gain, bias, weights, time=7.5):
    width, wide = rows[0].shape[1], weights.shape[1]
    count = sum(part.shape[0] for part in rows)

    def body(*refs):
        value = stacked_rows(refs, rows)
        gain_ref, bias_ref, weight_ref, out_ref, norm_ref = refs[len(rows) :]
        norm = normalize(value.astype(F32), gain_ref[...], bias_ref[...])[0].astype(BF16)
        norm_ref[...] = norm
        out_ref[...] = product(norm, weight_ref[...]).astype(BF16)

    return call(
        body,
        count // ROW_BLOCK,
        stacked(rows) + [(gain, whole(gain)), (bias, whole(bias)), (weights, whole(weights))],
        [((count, wide), BF16, by_rows(wide)), ((count, width), BF16, by_rows(width))],
        "norm_project",
        time,
    )


def cotangent_down(pair, rest, weights):
    wide = weights.shape[0]

    def body(pair_ref, rest_ref, weight_ref, out_ref):
        out_ref[...] = contract_cols(pick(pair_ref, rest_ref), weight_ref[...])

    return call(
        body,
        4,
        pair_inputs(pair, rest) + [(weights, whole(weights))],
        [((4 * ROW_BLOCK, wide), F32, by_rows(wide))],
        "cotangent_down",
        10.0,
    )[0]


def feed_forward(attended, out_weights, latent_rows, pulled, w_up, gain, bias):
    width = attended[0].shape[1]
    dim = w_up.shape[0]
    wide = w_up.shape[1]

    def body(*refs):
        own, near, across, beyond, first_ref, second_ref, lat_ref, lat_rest, pulled_ref = refs[:9]
        up_ref, gain_ref, bias_ref, middle_ref, ffn_ref, hidden_ref, grad_ref, low_ref, high_ref = (
            refs[9:]
        )
        rows = pick(lat_ref, lat_rest).astype(F32)
        rows = rows + product(jnp.concatenate([own[...], near[...]], axis=1), first_ref[...])
        rows = rows + product(jnp.concatenate([across[...], beyond[...]], axis=1), second_ref[...])
        middle_ref[...] = rows
        norm = normalize(rows, gain_ref[...], bias_ref[...])[0].astype(BF16)
        ffn_ref[...] = norm
        step = wide // 3
        for i in range(3):
            at = slice(i * step, (i + 1) * step)
            activated, slope = gelu_parts(product(norm, up_ref[:, at]))
            hidden_ref[:, at] = activated.astype(BF16)
            grad_ref[:, at] = (pulled_ref[:, at] * slope).astype(BF16)
        back = contract_cols(grad_ref[...], up_ref[...]).astype(BF16)
        put_halves(low_ref, high_ref, back)

    count = 4 * ROW_BLOCK
    return call(
        body,
        4,
        [
            (attended[0], by_rows(width)),
            (attended[1], by_rows(width, lambda i: i ^ 2)),
            (attended[2], by_rows(width, lambda i: i ^ 1)),
            (attended[3], by_rows(width, lambda i: i ^ 3)),
            (out_weights[0], whole(out_weights[0])),
            (out_weights[1], whole(out_weights[1])),
        ]
        + pair_inputs(*latent_rows)
        + [
            (pulled, by_rows(wide)),
            (w_up, whole(w_up)),
            (gain, whole(gain)),
            (bias, whole(bias)),
        ],
        [
            ((count, dim), F32, by_rows(dim)),
            ((count, dim), BF16, by_rows(dim)),
            ((count, wide), BF16, by_rows(wide)),
            ((count, wide), BF16, by_rows(wide)),
        ]
        + half_outputs(dim),
        "feed_forward",
        27.0,
    )


def part(value, rows=None, at=0, columns=slice(None)):
    return (value, value.shape[0] if rows is None else rows, at, columns)


def grad_halves(side, pairs, name):
    half = pairs[0][0].shape[1] // 2
    inputs = []
    for left, rights in pairs:
        inputs.append(
            (
                left,
                pl.BlockSpec(
                    (left.shape[0], half),
                    lambda i, x: (0, (i + 1 + x[0]) % 2),
                ),
            )
        )
        for value, rows, at, _ in rights:
            spec = pl.BlockSpec(
                (rows, value.shape[1]), lambda i, x, at=at: (at, 0), pipeline_mode=pl.Buffered(1)
            )
            inputs.append((value, spec))
    value, _, _, columns = pairs[0][1][0]
    wide = len(range(*columns.indices(value.shape[1])))

    def body(x_ref, *refs):
        total = None
        index = 0
        for left, rights in pairs:
            left_ref = refs[index]
            row = 0
            for i, (_, rows, _, columns) in enumerate(rights):
                value = contract_rows(
                    left_ref[row : row + rows, :], refs[index + 1 + i][:, columns]
                )
                row += rows
                total = value if total is None else total + value
            index += 1 + len(rights)
        put_sides(refs[-2], refs[-1], total.astype(BF16))

    return side_call(body, side, inputs, half, wide, name)


def put_sides(other_ref, mine_ref, value):
    @pl.when(pl.program_id(0) == 0)
    def _():
        other_ref[...] = value

    @pl.when(pl.program_id(0) == 1)
    def _():
        mine_ref[...] = value


def side_call(body, side, inputs, half, wide, name):
    out = pl.BlockSpec((half, wide), lambda i, x: (0, 0))
    return pl.pallas_call(
        body,
        out_shape=(jax.ShapeDtypeStruct((half, wide), BF16),) * 2,
        grid_spec=pltpu.PrefetchScalarGridSpec(
            num_scalar_prefetch=1,
            grid=(2,),
            in_specs=[spec for _, spec in inputs],
            out_specs=(out, out),
        ),
        compiler_params=pltpu.CompilerParams(
            dimension_semantics=("arbitrary",), vmem_limit_bytes=56 << 20
        ),
        cost_estimate=cost(0.5),
        name=name,
    )(side, *[value for value, _ in inputs])


def late_grads(side, latent_back, latent_low, attended, grad_branch):
    width = attended.shape[1]
    wide = grad_branch.shape[1]

    def body(x_ref, back_ref, low_ref, attended_ref, branch_ref, other_ref, mine_ref):
        which = (pl.program_id(0) + 1 + x_ref[0]) % 2

        @pl.when(which == 0)
        def _():
            value = contract_rows(back_ref[...], low_ref[...]).astype(BF16)
            put_sides(other_ref, mine_ref, value)

        @pl.when(which == 1)
        def _():
            value = contract_rows(attended_ref[...], branch_ref[...]).astype(BF16)
            put_sides(other_ref, mine_ref, value)

    inputs = [
        (
            value,
            pl.BlockSpec(
                (value.shape[0], min(value.shape[1], size)),
                lambda i, x: (0, 0),
                pipeline_mode=pl.Buffered(1),
            ),
        )
        for value, size in (
            (latent_back, width),
            (latent_low, wide),
            (attended, width),
            (grad_branch, wide),
        )
    ]
    return side_call(body, side, inputs, width, wide, "late_grads")


def join_rows(place, parts, splits):
    size = parts[0].shape[0]
    count = len(parts)

    def body(place_ref, *refs):
        step = pl.program_id(0)
        for i in range(count):

            @pl.when(step == i)
            def _():
                for (first, last), out_ref in zip(splits, refs[count:]):
                    out_ref[...] = refs[i][:, first:last].astype(F32)

    inputs = [
        pl.BlockSpec(value.shape, lambda i, p: (0, 0), pipeline_mode=pl.Buffered(1))
        for value in parts
    ]
    return pl.pallas_call(
        body,
        out_shape=tuple(
            jax.ShapeDtypeStruct((count * size, last - first), F32) for first, last in splits
        ),
        grid_spec=pltpu.PrefetchScalarGridSpec(
            num_scalar_prefetch=1,
            grid=(count,),
            in_specs=inputs,
            out_specs=tuple(
                pl.BlockSpec((size, last - first), lambda i, p: (i ^ p[0], 0))
                for first, last in splits
            ),
        ),
        compiler_params=pltpu.CompilerParams(
            dimension_semantics=("arbitrary",), vmem_limit_bytes=56 << 20
        ),
        cost_estimate=cost(0.5),
        name="join_rows",
    )(place, *parts)


def join_late(place, parts):
    size, dim = parts[0].shape

    def body(place_ref, own_ref, pair_ref, side_ref, last_ref, query_ref, out_ref):
        odd = place_ref[0] % 2 == 1
        first = place_ref[0] < 2

        def rows(low_ref, high_ref):
            low, high = low_ref[...], high_ref[...]
            return jnp.concatenate(
                [jnp.where(odd, high, low), jnp.where(odd, low, high)], axis=0
            ).astype(F32)

        mine, other = rows(own_ref, pair_ref), rows(side_ref, last_ref)
        query_ref[...] = jnp.where(first, mine, other).T
        out_ref[...] = jnp.where(first, other, mine)

    spec = pl.BlockSpec((size, 384), lambda i, p: (0, i))
    return pl.pallas_call(
        body,
        out_shape=(
            jax.ShapeDtypeStruct((dim, 2 * size), F32),
            jax.ShapeDtypeStruct((2 * size, dim), F32),
        ),
        grid_spec=pltpu.PrefetchScalarGridSpec(
            num_scalar_prefetch=1,
            grid=(dim // 384,),
            in_specs=[spec] * 4,
            out_specs=(
                pl.BlockSpec((384, 2 * size), lambda i, p: (i, 0)),
                pl.BlockSpec((2 * size, 384), lambda i, p: (0, i)),
            ),
        ),
        compiler_params=pltpu.CompilerParams(dimension_semantics=("arbitrary",)),
        cost_estimate=cost(0.5),
        name="join_late",
    )(place, *parts)


def project_halves(rows, weights, transposed, name):
    wide = weights.shape[0] if transposed else weights.shape[1]

    def body(rows_ref, weight_ref, low_ref, high_ref):
        if transposed:
            out = contract_cols(rows_ref[...], weight_ref[...])
        else:
            out = product(rows_ref[...], weight_ref[...])
        put_halves(low_ref, high_ref, out.astype(BF16))

    return call(
        body,
        4,
        [(rows, by_rows(rows.shape[1])), (weights, whole(weights))],
        half_outputs(wide),
        name,
        0.5,
    )


def project_slot(rows, slot, weights, added=()):
    wide = weights.shape[0]
    blocks_in = LEN // ROW_BLOCK

    def body(rows_ref, weight_ref, *refs):
        out = contract_cols(rows_ref[...], weight_ref[...])
        if added:
            out = out + stacked_rows(refs, added).astype(F32)
        refs[-1][...] = out.astype(BF16)

    return call(
        body,
        blocks_in,
        [
            (rows, by_rows(rows.shape[1], lambda i: i + slot * blocks_in)),
            (weights, whole(weights)),
        ]
        + (stacked(added) if added else []),
        [((LEN, wide), BF16, by_rows(wide))],
        "project_slot",
        0.5,
    )[0]


def middle_back(grads, middle, cotangents, gain, bias, w_out):
    dim = middle.shape[1]
    width = w_out.shape[0]

    def body(*refs):
        grad_ref, third_ref, fourth_ref, middle_ref, cot_ref, cot_rest = refs[:6]
        gain_ref, bias_ref, out_ref, branch_ref, own_ref, attended_ref, gain_sum, bias_sum = refs[6:]
        step = pl.program_id(0)
        grad = jnp.where(step == 2, third_ref[...], fourth_ref[...])
        grad = jnp.where(step < 2, grad_ref[...], grad).astype(F32)
        _, hat, inv = normalize(middle_ref[...], gain_ref[...], bias_ref[...])
        weighted = grad * gain_ref[...]
        moved = grad * hat
        first_mean = jnp.mean(weighted, axis=-1, keepdims=True)
        second_mean = jnp.mean(weighted * hat, axis=-1, keepdims=True)
        value = pick(cot_ref, cot_rest).astype(F32) + inv * (
            weighted - first_mean - hat * second_mean
        )
        low = value.astype(BF16)
        branch_ref[...] = low
        attended_ref[...] = contract_cols(low, out_ref[...]).astype(BF16)
        add_up(gain_sum, moved)
        add_up(bias_sum, grad)

        @pl.when(pl.program_id(0) == 0)
        def _():
            own_ref[...] = value

    count = 4 * ROW_BLOCK
    return call(
        body,
        4,
        [(grads[0], by_rows(dim, low_half))]
        + [(grad, whole(grad)) for grad in grads[1:]]
        + [(middle, by_rows(dim))]
        + pair_inputs(*cotangents)
        + [(gain, whole(gain)), (bias, whole(bias)), (w_out, whole(w_out))],
        [
            ((count, dim), BF16, by_rows(dim)),
            ((ROW_BLOCK, dim), F32, by_rows(dim, lambda i: 0)),
            ((count, width), BF16, by_rows(width)),
            sum_output(dim),
            sum_output(dim),
        ],
        "middle_back",
        0.5,
    )


def norm_back(near, far, rows, gain, bias, added=None):
    dim = rows.shape[1]
    extra = [] if added is None else [(added, by_rows(dim))]

    def body(*refs):
        near_ref, far_ref, rows_ref, gain_ref, bias_ref = refs[:5]
        out_ref, gain_sum, bias_sum = refs[-3:]
        grad = near_ref[...].astype(F32) + far_ref[...].astype(F32)
        _, hat, inv = normalize(rows_ref[...].astype(F32), gain_ref[...], bias_ref[...])
        weighted = grad * gain_ref[...]
        first_mean = jnp.mean(weighted, axis=-1, keepdims=True)
        second_mean = jnp.mean(weighted * hat, axis=-1, keepdims=True)
        value = inv * (weighted - first_mean - hat * second_mean)
        if extra:
            value = refs[5][...] + value
        out_ref[...] = value.astype(BF16)
        add_up(gain_sum, grad * hat)
        add_up(bias_sum, grad)

    return call(
        body,
        rows.shape[0] // ROW_BLOCK,
        [(near, by_rows(dim)), (far, by_rows(dim)), (rows, by_rows(dim))]
        + [(gain, whole(gain)), (bias, whole(bias))]
        + extra,
        [(rows.shape, BF16, by_rows(dim)), sum_output(dim), sum_output(dim)],
        "norm_back",
        0.5,
    )


def swap_head(value, bit):
    size = lax.axis_size("head")
    return lax.ppermute(value, "head", [(i, i ^ bit) for i in range(size)])


def swap_seq(value, bit):
    size = lax.axis_size("seq")
    return lax.ppermute(value, "seq", [(i, i ^ bit) for i in range(size)])


def sum_seq(value):
    size = lax.axis_size("seq")
    bit = 1
    while bit < size:
        value = value + swap_seq(value, bit)
        bit *= 2
    return value


def sum_head(value):
    size = lax.axis_size("head")
    bit = 1
    while bit < size:
        value = value + swap_head(value, bit)
        bit *= 2
    return value


OVER_Z = (False, False, True, False)


class Values:
    pass


class Order:
    def __init__(self):
        self.last = None

    def __call__(self, step, *values):
        if self.last is not None:
            *values, _ = lax.optimization_barrier((*values, self.last))
        out = step(*values)
        self.last = out[0] if isinstance(out, (tuple, list)) else out
        return out

    def gate(self, value):
        return lax.optimization_barrier((value, self.last))[0]

    def pin(self, value):
        self.last = self.gate(value)
        return self.last


class SeqSum:
    def __init__(self, order, halves, over_z):
        other, self.mine = halves
        self.order = order
        self.over_z = over_z
        self.moving = swap_seq(other, 1)

    def split(self):
        odd = lax.axis_index("seq") // 2 % 2
        quarter = self.mine.shape[0] // 2

        def run(mine, moving):
            total = mine + moving
            return [
                lax.dynamic_slice_in_dim(total, which * quarter, quarter, axis=0)
                for which in (1 - odd, odd)
            ]

        other, self.mine = self.order(run, self.mine, self.moving)
        self.moving = swap_seq(other, 2)

    def across(self):
        self.mine = self.order(lambda v, r: v + r, self.mine, self.moving)
        self.moving = swap_seq(self.mine, 4)

    def spread(self):
        self.mine = self.order(lambda v, r: v + r, self.mine, self.moving)
        self.side = swap_seq(self.mine, 1)
        self.pair = swap_seq(self.mine, 2)

    def corner(self):
        if self.over_z:
            self.side = self.order.pin(self.side)
            self.last = swap_seq(self.side, 2)
        else:
            self.pair = self.order.pin(self.pair)
            self.last = swap_seq(self.pair, 1)

    def pieces(self):
        return [self.mine, self.pair, self.side, self.last]


def blocks(value, count):
    size = value.shape[0] // count
    return [value[i * size : (i + 1) * size] for i in range(count)]


def shards_quad(
    media,
    media_ids,
    image_seq,
    image_valid,
    latents,
    w_query,
    w_key,
    w_value,
    w_out,
    w_up,
    w_down,
    media_gain,
    media_bias,
    latent_gain,
    latent_bias,
    ffn_gain,
    ffn_bias,
    cotangent,
):
    seq_index = lax.axis_index("seq")
    head_index = lax.axis_index("head")
    seq_size = lax.axis_size("seq")
    images = image_seq.shape[0]
    sequences = media_ids.shape[0] // LEN
    own_rows = latents.shape[0]
    width = w_query.shape[1]
    dim = media.shape[1]
    order = Order()
    media_gain, media_bias, latent_gain, latent_bias, ffn_gain, ffn_bias = (
        value.reshape(1, dim)
        for value in (media_gain, media_bias, latent_gain, latent_bias, ffn_gain, ffn_bias)
    )

    slots = jnp.array([0, 2, 1, 3], jnp.int32)
    per_device = images // 4
    which = ((slots ^ head_index)[:, None] * per_device + jnp.arange(per_device)[None, :]).reshape(-1)
    owners = seq_index * images + which
    local_seq = jnp.take(image_seq, which) - seq_index * sequences
    valid_float = jnp.take(image_valid, which).astype(F32)
    matches = media_ids[None, :] == owners[:, None]
    place = jnp.arange(media_ids.shape[0], dtype=jnp.int32)[None, :]
    run = jnp.sum(matches.astype(jnp.int32), axis=1)
    start = jnp.min(jnp.where(matches, place, media_ids.shape[0]), axis=1)
    low = jnp.where(run > 0, start - local_seq * LEN, 0)
    high = low + run
    slot = local_seq ^ head_index

    share = width // seq_size
    used = jnp.full((16, dim), jnp.sum(valid_float)).astype(BF16)
    out_piece = jnp.concatenate(
        [lax.dynamic_slice_in_dim(w_out, seq_index * share, share, axis=0), used], axis=0
    )
    latents_across = swap_head(latents, 2)
    raw_near = swap_head(media, 1)
    out_piece = swap_head(out_piece, 2)
    out_near = swap_head(w_out, 1)

    w_kv = jnp.concatenate([w_key, w_value], axis=1)
    w_qkv = jnp.concatenate([w_query, w_kv], axis=1)

    def media_step(rows, weights):
        return norm_project([rows], media_gain, media_bias, weights, 1.0)

    def stack(*values):
        return jnp.concatenate(values, axis=0)

    def add(left, right):
        return left + right

    kv_own, norm_own = order(media_step, media, w_kv)
    raw = order(lambda v: tuple(blocks(v, 2)), media)
    latent_pair = order(stack, latents, latents_across)
    latent_rest = swap_head(latent_pair, 1)
    raw = lax.optimization_barrier((*raw, latent_pair, out_piece))[:2]
    raw_across = [swap_head(piece, 2) for piece in raw]
    kv_near, norm_near = order(media_step, raw_near, w_kv)
    cotangent_across = swap_head(order.gate(cotangent), 2)
    out_far = lax.all_gather(order.gate(out_piece), "seq", axis=0, tiled=True)
    latent_qkv, latent_low = order(
        lambda v, r, w: norm_project([v, r], latent_gain, latent_bias, w, 1.0),
        latent_pair,
        latent_rest,
        w_qkv,
    )
    near_part = order(
        lambda *v: attention_forward(*v[:3], v[3:5], v[5], time=1.0),
        slot,
        low,
        high,
        kv_own,
        kv_near,
        latent_qkv,
    )
    out_first = order(stack, w_out, out_near)
    across, beyond = [], []
    for piece in raw_across:
        piece = order.gate(piece)
        moved = [swap_head(half, 1) for half in blocks(piece, 2)]
        across.append(order(media_step, piece, w_kv))
        beyond.append(
            order(
                lambda v, r, w: norm_project([v, r], media_gain, media_bias, w, 1.0), *moved, w_kv
            )
        )
    far = across + beyond
    out_far = order.gate(out_far)
    pieces = blocks(out_far, seq_size)
    count_all = sum(piece[share, 0].astype(F32) for piece in pieces)
    out_far = order(stack, *[piece[:share] for piece in pieces])
    out_beyond = swap_head(out_far, 1)
    pen_scale = 1.0 / (HEADS * LATENTS * count_all)
    weighted_scale = 4.0 * images * seq_size / count_all
    attended, lse, entropy = order(
        lambda *v: attention_forward(*v[:3], v[3:7], v[7], 2, v[8:]),
        slot,
        low,
        high,
        *[kv for kv, _ in far],
        latent_qkv,
        *near_part,
    )
    attended_across = swap_head(attended, 2)
    attended_near = swap_head(attended, 1)
    cotangent_pair = order(stack, cotangent, cotangent_across)
    cotangent_rest = swap_head(cotangent_pair, 1)
    out_second = order(stack, out_far, out_beyond)
    pulled = order(cotangent_down, cotangent_pair, cotangent_rest, w_down)
    attended_across = order.gate(attended_across)
    attended_beyond = swap_head(attended_across, 1)
    middle, ffn_low, hidden, grad_before, lower, upper = order(
        lambda *v: feed_forward(v[:4], v[4:6], v[6:8], v[8], v[9], ffn_gain, ffn_bias),
        attended,
        attended_near,
        attended_across,
        attended_beyond,
        out_first,
        out_second,
        latent_pair,
        latent_rest,
        pulled,
        w_up,
    )
    side = (seq_index % 2).reshape(1)
    place = (seq_index % 2 * 2 + seq_index // 2 % 2).reshape(1)
    v = Values()
    v.upper = swap_head(upper, 1)

    def lowadd():
        v.lower = order(add, lower, v.upper)
        v.Y = swap_head(v.lower, 2)

    def sum_steps(grads, over_z):
        made = []

        def start():
            made.append(SeqSum(order, grads(), over_z))

        return (
            start,
            lambda: made[0].split(),
            lambda: made[0].across(),
            lambda: made[0].spread(),
            lambda: made[0].corner(),
            lambda: made[0].pieces(),
        )

    def down_grads():
        return order(
            lambda x, h, g, r: grad_halves(x, [(h, [part(g), part(r)])], "down_grad"),
            side,
            hidden,
            cotangent_pair,
            cotangent_rest,
        )

    def up_grads():
        return order(
            lambda x, h, g: grad_halves(x, [(h, [part(g)])], "up_grad"),
            side,
            ffn_low,
            grad_before,
        )

    half_len = LEN // 2
    norms = (norm_own, norm_near, *[norm for _, norm in far])

    def key_pairs(x, own, near, first, second, third, fourth, back, latent, latent_part):
        pairs = [(own, [part(back, LEN, 0)]), (near, [part(back, LEN, 1)])]
        for i, rows in enumerate((first, second, third, fourth)):
            pairs.append((rows, [part(back, half_len, 4 + i)]))
        pairs.append((latent, [part(latent_part, columns=slice(width, None))]))
        return grad_halves(x, pairs, "key_grad")

    def key_grads():
        return order(key_pairs, side, *norms, v.kv_back, latent_low, v.latent_back)

    d, d_1, d_2, d_3, d_4, down_parts = sum_steps(down_grads, OVER_Z[0])
    u, u_1, u_2, u_3, u_4, up_parts = sum_steps(up_grads, OVER_Z[1])
    k, k_1, k_2, k_3, k_4, key_parts = sum_steps(key_grads, OVER_Z[2])
    l, l_1, l_2, l_3, l_4, late_parts = sum_steps(
        lambda: order(late_grads, side, v.latent_back, latent_low, attended, v.grad_branch),
        OVER_Z[3],
    )

    def branch():
        v.branch, v.branch_upper = order(
            lambda h, w: project_halves(h, w, False, "branch"), hidden, w_down
        )
        v.BC = swap_head(v.branch_upper, 1)

    def bradd():
        v.branch = order(add, v.branch, v.BC)
        v.BY = swap_head(v.branch[own_rows:], 2)

    def res():
        v.result = order(
            lambda m, b, r: (m[:own_rows] + b[:own_rows].astype(F32) + r.astype(F32)).astype(BF16),
            middle,
            v.branch,
            v.BY,
        )

    def gpair():
        v.pair = order(
            lambda a, r: a + jnp.concatenate(blocks(r, 2)[::-1], axis=0), v.lower, v.Y
        )
        v.G = [swap_head(piece, 1) for piece in blocks(v.pair, 2)]

    def mback():
        out = order(
            lambda *a: middle_back(a[:3], a[3], a[4:6], ffn_gain, ffn_bias, a[6]),
            v.pair,
            *v.G,
            middle,
            cotangent_pair,
            cotangent_rest,
            w_out,
        )
        v.grad_branch, v.grad_middle, v.grad_attended = out[:3]
        v.ffn_sums = out[3:]

    def attb():
        v.latent_back, v.kv_back = order(
            lambda *a: attention_backward(*a[:4], a[4:10], *a[10:]),
            slot,
            low,
            high,
            valid_float * weighted_scale,
            kv_own,
            kv_near,
            *[kv for kv, _ in far],
            latent_qkv,
            v.grad_attended,
            lse,
            entropy,
        )

    def swap_pieces(value):
        return [swap_head(piece, 1) for piece in blocks(value, 2)]

    def pb():
        v.K1 = swap_pieces(order(lambda a, w: project_slot(a, 3, w), v.kv_back, w_kv))

    def pa():
        v.MF = swap_head(
            order(lambda a, w, *r: project_slot(a, 2, w, r), v.kv_back, w_kv, *v.K1), 2
        )

    def pn():
        v.K2 = swap_pieces(order(lambda a, w: project_slot(a, 1, w), v.kv_back, w_kv))

    def po():
        v.media_near = order(
            lambda a, w, *r: project_slot(a, 0, w, r), v.kv_back, w_kv, *v.K2
        )

    def lb():
        v.latent_lower, upper = order(
            lambda a, w: project_halves(a, w, True, "latent_back"), v.latent_back, w_qkv
        )
        v.LC = swap_head(upper, 1)

    def ladd():
        v.latent_lower = order(add, v.latent_lower, v.LC)
        v.LY = swap_head(v.latent_lower[own_rows:], 2)

    def nbm():
        v.media_grad, *v.media_sums = order(
            lambda *a: norm_back(*a, media_gain, media_bias), v.media_near, v.MF, media
        )

    def nbl():
        v.latents_grad, *v.latent_sums = order(
            lambda *a: norm_back(*a[:3], latent_gain, latent_bias, a[3]),
            v.latent_lower,
            v.LY,
            latents,
            v.grad_middle,
        )

    def s0():
        entropy_local = jnp.sum(entropy.reshape(images, -1) * valid_float[:, None])
        part_of = 1.0 / lax.axis_size("head")
        v.sums = order(
            stack,
            *v.media_sums,
            *v.latent_sums,
            *[value * part_of for value in v.ffn_sums],
            jnp.broadcast_to(entropy_local, (2, dim)),
        )
        v.moved = swap_head(v.sums, 1)

    def add_moved():
        v.sums = order(add, v.sums, v.moved)

    def s1():
        add_moved()
        v.moved = swap_head(v.sums, 2)

    def s2():
        add_moved()
        v.moved = swap_seq(v.sums, 1)

    def s3():
        add_moved()
        v.moved = swap_seq(v.sums, 2)

    def s4():
        add_moved()
        v.moved = swap_seq(v.sums, 4)

    s5 = add_moved

    def d_5():
        parts = down_parts()
        v.down = order(lambda p, *a: join_rows(p, a, ((0, dim),))[0], place, *parts)

    def u_5():
        parts = up_parts()
        v.up = order(lambda p, *a: join_rows(p, a, ((0, dim),))[0], place, *parts)

    def k_5():
        parts = key_parts()
        v.key, v.value = order(
            lambda p, *a: join_rows(p, a, ((0, width), (width, 2 * width))), place, *parts
        )

    def l_5():
        v.query, v.out = order(lambda p, *a: join_late(p, a), place, *late_parts())

    steps = (
        d, lowadd, u, gpair, mback, d_1, attb, d_2, lb, pb, l, u_1, k, d_3, l_1, ladd, u_2,
        pa, nbl, k_1, branch, d_4, pn, u_3, d_5, l_2, k_2, bradd, po, u_4, nbm, s0, l_3, s1,
        s2, k_3, u_5, l_4, s3, k_4, k_5, s4, res, s5, l_5,
    )
    for step in steps:
        step()
    sums = v.sums
    return (
        v.result,
        sums[6, 0] * pen_scale,
        v.media_grad,
        v.latents_grad,
        v.query,
        v.key,
        v.value,
        v.out,
        v.up,
        v.down,
        sums[0],
        sums[1],
        sums[2],
        sums[3],
        sums[4],
        sums[5],
    )


def shards_any(
    media,
    media_ids,
    image_seq,
    image_valid,
    latents,
    w_query,
    w_key,
    w_value,
    w_out,
    w_up,
    w_down,
    media_gain,
    media_bias,
    latent_gain,
    latent_bias,
    ffn_gain,
    ffn_bias,
    cotangent,
):
    seq_index = lax.axis_index("seq")
    head_index = lax.axis_index("head")
    images = image_seq.shape[0]
    sequences = media_ids.shape[0] // LEN
    own_rows = latents.shape[0]
    inner_width = w_query.shape[1]
    seq_size = lax.axis_size("seq")
    valid_float = image_valid.astype(F32)

    media_norm, media_hat, media_inv = normalize(media.astype(F32), media_gain, media_bias)
    latent_rows = lax.all_gather(latents, "head", axis=0, tiled=True)
    media_all = lax.all_gather(media_norm.astype(BF16), "head", axis=0, tiled=True)
    grad_all = lax.all_gather(cotangent, "head", axis=0, tiled=True)
    latent_float = latent_rows.astype(F32)
    latent_norm, latent_hat, latent_inv = normalize(latent_float, latent_gain, latent_bias)
    latent_low = latent_norm.astype(BF16)

    count_all = jnp.sum(valid_float).reshape(1, 1)
    count_all = sum_seq(jnp.broadcast_to(count_all, (8, 128)))[0, 0]
    pen_scale = 1.0 / (HEADS * LATENTS * count_all)
    weighted_scale = 4.0 * images * seq_size / count_all

    owners = seq_index * images + jnp.arange(images, dtype=jnp.int32)
    local_seq = image_seq - seq_index * sequences
    matches = media_ids[None, :] == owners[:, None]
    place = jnp.arange(media_ids.shape[0], dtype=jnp.int32)[None, :]
    run = jnp.sum(matches.astype(jnp.int32), axis=1)
    start = jnp.min(jnp.where(matches, place, media_ids.shape[0]), axis=1)
    low = jnp.where(run > 0, start - local_seq * LEN, 0)
    high = low + run
    slot = local_seq

    w_kv = jnp.concatenate([w_key, w_value], axis=1)
    w_qkv = jnp.concatenate([w_query, w_kv], axis=1)
    latent_qkv = product(latent_low, w_qkv).astype(BF16)
    kv_slots = [product(media_all, w_kv).astype(BF16)]
    attended, lse, entropy = attention_forward(slot, low, high, kv_slots, latent_qkv)

    branch = lax.psum(product(attended, w_out).astype(BF16), "head").astype(F32)
    middle = latent_float + branch
    ffn_norm, ffn_hat, ffn_inv = normalize(middle, ffn_gain, ffn_bias)
    ffn_low = ffn_norm.astype(BF16)
    before_gelu = product(ffn_low, w_up)
    activated, gelu_slope = gelu_parts(before_gelu)
    hidden = activated.astype(BF16)
    grad_before = (contract_cols(grad_all, w_down) * gelu_slope).astype(BF16)
    grad_ffn_part = contract_cols(grad_before, w_up).astype(BF16)
    grad_ffn = lax.psum(grad_ffn_part, "head").astype(F32)
    down_grad = contract_rows(hidden, grad_all).astype(BF16)
    up_grad = contract_rows(ffn_low, grad_before).astype(BF16)
    up_grad, down_grad = lax.psum((up_grad, down_grad), "seq")

    ffn_branch = product(hidden, w_down).astype(BF16)
    ffn_branch = lax.psum_scatter(ffn_branch, "head", scatter_dimension=0, tiled=True)

    def own(value):
        return lax.dynamic_slice_in_dim(value, head_index * own_rows, own_rows, axis=0)

    result = (own(middle) + ffn_branch.astype(F32)).astype(BF16)

    middle_part, ffn_gain_part, ffn_bias_part = normalize_back(
        grad_ffn, ffn_hat, ffn_inv, ffn_gain
    )
    grad_middle = grad_all.astype(F32) + middle_part
    grad_branch = grad_middle.astype(BF16)
    grad_attended = contract_cols(grad_branch, w_out).astype(BF16)
    out_grad = contract_rows(attended, grad_branch)
    back = attention_backward(
        slot,
        low,
        high,
        valid_float * weighted_scale,
        kv_slots,
        latent_qkv,
        grad_attended,
        lse,
        entropy,
    )
    latent_back, kv_back = back
    grad_media_norm = lax.psum_scatter(
        contract_cols(kv_back, w_kv).astype(BF16), "head", scatter_dimension=0, tiled=True
    ).astype(F32)
    grad_latent_part = contract_cols(latent_back, w_qkv).astype(BF16)
    grad_latent_norm = lax.psum_scatter(
        grad_latent_part, "head", scatter_dimension=0, tiled=True
    ).astype(F32)
    latent_grads = contract_rows(latent_low, latent_back)
    kv_grads = latent_grads[:, inner_width:] + contract_rows(media_all, kv_back)
    late = (
        latent_grads[:, :inner_width].astype(BF16),
        kv_grads.astype(BF16),
        out_grad.astype(BF16),
    )
    up_grad, down_grad, *late = lax.optimization_barrier((up_grad, down_grad) + late)
    query_grad, kv_grads, out_grad = lax.psum(tuple(late), "seq")

    media_rows_grad, media_gain_part, media_bias_part = normalize_back(
        grad_media_norm, media_hat, media_inv, media_gain
    )
    latent_part, latent_gain_part, latent_bias_part = normalize_back(
        grad_latent_norm, own(latent_hat), own(latent_inv), latent_gain
    )
    latents_grad = (own(grad_middle) + latent_part).astype(BF16)
    entropy_local = jnp.sum(entropy.reshape(images, -1) * valid_float[:, None])
    share = 1.0 / lax.axis_size("head")
    sums = jnp.stack(
        [
            media_gain_part,
            media_bias_part,
            latent_gain_part,
            latent_bias_part,
            ffn_gain_part * share,
            ffn_bias_part * share,
            jnp.broadcast_to(entropy_local, media_gain.shape),
            jnp.zeros_like(media_gain),
        ]
    )
    sums = sum_seq(sum_head(sums))
    return (
        result,
        sums[6, 0] * pen_scale,
        media_rows_grad.astype(BF16),
        latents_grad,
        query_grad.astype(F32),
        kv_grads[:, :inner_width].astype(F32),
        kv_grads[:, inner_width:].astype(F32),
        out_grad.astype(F32),
        up_grad.astype(F32),
        down_grad.astype(F32),
        sums[0],
        sums[1],
        sums[2],
        sums[3],
        sums[4],
        sums[5],
    )


def solution(mesh):
    rows = P(("seq", "head"), None)
    columns = P(None, "head")
    lines = P("head", None)
    quad = mesh.shape["head"] == 4 and mesh.shape["seq"] == 8
    return jax.shard_map(
        shards_quad if quad else shards_any,
        mesh=mesh,
        in_specs=(
            (rows, P("seq"), P("seq"), P("seq"), rows)
            + (columns, columns, columns, lines, columns, lines)
            + (P(),) * 6
            + (rows,)
        ),
        out_specs=(
            (rows, P(), rows, rows)
            + (columns, columns, columns, lines, columns, lines)
            + (P(),) * 6
        ),
        check_vma=False,
    )
```

```python
import jax
import jax.numpy as jnp
from jax import lax
from jax.experimental import pallas as pl
from jax.experimental.pallas import tpu as pltpu
from jax.sharding import PartitionSpec as P

HEADS = 16
HEAD_DIM = 96
LATENTS = 64
LEN = 1024
KEY_BLOCK = 256

epsilon = 1e-05
BF16 = jnp.bfloat16


def cost(microseconds):
    return pl.CostEstimate(
        flops=int(microseconds * 1.1e9), transcendentals=0, bytes_accessed=int(microseconds * 3e6)
    )


F32 = jnp.float32


def normalize(row_values, norm_gain, norm_bias):
    row_mean = jnp.mean(row_values, axis=-1, keepdims=True)
    centred = row_values - row_mean
    variance = jnp.mean(centred * centred, axis=-1, keepdims=True)
    inverse = lax.rsqrt(variance + epsilon)
    scaled = centred * inverse
    return (scaled * norm_gain + norm_bias, scaled, inverse)


def normalize_back(incoming, scaled, inverse, norm_gain):
    weighted = incoming * norm_gain
    first_mean = jnp.mean(weighted, axis=-1, keepdims=True)
    second_mean = jnp.mean(weighted * scaled, axis=-1, keepdims=True)
    outgoing = inverse * (weighted - first_mean - scaled * second_mean)
    return (outgoing, jnp.sum(incoming * scaled, axis=0), jnp.sum(incoming, axis=0))


def product(left_side, right_side):
    return jnp.dot(left_side, right_side, preferred_element_type=F32)


def contract_rows(left_side, right_side):
    return lax.dot_general(
        left_side, right_side, (((0,), (0,)), ((), ())), preferred_element_type=F32
    )


def contract_cols(left_side, right_side):
    return lax.dot_general(
        left_side, right_side, (((1,), (1,)), ((), ())), preferred_element_type=F32
    )


def gelu_parts(inputs):
    normal_cdf = 0.5 * (1.0 + lax.erf(inputs * 0.7071067811865476))
    density = jnp.exp(-0.5 * inputs * inputs) * 0.3989422804014327
    return (inputs * normal_cdf, normal_cdf + inputs * density)


def block_diagonal(rows, heads):
    lane = lax.broadcasted_iota(jnp.int32, rows.shape, 1)
    parts = []
    for head in range(heads):
        inside = (lane >= head * HEAD_DIM) & (lane < (head + 1) * HEAD_DIM)
        parts.append(jnp.where(inside, rows, jnp.zeros_like(rows)))
    return jnp.concatenate(parts, axis=0)


def take_diagonal(wide, heads):
    lane = lax.broadcasted_iota(jnp.int32, (LATENTS, wide.shape[1]), 1)
    out = wide[:LATENTS]
    for head in range(1, heads):
        out = jnp.where(lane >= head * HEAD_DIM, wide[head * LATENTS : (head + 1) * LATENTS], out)
    return out


def start_loads(kv_hbm, kv_vmem, sems):
    copies = []
    at = 0
    for i, ref in enumerate(kv_hbm):
        size = ref.shape[0]
        copies.append(pltpu.make_async_copy(ref, kv_vmem.at[pl.ds(at, size), :], sems.at[i]))
        at += size
    for copy in copies:
        copy.start()
    return copies


WINDOWS = (256, 512)


def image_rows(image):
    return pl.ds(pl.multiple_of(image * LATENTS, LATENTS), LATENTS)


def window_start(lo, size):
    return jnp.minimum(lo // 16 * 16, LEN - size)


def list_images(here, low, high):
    images = here.shape[0]
    kind = len(WINDOWS) - sum(
        (high - window_start(low, size) <= size).astype(jnp.int32) for size in WINDOWS
    )
    kind = jnp.where(here, kind, len(WINDOWS) + 1)
    number = jnp.arange(images, dtype=jnp.int32)
    key = kind * images + number
    rank = jnp.sum((key[None, :] < key[:, None]).astype(jnp.int32), axis=1)
    listed = jnp.sum(jnp.where(rank[None, :] == number[:, None], number[None, :], 0), axis=1)
    ends = [jnp.sum((kind <= i).astype(jnp.int32)).reshape(1) for i in range(len(WINDOWS) + 1)]
    return jnp.concatenate([listed, *ends])


def each_image(listed_ref, images, short, long):
    begin = 0
    for i, size in enumerate(WINDOWS):
        end = listed_ref[images + i]

        def pair(index, _, size=size, begin=begin, end=end):
            at = begin + 2 * index
            short(size, [listed_ref[at], listed_ref[jnp.minimum(at + 1, end - 1)]])
            return 0

        lax.fori_loop(0, (end - begin + 1) // 2, pair, 0)
        begin = end

    def single(index, _):
        long(listed_ref[index])
        return 0

    lax.fori_loop(begin, listed_ref[images + len(WINDOWS)], single, 0)


def attention_forward(
    listed, slot, low, high, kv_slots, latent_qkv, offset=0, before=None, time=15.0
):
    images = slot.shape[0]
    count = len(kv_slots)
    keys = sum(kv.shape[0] for kv in kv_slots)
    width = latent_qkv.shape[1] // 3
    heads = width // HEAD_DIM
    rows = heads * LATENTS
    scale = HEAD_DIM ** (-0.5)
    given = () if before is None else tuple(before)
    whole_rows = latent_qkv.shape[0] == images * LATENTS

    def source_rows(image):
        return image_rows(image if whole_rows else image // 8 * 4 + image % 4)


    def body(listed_ref, slot_ref, low_ref, high_ref, *refs):
        kv_hbm = refs[:count]
        qkv_ref = refs[count]
        given_refs = refs[count + 1 : count + 1 + len(given)]
        out_ref, lse_ref, ent_ref, kv_vmem, scores, sems = refs[count + 1 + len(given) :]
        copies = start_loads(kv_hbm, kv_vmem, sems)
        if given:
            out_ref[...] = given_refs[0][...]
            lse_ref[...] = given_refs[1][...]
            ent_ref[...] = given_refs[2][...]
        for copy in copies:
            copy.wait()

        def short(size, pair):
            for image in pair:
                at = source_rows(image)
                lo = low_ref[image]
                hi = high_ref[image]
                start = window_start(lo, size)
                place = pl.multiple_of((slot_ref[image] - offset) * LEN + start, 16)
                query = block_diagonal(qkv_ref[at, :width], heads)
                own = contract_cols(qkv_ref[at, width : 2 * width], query) * scale
                part = contract_cols(kv_vmem[pl.ds(place, size), :width], query) * scale
                key = start + lax.broadcasted_iota(jnp.int32, part.shape, 0)
                part = jnp.where((key >= lo) & (key < hi), part, -1e30)
                peak = jnp.maximum(
                    jnp.max(own, axis=0, keepdims=True), jnp.max(part, axis=0, keepdims=True)
                )
                own = own - peak
                part = part - peak
                own_exp = jnp.exp(own)
                part_exp = jnp.exp(part)
                total = jnp.sum(own_exp, axis=0, keepdims=True) + jnp.sum(
                    part_exp, axis=0, keepdims=True
                )
                moment = jnp.sum(own_exp * own, axis=0, keepdims=True) + jnp.sum(
                    part_exp * part, axis=0, keepdims=True
                )
                inverse = 1.0 / total
                log_total = jnp.log(total)
                lse_ref[image] = peak + log_total
                ent_ref[image] = log_total - moment * inverse
                wide = contract_rows((own_exp * inverse).astype(BF16), qkv_ref[at, 2 * width :])
                wide = wide + contract_rows(
                    (part_exp * inverse).astype(BF16), kv_vmem[pl.ds(place, size), width:]
                )
                out_ref[image_rows(image), :] = take_diagonal(wide, heads).astype(BF16)

        def long(image):
            at = source_rows(image)
            base = (slot_ref[image] - offset) * LEN
            lo = low_ref[image]
            hi = high_ref[image]
            first = lo // KEY_BLOCK
            last = (hi + KEY_BLOCK - 1) // KEY_BLOCK
            query = block_diagonal(qkv_ref[at, :width], heads)
            own = contract_cols(qkv_ref[at, width : 2 * width], query) * scale
            peak = jnp.max(own, axis=0, keepdims=True)

            def first_pass(block, peak):
                row = pl.multiple_of(base + block * KEY_BLOCK, KEY_BLOCK)
                part = contract_cols(kv_vmem[pl.ds(row, KEY_BLOCK), :width], query) * scale
                key = block * KEY_BLOCK + lax.broadcasted_iota(jnp.int32, part.shape, 0)
                part = jnp.where((key >= lo) & (key < hi), part, -1e30)
                to = pl.multiple_of((block - first) * KEY_BLOCK, KEY_BLOCK)
                scores[pl.ds(to, KEY_BLOCK), :] = part
                return jnp.maximum(peak, jnp.max(part, axis=0, keepdims=True))

            peak = lax.fori_loop(first, last, first_pass, peak)
            own = own - peak
            own_exp = jnp.exp(own)
            total = jnp.sum(own_exp, axis=0, keepdims=True)
            moment = jnp.sum(own_exp * own, axis=0, keepdims=True)

            def second_pass(block, carry):
                total, moment = carry
                to = pl.multiple_of((block - first) * KEY_BLOCK, KEY_BLOCK)
                part = scores[pl.ds(to, KEY_BLOCK), :] - peak
                part_exp = jnp.exp(part)
                scores[pl.ds(to, KEY_BLOCK), :] = part_exp
                return (
                    total + jnp.sum(part_exp, axis=0, keepdims=True),
                    moment + jnp.sum(part_exp * part, axis=0, keepdims=True),
                )

            total, moment = lax.fori_loop(first, last, second_pass, (total, moment))
            inverse = 1.0 / total
            log_total = jnp.log(total)
            lse_ref[image] = peak + log_total
            ent_ref[image] = log_total - moment * inverse
            wide = contract_rows((own_exp * inverse).astype(BF16), qkv_ref[at, 2 * width :])

            def third_pass(block, wide):
                to = pl.multiple_of((block - first) * KEY_BLOCK, KEY_BLOCK)
                row = pl.multiple_of(base + block * KEY_BLOCK, KEY_BLOCK)
                low_prob = (scores[pl.ds(to, KEY_BLOCK), :] * inverse).astype(BF16)
                return wide + contract_rows(low_prob, kv_vmem[pl.ds(row, KEY_BLOCK), width:])

            wide = lax.fori_loop(first, last, third_pass, wide)
            out_ref[image_rows(image), :] = take_diagonal(wide, heads).astype(BF16)

        each_image(listed_ref, images, short, long)

    shapes = (
        jax.ShapeDtypeStruct((images * LATENTS, width), BF16),
        jax.ShapeDtypeStruct((images, 1, rows), F32),
        jax.ShapeDtypeStruct((images, 1, rows), F32),
    )
    scalar = pl.BlockSpec(memory_space=pltpu.SMEM)
    vmem = pl.BlockSpec(memory_space=pltpu.VMEM)
    return pl.pallas_call(
        body,
        out_shape=shapes,
        in_specs=[scalar] * 4
        + [pl.BlockSpec(memory_space=pl.ANY)] * count
        + [vmem] * (1 + len(given)),
        out_specs=(vmem,) * 3,
        scratch_shapes=[
            pltpu.VMEM((keys, 2 * width), BF16),
            pltpu.VMEM((LEN, rows), F32),
            pltpu.SemaphoreType.DMA((count,)),
        ],
        compiler_params=pltpu.CompilerParams(vmem_limit_bytes=48 << 20),
        cost_estimate=cost(time),
        name="attention_forward",
    )(listed, slot, low, high, *kv_slots, latent_qkv, *given)


def attention_backward(
    listed, slot, low, high, weight, kv_slots, latent_qkv, grad_out, lse, entropy
):
    images = slot.shape[0]
    count = len(kv_slots)
    keys = sum(kv.shape[0] for kv in kv_slots)
    width = latent_qkv.shape[1] // 3
    heads = width // HEAD_DIM
    rows = heads * LATENTS
    scale = HEAD_DIM ** (-0.5)

    def body(listed_ref, slot_ref, low_ref, high_ref, weight_ref, *refs):
        kv_hbm = refs[:count]
        qkv_ref, grad_ref, lse_ref, ent_ref = refs[count : count + 4]
        own_out, key_out, kv_vmem, probs, slopes, totals, sems = refs[count + 4 :]
        copies = start_loads(kv_hbm, kv_vmem, sems)
        totals[...] = jnp.zeros_like(totals)
        for copy in copies:
            copy.wait()

        def short(size, pair):
            for which, image in enumerate(pair):
                repeated = jnp.logical_and(which == 1, pair[0] == image)
                at = image_rows(image)
                lo = low_ref[image]
                hi = high_ref[image]
                pull = weight_ref[image]
                start = window_start(lo, size)
                place = pl.multiple_of(slot_ref[image] * LEN + start, 16)
                window = pl.ds(place, size)
                query = block_diagonal(qkv_ref[at, :width], heads)
                grad = block_diagonal(grad_ref[at, :], heads)
                log_total = lse_ref[image]
                ent = ent_ref[image]
                own_key = qkv_ref[at, width : 2 * width]
                own_log = contract_cols(own_key, query) * scale - log_total
                own_prob = jnp.exp(own_log)
                own_slope = contract_cols(qkv_ref[at, 2 * width :], grad)
                part = contract_cols(kv_vmem[window, :width], query) * scale
                key = start + lax.broadcasted_iota(jnp.int32, part.shape, 0)
                part = jnp.where((key >= lo) & (key < hi), part - log_total, -1e30)
                prob = jnp.exp(part)
                slope = contract_cols(kv_vmem[window, width:], grad)
                centre = jnp.sum(own_prob * own_slope, axis=0, keepdims=True)
                centre = centre + jnp.sum(prob * slope, axis=0, keepdims=True)
                own_low = own_prob * (own_slope - pull * (own_log + ent) - centre)
                own_low = own_low.astype(BF16)
                low_grad = (prob * (slope - pull * (part + ent) - centre)).astype(BF16)
                grad_query = contract_rows(own_low, own_key)
                grad_query = grad_query + contract_rows(low_grad, kv_vmem[window, :width])
                own_out[at, width : 2 * width] = (product(own_low, query) * scale).astype(BF16)
                own_out[at, 2 * width :] = product(own_prob.astype(BF16), grad).astype(BF16)
                once = jnp.where(repeated, 0.0, 1.0)
                totals[window, :width] += product(low_grad, query) * (scale * once)
                totals[window, width:] += product(prob.astype(BF16), grad) * once
                own_out[at, :width] = (take_diagonal(grad_query, heads) * scale).astype(BF16)

        def long(image):
            at = image_rows(image)
            base = slot_ref[image] * LEN
            lo = low_ref[image]
            hi = high_ref[image]
            pull = weight_ref[image]
            first = lo // KEY_BLOCK
            last = (hi + KEY_BLOCK - 1) // KEY_BLOCK
            query = block_diagonal(qkv_ref[at, :width], heads)
            grad = block_diagonal(grad_ref[at, :], heads)
            log_total = lse_ref[image]
            ent = ent_ref[image]
            own_key = qkv_ref[at, width : 2 * width]
            own_log = contract_cols(own_key, query) * scale - log_total
            own_prob = jnp.exp(own_log)
            own_slope = contract_cols(qkv_ref[at, 2 * width :], grad)
            centre = jnp.sum(own_prob * own_slope, axis=0, keepdims=True)
            own_slope = own_slope - pull * (own_log + ent)

            def first_pass(block, centre):
                row = pl.multiple_of(base + block * KEY_BLOCK, KEY_BLOCK)
                to = pl.multiple_of((block - first) * KEY_BLOCK, KEY_BLOCK)
                part = contract_cols(kv_vmem[pl.ds(row, KEY_BLOCK), :width], query) * scale
                key = block * KEY_BLOCK + lax.broadcasted_iota(jnp.int32, part.shape, 0)
                part = jnp.where((key >= lo) & (key < hi), part - log_total, -1e30)
                prob = jnp.exp(part)
                slope = contract_cols(kv_vmem[pl.ds(row, KEY_BLOCK), width:], grad)
                probs[pl.ds(to, KEY_BLOCK), :] = prob
                slopes[pl.ds(to, KEY_BLOCK), :] = slope - pull * (part + ent)
                return centre + jnp.sum(prob * slope, axis=0, keepdims=True)

            centre = lax.fori_loop(first, last, first_pass, centre)
            own_low = (own_prob * (own_slope - centre)).astype(BF16)
            grad_query = contract_rows(own_low, own_key)
            own_out[at, width : 2 * width] = (product(own_low, query) * scale).astype(BF16)
            own_out[at, 2 * width :] = product(own_prob.astype(BF16), grad).astype(BF16)

            def second_pass(block, grad_query):
                row = pl.multiple_of(base + block * KEY_BLOCK, KEY_BLOCK)
                to = pl.multiple_of((block - first) * KEY_BLOCK, KEY_BLOCK)
                prob = probs[pl.ds(to, KEY_BLOCK), :]
                low_grad = (prob * (slopes[pl.ds(to, KEY_BLOCK), :] - centre)).astype(BF16)
                totals[pl.ds(row, KEY_BLOCK), :width] += product(low_grad, query) * scale
                totals[pl.ds(row, KEY_BLOCK), width:] += product(prob.astype(BF16), grad)
                return grad_query + contract_rows(
                    low_grad, kv_vmem[pl.ds(row, KEY_BLOCK), :width]
                )

            grad_query = lax.fori_loop(first, last, second_pass, grad_query)
            own_out[at, :width] = (take_diagonal(grad_query, heads) * scale).astype(BF16)

        each_image(listed_ref, images, short, long)
        key_out[...] = totals[...].astype(BF16)

    scalar = pl.BlockSpec(memory_space=pltpu.SMEM)
    vmem = pl.BlockSpec(memory_space=pltpu.VMEM)
    return pl.pallas_call(
        body,
        out_shape=(
            jax.ShapeDtypeStruct((images * LATENTS, 3 * width), BF16),
            jax.ShapeDtypeStruct((keys, 2 * width), BF16),
        ),
        in_specs=[scalar] * 5 + [pl.BlockSpec(memory_space=pl.ANY)] * count + [vmem] * 4,
        out_specs=(vmem, vmem),
        scratch_shapes=[
            pltpu.VMEM((keys, 2 * width), BF16),
            pltpu.VMEM((LEN, rows), F32),
            pltpu.VMEM((LEN, rows), F32),
            pltpu.VMEM((keys, 2 * width), F32),
            pltpu.SemaphoreType.DMA((count,)),
        ],
        compiler_params=pltpu.CompilerParams(vmem_limit_bytes=56 << 20),
        cost_estimate=cost(0.5),
        name="attention_backward",
    )(listed, slot, low, high, weight, *kv_slots, latent_qkv, grad_out, lse, entropy)


ROW_BLOCK = 256


def call(body, grid, inputs, outputs, name, time=5.0, scratch=()):
    return pl.pallas_call(
        body,
        out_shape=tuple(jax.ShapeDtypeStruct(shape, dtype) for shape, dtype, _ in outputs),
        grid=(grid,),
        in_specs=[spec for _, spec in inputs],
        out_specs=tuple(spec for _, _, spec in outputs),
        scratch_shapes=list(scratch),
        compiler_params=pltpu.CompilerParams(
            dimension_semantics=("arbitrary",), vmem_limit_bytes=56 << 20
        ),
        cost_estimate=cost(time),
        name=name,
    )(*[value for value, _ in inputs])


def by_rows(width, move=lambda i: i, size=ROW_BLOCK):
    return pl.BlockSpec((size, width), lambda i: (move(i), 0))


def whole(value):
    return pl.BlockSpec(value.shape, lambda i: (0,) * value.ndim, pipeline_mode=pl.Buffered(1))


def stacked(values):
    steps = values[0].shape[0] // ROW_BLOCK
    return [
        (value, by_rows(value.shape[1], lambda i, k=k: jnp.clip(i - k * steps, 0, steps - 1)))
        for k, value in enumerate(values)
    ]


def stacked_rows(refs, values):
    steps = values[0].shape[0] // ROW_BLOCK
    rows = refs[0][...]
    for k in range(1, len(values)):
        rows = jnp.where(pl.program_id(0) >= k * steps, refs[k][...], rows)
    return rows


def low_half(i):
    return jnp.minimum(i, 1)


def high_half(i):
    return jnp.maximum(i - 2, 0)


def pair_inputs(pair, rest):
    return [(pair, by_rows(pair.shape[1], low_half)), (rest, by_rows(rest.shape[1], high_half))]


def pick(pair_ref, rest_ref):
    return jnp.where(pl.program_id(0) < 2, pair_ref[...], rest_ref[...])


def put_halves(low_ref, high_ref, value):
    @pl.when(pl.program_id(0) < 2)
    def _():
        low_ref[...] = value

    @pl.when(pl.program_id(0) >= 2)
    def _():
        high_ref[...] = value


def half_outputs(width):
    return [
        ((2 * ROW_BLOCK, width), BF16, by_rows(width, low_half)),
        ((2 * ROW_BLOCK, width), BF16, by_rows(width, high_half)),
    ]


def add_up(ref, value):
    total = jnp.sum(value, axis=0, keepdims=True)

    @pl.when(pl.program_id(0) == 0)
    def _():
        ref[...] = total

    @pl.when(pl.program_id(0) > 0)
    def _():
        ref[...] += total


def sum_output(width):
    return ((1, width), F32, pl.BlockSpec((1, width), lambda i: (0, 0)))


def norm_project(rows, gain, bias, weights, time=7.5, count=None):
    width, wide = rows[0].shape[1], weights.shape[1]
    count = count or sum(part.shape[0] for part in rows)

    def body(*refs):
        value = stacked_rows(refs, rows)
        gain_ref, bias_ref, weight_ref, out_ref, norm_ref = refs[len(rows) :]
        norm = normalize(value.astype(F32), gain_ref[...], bias_ref[...])[0].astype(BF16)
        norm_ref[...] = norm
        out_ref[...] = product(norm, weight_ref[...]).astype(BF16)

    return call(
        body,
        count // ROW_BLOCK,
        stacked(rows) + [(gain, whole(gain)), (bias, whole(bias)), (weights, whole(weights))],
        [((count, wide), BF16, by_rows(wide)), ((count, width), BF16, by_rows(width))],
        "norm_project",
        time,
    )


def cotangent_down(rows, weights):
    wide = weights.shape[0]

    def body(*refs):
        refs[-1][...] = contract_cols(stacked_rows(refs, rows), refs[-2][...])

    return call(
        body,
        4,
        stacked(rows) + [(weights, whole(weights))],
        [((4 * ROW_BLOCK, wide), F32, by_rows(wide))],
        "cotangent_down",
        10.0,
    )[0]


def feed_forward(attended, near_weights, far_weights, latent_rows, pulled, w_up, gain, bias):
    width = attended[0].shape[1]
    dim = w_up.shape[0]
    wide = w_up.shape[1]

    def body(*refs):
        own, near, across, beyond, first_ref, far_ref, far_rest, *lat_refs = refs[:11]
        pulled_ref, up_ref, gain_ref, bias_ref, middle_ref, ffn_ref, hidden_ref, grad_ref = refs[
            11:19
        ]
        low_ref, high_ref, second_ref = refs[19:]

        @pl.when(pl.program_id(0) == 0)
        def _():
            second_ref[:width, :] = far_ref[...]
            second_ref[width:, :] = far_rest[...]

        rows = stacked_rows(lat_refs, latent_rows).astype(F32)
        rows = rows + product(jnp.concatenate([own[...], near[...]], axis=1), first_ref[...])
        rows = rows + product(jnp.concatenate([across[...], beyond[...]], axis=1), second_ref[...])
        middle_ref[...] = rows
        norm = normalize(rows, gain_ref[...], bias_ref[...])[0].astype(BF16)
        ffn_ref[...] = norm
        step = wide // 3
        for i in range(3):
            at = slice(i * step, (i + 1) * step)
            activated, slope = gelu_parts(product(norm, up_ref[:, at]))
            hidden_ref[:, at] = activated.astype(BF16)
            grad_ref[:, at] = (pulled_ref[:, at] * slope).astype(BF16)
        back = contract_cols(grad_ref[...], up_ref[...]).astype(BF16)
        put_halves(low_ref, high_ref, back)

    count = 4 * ROW_BLOCK
    return call(
        body,
        4,
        [
            (attended[0], by_rows(width)),
            (attended[1], by_rows(width, lambda i: i ^ 2)),
            (attended[2], by_rows(width, lambda i: i ^ 1)),
            (attended[3], by_rows(width, lambda i: i ^ 3)),
            (near_weights, whole(near_weights)),
            (far_weights[0], whole(far_weights[0])),
            (far_weights[1], whole(far_weights[1])),
        ]
        + stacked(latent_rows)
        + [
            (pulled, by_rows(wide)),
            (w_up, whole(w_up)),
            (gain, whole(gain)),
            (bias, whole(bias)),
        ],
        [
            ((count, dim), F32, by_rows(dim)),
            ((count, dim), BF16, by_rows(dim)),
            ((count, wide), BF16, by_rows(wide)),
            ((count, wide), BF16, by_rows(wide)),
        ]
        + half_outputs(dim),
        "feed_forward",
        27.0,
        scratch=[pltpu.VMEM((2 * width, dim), BF16)],
    )


def part(value, rows=None, at=0, columns=slice(None)):
    return (value, value.shape[0] if rows is None else rows, at, columns)


def grad_halves(side, pairs, name):
    half = pairs[0][0].shape[1] // 2
    inputs = []
    for left, rights in pairs:
        inputs.append(
            (
                left,
                pl.BlockSpec(
                    (left.shape[0], half),
                    lambda i, x: (0, (i + 1 + x[0]) % 2),
                ),
            )
        )
        for value, rows, at, _ in rights:
            spec = pl.BlockSpec(
                (rows, value.shape[1]), lambda i, x, at=at: (at, 0), pipeline_mode=pl.Buffered(1)
            )
            inputs.append((value, spec))
    value, _, _, columns = pairs[0][1][0]
    wide = len(range(*columns.indices(value.shape[1])))

    def body(x_ref, *refs):
        total = None
        index = 0
        for left, rights in pairs:
            left_ref = refs[index]
            row = 0
            for i, (_, rows, _, columns) in enumerate(rights):
                value = contract_rows(
                    left_ref[row : row + rows, :], refs[index + 1 + i][:, columns]
                )
                row += rows
                total = value if total is None else total + value
            index += 1 + len(rights)
        put_sides(refs[-2], refs[-1], total.astype(BF16))

    return side_call(body, side, inputs, half, wide, name)


def put_sides(other_ref, mine_ref, value):
    @pl.when(pl.program_id(0) == 0)
    def _():
        other_ref[...] = value

    @pl.when(pl.program_id(0) == 1)
    def _():
        mine_ref[...] = value


def side_call(body, side, inputs, half, wide, name):
    out = pl.BlockSpec((half, wide), lambda i, x: (0, 0))
    return pl.pallas_call(
        body,
        out_shape=(jax.ShapeDtypeStruct((half, wide), BF16),) * 2,
        grid_spec=pltpu.PrefetchScalarGridSpec(
            num_scalar_prefetch=1,
            grid=(2,),
            in_specs=[spec for _, spec in inputs],
            out_specs=(out, out),
        ),
        compiler_params=pltpu.CompilerParams(
            dimension_semantics=("arbitrary",), vmem_limit_bytes=56 << 20
        ),
        cost_estimate=cost(0.5),
        name=name,
    )(side, *[value for value, _ in inputs])


def late_grads(side, latent_back, early_low, late_low, attended, grad_branch):
    width = attended.shape[1]
    wide = grad_branch.shape[1]

    def body(x_ref, back_ref, early_ref, late_ref, attended_ref, branch_ref, other_ref, mine_ref):
        size = early_low.shape[0] // 2
        which = (pl.program_id(0) + 1 + x_ref[0]) % 2

        @pl.when(which == 0)
        def _():
            value = jnp.zeros((width, wide), F32)
            for i, low_ref in enumerate((early_ref, late_ref, early_ref, late_ref)):
                value = value + contract_rows(
                    back_ref[i * size : (i + 1) * size, :],
                    low_ref[i // 2 * size : (i // 2 + 1) * size, :],
                )
            put_sides(other_ref, mine_ref, value.astype(BF16))

        @pl.when(which == 1)
        def _():
            value = contract_rows(attended_ref[...], branch_ref[...]).astype(BF16)
            put_sides(other_ref, mine_ref, value)

    inputs = [
        (
            value,
            pl.BlockSpec(
                (value.shape[0], min(value.shape[1], size)),
                lambda i, x: (0, 0),
                pipeline_mode=pl.Buffered(1),
            ),
        )
        for value, size in (
            (latent_back, width),
            (early_low, wide),
            (late_low, wide),
            (attended, width),
            (grad_branch, wide),
        )
    ]
    return side_call(body, side, inputs, width, wide, "late_grads")


def join_rows(place, parts, splits):
    size = parts[0].shape[0]
    count = len(parts)

    def body(place_ref, *refs):
        step = pl.program_id(0)
        for i in range(count):

            @pl.when(step == i)
            def _():
                for (first, last), out_ref in zip(splits, refs[count:]):
                    out_ref[...] = refs[i][:, first:last].astype(F32)

    inputs = [
        pl.BlockSpec(value.shape, lambda i, p: (0, 0), pipeline_mode=pl.Buffered(1))
        for value in parts
    ]
    return pl.pallas_call(
        body,
        out_shape=tuple(
            jax.ShapeDtypeStruct((count * size, last - first), F32) for first, last in splits
        ),
        grid_spec=pltpu.PrefetchScalarGridSpec(
            num_scalar_prefetch=1,
            grid=(count,),
            in_specs=inputs,
            out_specs=tuple(
                pl.BlockSpec((size, last - first), lambda i, p: (i ^ p[0], 0))
                for first, last in splits
            ),
        ),
        compiler_params=pltpu.CompilerParams(
            dimension_semantics=("arbitrary",), vmem_limit_bytes=56 << 20
        ),
        cost_estimate=cost(0.5),
        name="join_rows",
    )(place, *parts)


def join_late(place, parts):
    size, dim = parts[0].shape

    def body(place_ref, own_ref, pair_ref, side_ref, last_ref, query_ref, out_ref):
        odd = place_ref[0] % 2 == 1
        first = place_ref[0] < 2

        def rows(low_ref, high_ref):
            low, high = low_ref[...], high_ref[...]
            return jnp.concatenate(
                [jnp.where(odd, high, low), jnp.where(odd, low, high)], axis=0
            ).astype(F32)

        mine, other = rows(own_ref, pair_ref), rows(side_ref, last_ref)
        query_ref[...] = jnp.where(first, mine, other).T
        out_ref[...] = jnp.where(first, other, mine)

    spec = pl.BlockSpec((size, 384), lambda i, p: (0, i))
    return pl.pallas_call(
        body,
        out_shape=(
            jax.ShapeDtypeStruct((dim, 2 * size), F32),
            jax.ShapeDtypeStruct((2 * size, dim), F32),
        ),
        grid_spec=pltpu.PrefetchScalarGridSpec(
            num_scalar_prefetch=1,
            grid=(dim // 384,),
            in_specs=[spec] * 4,
            out_specs=(
                pl.BlockSpec((384, 2 * size), lambda i, p: (i, 0)),
                pl.BlockSpec((2 * size, 384), lambda i, p: (0, i)),
            ),
        ),
        compiler_params=pltpu.CompilerParams(dimension_semantics=("arbitrary",)),
        cost_estimate=cost(0.5),
        name="join_late",
    )(place, *parts)


def project_halves(rows, weights, transposed, name):
    wide = weights.shape[0] if transposed else weights.shape[1]

    def body(rows_ref, weight_ref, low_ref, high_ref):
        if transposed:
            out = contract_cols(rows_ref[...], weight_ref[...])
        else:
            out = product(rows_ref[...], weight_ref[...])
        put_halves(low_ref, high_ref, out.astype(BF16))

    return call(
        body,
        4,
        [(rows, by_rows(rows.shape[1])), (weights, whole(weights))],
        half_outputs(wide),
        name,
        0.5,
    )


def project_slot(rows, slot, weights, added=()):
    wide = weights.shape[0]
    blocks_in = LEN // ROW_BLOCK

    def body(rows_ref, weight_ref, *refs):
        out = contract_cols(rows_ref[...], weight_ref[...])
        if added:
            out = out + stacked_rows(refs, added).astype(F32)
        refs[-1][...] = out.astype(BF16)

    return call(
        body,
        blocks_in,
        [
            (rows, by_rows(rows.shape[1], lambda i: i + slot * blocks_in)),
            (weights, whole(weights)),
        ]
        + (stacked(added) if added else []),
        [((LEN, wide), BF16, by_rows(wide))],
        "project_slot",
        0.5,
    )[0]


def middle_back(grads, middle, cotangents, gain, bias, w_out):
    dim = middle.shape[1]
    width = w_out.shape[0]

    def body(*refs):
        grad_ref, third_ref, fourth_ref, middle_ref, *cot_refs = refs[:8]
        gain_ref, bias_ref, out_ref, branch_ref, own_ref, attended_ref, gain_sum, bias_sum = refs[8:]
        step = pl.program_id(0)
        grad = jnp.where(step == 2, third_ref[...], fourth_ref[...])
        grad = jnp.where(step < 2, grad_ref[...], grad).astype(F32)
        _, hat, inv = normalize(middle_ref[...], gain_ref[...], bias_ref[...])
        weighted = grad * gain_ref[...]
        moved = grad * hat
        first_mean = jnp.mean(weighted, axis=-1, keepdims=True)
        second_mean = jnp.mean(weighted * hat, axis=-1, keepdims=True)
        value = stacked_rows(cot_refs, cotangents).astype(F32) + inv * (
            weighted - first_mean - hat * second_mean
        )
        low = value.astype(BF16)
        branch_ref[...] = low
        attended_ref[...] = contract_cols(low, out_ref[...]).astype(BF16)
        add_up(gain_sum, moved)
        add_up(bias_sum, grad)

        @pl.when(pl.program_id(0) == 0)
        def _():
            own_ref[...] = value

    count = 4 * ROW_BLOCK
    return call(
        body,
        4,
        [(grads[0], by_rows(dim, low_half))]
        + [(grad, whole(grad)) for grad in grads[1:]]
        + [(middle, by_rows(dim))]
        + stacked(cotangents)
        + [(gain, whole(gain)), (bias, whole(bias)), (w_out, whole(w_out))],
        [
            ((count, dim), BF16, by_rows(dim)),
            ((ROW_BLOCK, dim), F32, by_rows(dim, lambda i: 0)),
            ((count, width), BF16, by_rows(width)),
            sum_output(dim),
            sum_output(dim),
        ],
        "middle_back",
        0.5,
    )


def norm_back(near, far, rows, gain, bias, added=None):
    dim = rows.shape[1]
    extra = [] if added is None else [(added, by_rows(dim))]

    def body(*refs):
        near_ref, far_ref, rows_ref, gain_ref, bias_ref = refs[:5]
        out_ref, gain_sum, bias_sum = refs[-3:]
        grad = near_ref[...].astype(F32) + far_ref[...].astype(F32)
        _, hat, inv = normalize(rows_ref[...].astype(F32), gain_ref[...], bias_ref[...])
        weighted = grad * gain_ref[...]
        first_mean = jnp.mean(weighted, axis=-1, keepdims=True)
        second_mean = jnp.mean(weighted * hat, axis=-1, keepdims=True)
        value = inv * (weighted - first_mean - hat * second_mean)
        if extra:
            value = refs[5][...] + value
        out_ref[...] = value.astype(BF16)
        add_up(gain_sum, grad * hat)
        add_up(bias_sum, grad)

    return call(
        body,
        rows.shape[0] // ROW_BLOCK,
        [(near, by_rows(dim)), (far, by_rows(dim)), (rows, by_rows(dim))]
        + [(gain, whole(gain)), (bias, whole(bias))]
        + extra,
        [(rows.shape, BF16, by_rows(dim)), sum_output(dim), sum_output(dim)],
        "norm_back",
        0.5,
    )


def swap_head(value, bit):
    size = lax.axis_size("head")
    return lax.ppermute(value, "head", [(i, i ^ bit) for i in range(size)])


def swap_seq(value, bit):
    size = lax.axis_size("seq")
    return lax.ppermute(value, "seq", [(i, i ^ bit) for i in range(size)])


def sum_seq(value):
    size = lax.axis_size("seq")
    bit = 1
    while bit < size:
        value = value + swap_seq(value, bit)
        bit *= 2
    return value


def sum_head(value):
    size = lax.axis_size("head")
    bit = 1
    while bit < size:
        value = value + swap_head(value, bit)
        bit *= 2
    return value


OVER_Z = (False, False, True, False)


class Values:
    pass


class Order:
    def __init__(self):
        self.last = None

    def __call__(self, step, *values):
        if self.last is not None:
            *values, _ = lax.optimization_barrier((*values, self.last))
        out = step(*values)
        self.last = tuple(out) if isinstance(out, (tuple, list)) else out
        return out

    def gate(self, value):
        return lax.optimization_barrier((value, self.last))[0]

    def pin(self, value):
        self.last = self.gate(value)
        return self.last


class SeqSum:
    def __init__(self, order, halves, over_z):
        other, self.mine = halves
        self.order = order
        self.over_z = over_z
        self.moving = swap_seq(other, 1)

    def split(self):
        odd = lax.axis_index("seq") // 2 % 2
        quarter = self.mine.shape[0] // 2

        def run(mine, moving):
            total = mine + moving
            return [
                lax.dynamic_slice_in_dim(total, which * quarter, quarter, axis=0)
                for which in (1 - odd, odd)
            ]

        other, self.mine = self.order(run, self.mine, self.moving)
        self.moving = swap_seq(other, 2)

    def across(self):
        self.mine = self.order(lambda v, r: v + r, self.mine, self.moving)
        self.moving = swap_seq(self.mine, 4)

    def spread(self):
        self.mine = self.order(lambda v, r: v + r, self.mine, self.moving)
        self.side = swap_seq(self.mine, 1)
        self.pair = swap_seq(self.mine, 2)

    def corner(self):
        if self.over_z:
            self.side = self.order.pin(self.side)
            self.last = swap_seq(self.side, 2)
        else:
            self.pair = self.order.pin(self.pair)
            self.last = swap_seq(self.pair, 1)

    def pieces(self):
        return [self.mine, self.pair, self.side, self.last]


def blocks(value, count):
    size = value.shape[0] // count
    return [value[i * size : (i + 1) * size] for i in range(count)]


def shards_quad(
    media,
    media_ids,
    image_seq,
    image_valid,
    latents,
    w_query,
    w_key,
    w_value,
    w_out,
    w_up,
    w_down,
    media_gain,
    media_bias,
    latent_gain,
    latent_bias,
    ffn_gain,
    ffn_bias,
    cotangent,
):
    seq_index = lax.axis_index("seq")
    head_index = lax.axis_index("head")
    seq_size = lax.axis_size("seq")
    images = image_seq.shape[0]
    sequences = media_ids.shape[0] // LEN
    own_rows = latents.shape[0]
    width = w_query.shape[1]
    dim = media.shape[1]
    order = Order()
    media_gain, media_bias, latent_gain, latent_bias, ffn_gain, ffn_bias = (
        value.reshape(1, dim)
        for value in (media_gain, media_bias, latent_gain, latent_bias, ffn_gain, ffn_bias)
    )

    slots = jnp.array([0, 2, 1, 3], jnp.int32)
    per_device = images // 4
    which = ((slots ^ head_index)[:, None] * per_device + jnp.arange(per_device)[None, :]).reshape(-1)
    owners = seq_index * images + which
    local_seq = jnp.take(image_seq, which) - seq_index * sequences
    valid_float = jnp.take(image_valid, which).astype(F32)
    matches = media_ids[None, :] == owners[:, None]
    place = jnp.arange(media_ids.shape[0], dtype=jnp.int32)[None, :]
    run = jnp.sum(matches.astype(jnp.int32), axis=1)
    start = jnp.min(jnp.where(matches, place, media_ids.shape[0]), axis=1)
    low = jnp.where(run > 0, start - local_seq * LEN, 0)
    high = low + run
    slot = local_seq ^ head_index

    share = width // seq_size
    out_piece = lax.dynamic_slice_in_dim(w_out, seq_index * share, share, axis=0)
    raw_across = swap_head(jnp.concatenate([media, out_piece], axis=0), 2)
    raw_near = swap_head(media, 1)
    latents_near = swap_head(latents, 1)
    out_near = swap_head(w_out, 1)

    cotangent_near = swap_head(cotangent, 1)
    w_kv = jnp.concatenate([w_key, w_value], axis=1)
    w_qkv = jnp.concatenate([w_query, w_kv], axis=1)

    def media_step(rows, weights):
        return norm_project([rows], media_gain, media_bias, weights, 1.0, LEN)

    def stack(*values):
        return jnp.concatenate(values, axis=0)

    def add(left, right):
        return left + right

    def latent_step(own, other, weights):
        return norm_project([own, other], latent_gain, latent_bias, weights, 1.0)

    def forward(lists, kv_slots, latent_qkv, offset, before):
        count = len(kv_slots)
        return order(
            lambda *v: attention_forward(
                *v[:4], v[4 : 4 + count], v[4 + count], offset, v[5 + count :] or None, time=1.0
            ),
            lists,
            slot,
            low,
            high,
            *kv_slots,
            latent_qkv,
            *before,
        )

    kv_own, norm_own = order(media_step, media, w_kv)
    latents_across = swap_head(order.gate(latents), 2)
    early_qkv, early_low = order(latent_step, latents, latents_near, w_qkv)
    early = jnp.arange(images) // per_device % 2 == 0
    near_list, rest_list, full_list = order(
        lambda s, a, b: (
            list_images(early & (s < 2), a, b),
            list_images(jnp.logical_not(early & (s < 2)), a, b),
            list_images(s >= 0, a, b),
        ),
        slot,
        low,
        high,
    )
    kv_near, norm_near = order(media_step, raw_near, w_kv)
    outcome = forward(near_list, (kv_own, kv_near), early_qkv, 0, ())
    cotangent_across = swap_head(order.gate(cotangent), 2)
    out_first = order(stack, w_out, out_near)
    count = order(
        lambda v: jnp.broadcast_to(jnp.sum(v).reshape(1, 1), (8, 128)), valid_float
    )
    for bit in (1, 2, 4):
        count = order(add, count, swap_seq(count, bit))
    penalty_weight, pen_scale = order(
        lambda v, c: (v * (4.0 * images * seq_size / c[0, 0]), 1.0 / (HEADS * LATENTS * c[0, 0])),
        valid_float,
        count,
    )
    raw_across = order.pin(raw_across)
    raw_beyond = swap_head(raw_across, 1)
    out_piece = order(lambda v: v[LEN:], raw_across)
    out_far = lax.all_gather(out_piece, "seq", axis=0, tiled=True)
    kv_across, norm_across = order(media_step, raw_across, w_kv)
    kv_beyond, norm_beyond = order(media_step, raw_beyond, w_kv)
    kv_far = (kv_across, kv_beyond)
    latents_across = order.pin(latents_across)
    latents_beyond = swap_head(latents_across, 1)
    late_qkv, late_low = order(latent_step, latents_across, latents_beyond, w_qkv)

    def interleave(first, second):
        first, second = blocks(first, 2), blocks(second, 2)
        return stack(first[0], second[0], first[1], second[1])

    latent_qkv = order(interleave, early_qkv, late_qkv)
    attended, lse, entropy = forward(
        rest_list, (kv_own, kv_near, *kv_far), latent_qkv, 0, outcome
    )
    attended_across = swap_head(attended, 2)
    attended_near = swap_head(attended, 1)
    cotangent_across = order.pin(cotangent_across)
    cotangent_beyond = swap_head(cotangent_across, 1)
    cotangents = (cotangent, cotangent_across, cotangent_near, cotangent_beyond)
    pulled = order(lambda *v: cotangent_down(v[:4], v[4]), *cotangents, w_down)
    out_far = order.pin(out_far)
    out_beyond = swap_head(out_far, 1)
    attended_across = order.gate(attended_across)
    attended_beyond = swap_head(attended_across, 1)
    middle, ffn_low, hidden, grad_before, lower, upper = order(
        lambda *v: feed_forward(v[:4], v[4], v[5:7], v[7:11], *v[11:], ffn_gain, ffn_bias),
        attended,
        attended_near,
        attended_across,
        attended_beyond,
        out_first,
        out_far,
        out_beyond,
        latents,
        latents_across,
        latents_near,
        latents_beyond,
        pulled,
        w_up,
    )
    side = (seq_index % 2).reshape(1)
    place = (seq_index % 2 * 2 + seq_index // 2 % 2).reshape(1)
    v = Values()
    v.upper = swap_head(upper, 1)

    def lowadd():
        v.lower = order(add, lower, v.upper)
        v.Y = swap_head(v.lower, 2)

    def sum_steps(grads, over_z):
        made = []

        def start():
            made.append(SeqSum(order, grads(), over_z))

        return (
            start,
            lambda: made[0].split(),
            lambda: made[0].across(),
            lambda: made[0].spread(),
            lambda: made[0].corner(),
            lambda: made[0].pieces(),
        )

    def down_grads():
        return order(
            lambda x, h, *g: grad_halves(x, [(h, [part(one) for one in g])], "down_grad"),
            side,
            hidden,
            *cotangents,
        )

    def up_grads():
        return order(
            lambda x, h, g: grad_halves(x, [(h, [part(g)])], "up_grad"),
            side,
            ffn_low,
            grad_before,
        )

    norms = (norm_own, norm_near, norm_across, norm_beyond)

    def key_pairs(
        x, own, near, across, beyond, back, early_rows, late_rows, latent_part
    ):
        pairs = [
            (rows, [part(back, LEN, i)]) for i, rows in enumerate((own, near, across, beyond))
        ]
        for rows, at in ((early_rows, 0), (late_rows, 1)):
            pairs.append(
                (
                    rows,
                    [
                        part(latent_part, own_rows, at + 2 * i, slice(width, None))
                        for i in range(2)
                    ],
                )
            )
        return grad_halves(x, pairs, "key_grad")

    def key_grads():
        return order(
            key_pairs, side, *norms, v.kv_back, early_low, late_low, v.latent_back
        )

    d, d_1, d_2, d_3, d_4, down_parts = sum_steps(down_grads, OVER_Z[0])
    u, u_1, u_2, u_3, u_4, up_parts = sum_steps(up_grads, OVER_Z[1])
    k, k_1, k_2, k_3, k_4, key_parts = sum_steps(key_grads, OVER_Z[2])
    l, l_1, l_2, l_3, l_4, late_parts = sum_steps(
        lambda: order(
            late_grads, side, v.latent_back, early_low, late_low, attended, v.grad_branch
        ),
        OVER_Z[3],
    )

    def branch():
        v.branch, v.branch_upper = order(
            lambda h, w: project_halves(h, w, False, "branch"), hidden, w_down
        )
        v.BC = swap_head(v.branch_upper, 1)

    def bradd():
        v.branch = order(add, v.branch, v.BC)
        v.BY = swap_head(v.branch[own_rows:], 2)

    def res():
        v.result = order(
            lambda m, b, r: (m[:own_rows] + b[:own_rows].astype(F32) + r.astype(F32)).astype(BF16),
            middle,
            v.branch,
            v.BY,
        )

    def gpair():
        v.pair = order(
            lambda a, r: a + jnp.concatenate(blocks(r, 2)[::-1], axis=0), v.lower, v.Y
        )
        v.G = [swap_head(piece, 1) for piece in blocks(v.pair, 2)]

    def mback():
        out = order(
            lambda *a: middle_back(a[:3], a[3], a[4:8], ffn_gain, ffn_bias, a[8]),
            v.pair,
            *v.G,
            middle,
            *cotangents,
            w_out,
        )
        v.grad_branch, v.grad_middle, v.grad_attended = out[:3]
        v.ffn_sums = out[3:]

    def attb():
        v.latent_back, v.kv_back = order(
            lambda *a: attention_backward(*a[:5], a[5:9], *a[9:]),
            full_list,
            slot,
            low,
            high,
            penalty_weight,
            kv_own,
            kv_near,
            *kv_far,
            latent_qkv,
            v.grad_attended,
            lse,
            entropy,
        )

    def swap_pieces(value):
        return [swap_head(piece, 1) for piece in blocks(value, 2)]

    def pb():
        v.K1 = swap_pieces(order(lambda a, w: project_slot(a, 3, w), v.kv_back, w_kv))

    def pa():
        v.MF = swap_head(
            order(lambda a, w, *r: project_slot(a, 2, w, r), v.kv_back, w_kv, *v.K1), 2
        )

    def pn():
        v.K2 = swap_pieces(order(lambda a, w: project_slot(a, 1, w), v.kv_back, w_kv))

    def po():
        v.media_near = order(
            lambda a, w, *r: project_slot(a, 0, w, r), v.kv_back, w_kv, *v.K2
        )

    def lb():
        v.latent_lower, upper = order(
            lambda a, w: project_halves(a, w, True, "latent_back"), v.latent_back, w_qkv
        )
        v.LC = swap_head(upper, 1)

    def ladd():
        v.latent_lower = order(add, v.latent_lower, v.LC)
        v.LY = swap_head(v.latent_lower[own_rows:], 2)

    def nbm():
        v.media_grad, *v.media_sums = order(
            lambda *a: norm_back(*a, media_gain, media_bias), v.media_near, v.MF, media
        )

    def nbl():
        v.latents_grad, *v.latent_sums = order(
            lambda *a: norm_back(*a[:3], latent_gain, latent_bias, a[3]),
            v.latent_lower,
            v.LY,
            latents,
            v.grad_middle,
        )

    def s0():
        entropy_local = jnp.sum(entropy.reshape(images, -1) * valid_float[:, None])
        part_of = 1.0 / lax.axis_size("head")
        v.sums = order(
            stack,
            *v.media_sums,
            *v.latent_sums,
            *[value * part_of for value in v.ffn_sums],
            jnp.broadcast_to(entropy_local, (2, dim)),
        )
        v.moved = swap_head(v.sums, 1)

    def add_moved():
        v.sums = order(add, v.sums, v.moved)

    def s1():
        add_moved()
        v.moved = swap_head(v.sums, 2)

    def s2():
        add_moved()
        v.moved = swap_seq(v.sums, 1)

    def s3():
        add_moved()
        v.moved = swap_seq(v.sums, 2)

    def s4():
        add_moved()
        v.moved = swap_seq(v.sums, 4)

    s5 = add_moved

    def d_5():
        parts = down_parts()
        v.down = order(lambda p, *a: join_rows(p, a, ((0, dim),))[0], place, *parts)

    def u_5():
        parts = up_parts()
        v.up = order(lambda p, *a: join_rows(p, a, ((0, dim),))[0], place, *parts)

    def k_5():
        parts = key_parts()
        v.key, v.value = order(
            lambda p, *a: join_rows(p, a, ((0, width), (width, 2 * width))), place, *parts
        )

    def l_5():
        v.query, v.out = order(lambda p, *a: join_late(p, a), place, *late_parts())

    steps = (
        d, lowadd, u, gpair, mback, d_1, attb, d_2, lb, pb, u_1, l, k, d_3, u_2, l_1, ladd,
        pa, k_1, d_4, branch, nbl, pn, u_3, l_2, d_5, k_2, bradd, po, u_4, nbm, s0, l_3, s1,
        k_3, s2, u_5, l_4, s3, k_4, k_5, s4, res, l_5, s5,
    )
    for step in steps:
        step()
    sums = v.sums
    return (
        v.result,
        sums[6, 0] * pen_scale,
        v.media_grad,
        v.latents_grad,
        v.query,
        v.key,
        v.value,
        v.out,
        v.up,
        v.down,
        sums[0],
        sums[1],
        sums[2],
        sums[3],
        sums[4],
        sums[5],
    )


def shards_any(
    media,
    media_ids,
    image_seq,
    image_valid,
    latents,
    w_query,
    w_key,
    w_value,
    w_out,
    w_up,
    w_down,
    media_gain,
    media_bias,
    latent_gain,
    latent_bias,
    ffn_gain,
    ffn_bias,
    cotangent,
):
    seq_index = lax.axis_index("seq")
    head_index = lax.axis_index("head")
    images = image_seq.shape[0]
    sequences = media_ids.shape[0] // LEN
    own_rows = latents.shape[0]
    inner_width = w_query.shape[1]
    seq_size = lax.axis_size("seq")
    valid_float = image_valid.astype(F32)

    media_norm, media_hat, media_inv = normalize(media.astype(F32), media_gain, media_bias)
    latent_rows = lax.all_gather(latents, "head", axis=0, tiled=True)
    media_all = lax.all_gather(media_norm.astype(BF16), "head", axis=0, tiled=True)
    grad_all = lax.all_gather(cotangent, "head", axis=0, tiled=True)
    latent_float = latent_rows.astype(F32)
    latent_norm, latent_hat, latent_inv = normalize(latent_float, latent_gain, latent_bias)
    latent_low = latent_norm.astype(BF16)

    count_all = jnp.sum(valid_float).reshape(1, 1)
    count_all = sum_seq(jnp.broadcast_to(count_all, (8, 128)))[0, 0]
    pen_scale = 1.0 / (HEADS * LATENTS * count_all)
    weighted_scale = 4.0 * images * seq_size / count_all

    owners = seq_index * images + jnp.arange(images, dtype=jnp.int32)
    local_seq = image_seq - seq_index * sequences
    matches = media_ids[None, :] == owners[:, None]
    place = jnp.arange(media_ids.shape[0], dtype=jnp.int32)[None, :]
    run = jnp.sum(matches.astype(jnp.int32), axis=1)
    start = jnp.min(jnp.where(matches, place, media_ids.shape[0]), axis=1)
    low = jnp.where(run > 0, start - local_seq * LEN, 0)
    high = low + run
    slot = local_seq
    listed = list_images(jnp.full((images,), True), low, high)

    w_kv = jnp.concatenate([w_key, w_value], axis=1)
    w_qkv = jnp.concatenate([w_query, w_kv], axis=1)
    latent_qkv = product(latent_low, w_qkv).astype(BF16)
    kv_slots = [product(media_all, w_kv).astype(BF16)]
    attended, lse, entropy = attention_forward(listed, slot, low, high, kv_slots, latent_qkv)

    branch = lax.psum(product(attended, w_out).astype(BF16), "head").astype(F32)
    middle = latent_float + branch
    ffn_norm, ffn_hat, ffn_inv = normalize(middle, ffn_gain, ffn_bias)
    ffn_low = ffn_norm.astype(BF16)
    before_gelu = product(ffn_low, w_up)
    activated, gelu_slope = gelu_parts(before_gelu)
    hidden = activated.astype(BF16)
    grad_before = (contract_cols(grad_all, w_down) * gelu_slope).astype(BF16)
    grad_ffn_part = contract_cols(grad_before, w_up).astype(BF16)
    grad_ffn = lax.psum(grad_ffn_part, "head").astype(F32)
    down_grad = contract_rows(hidden, grad_all).astype(BF16)
    up_grad = contract_rows(ffn_low, grad_before).astype(BF16)
    up_grad, down_grad = lax.psum((up_grad, down_grad), "seq")

    ffn_branch = product(hidden, w_down).astype(BF16)
    ffn_branch = lax.psum_scatter(ffn_branch, "head", scatter_dimension=0, tiled=True)

    def own(value):
        return lax.dynamic_slice_in_dim(value, head_index * own_rows, own_rows, axis=0)

    result = (own(middle) + ffn_branch.astype(F32)).astype(BF16)

    middle_part, ffn_gain_part, ffn_bias_part = normalize_back(
        grad_ffn, ffn_hat, ffn_inv, ffn_gain
    )
    grad_middle = grad_all.astype(F32) + middle_part
    grad_branch = grad_middle.astype(BF16)
    grad_attended = contract_cols(grad_branch, w_out).astype(BF16)
    out_grad = contract_rows(attended, grad_branch)
    back = attention_backward(
        listed,
        slot,
        low,
        high,
        valid_float * weighted_scale,
        kv_slots,
        latent_qkv,
        grad_attended,
        lse,
        entropy,
    )
    latent_back, kv_back = back
    grad_media_norm = lax.psum_scatter(
        contract_cols(kv_back, w_kv).astype(BF16), "head", scatter_dimension=0, tiled=True
    ).astype(F32)
    grad_latent_part = contract_cols(latent_back, w_qkv).astype(BF16)
    grad_latent_norm = lax.psum_scatter(
        grad_latent_part, "head", scatter_dimension=0, tiled=True
    ).astype(F32)
    latent_grads = contract_rows(latent_low, latent_back)
    kv_grads = latent_grads[:, inner_width:] + contract_rows(media_all, kv_back)
    late = (
        latent_grads[:, :inner_width].astype(BF16),
        kv_grads.astype(BF16),
        out_grad.astype(BF16),
    )
    up_grad, down_grad, *late = lax.optimization_barrier((up_grad, down_grad) + late)
    query_grad, kv_grads, out_grad = lax.psum(tuple(late), "seq")

    media_rows_grad, media_gain_part, media_bias_part = normalize_back(
        grad_media_norm, media_hat, media_inv, media_gain
    )
    latent_part, latent_gain_part, latent_bias_part = normalize_back(
        grad_latent_norm, own(latent_hat), own(latent_inv), latent_gain
    )
    latents_grad = (own(grad_middle) + latent_part).astype(BF16)
    entropy_local = jnp.sum(entropy.reshape(images, -1) * valid_float[:, None])
    share = 1.0 / lax.axis_size("head")
    sums = jnp.stack(
        [
            media_gain_part,
            media_bias_part,
            latent_gain_part,
            latent_bias_part,
            ffn_gain_part * share,
            ffn_bias_part * share,
            jnp.broadcast_to(entropy_local, media_gain.shape),
            jnp.zeros_like(media_gain),
        ]
    )
    sums = sum_seq(sum_head(sums))
    return (
        result,
        sums[6, 0] * pen_scale,
        media_rows_grad.astype(BF16),
        latents_grad,
        query_grad.astype(F32),
        kv_grads[:, :inner_width].astype(F32),
        kv_grads[:, inner_width:].astype(F32),
        out_grad.astype(F32),
        up_grad.astype(F32),
        down_grad.astype(F32),
        sums[0],
        sums[1],
        sums[2],
        sums[3],
        sums[4],
        sums[5],
    )


def solution(mesh):
    rows = P(("seq", "head"), None)
    columns = P(None, "head")
    lines = P("head", None)
    quad = mesh.shape["head"] == 4 and mesh.shape["seq"] == 8
    return jax.shard_map(
        shards_quad if quad else shards_any,
        mesh=mesh,
        in_specs=(
            (rows, P("seq"), P("seq"), P("seq"), rows)
            + (columns, columns, columns, lines, columns, lines)
            + (P(),) * 6
            + (rows,)
        ),
        out_specs=(
            (rows, P(), rows, rows)
            + (columns, columns, columns, lines, columns, lines)
            + (P(),) * 6
        ),
        check_vma=False,
    )
```

```python
import jax
import jax.numpy as jnp
from jax import lax
from jax.experimental import pallas as pl
from jax.experimental.pallas import tpu as pltpu
from jax.sharding import PartitionSpec as P

HEADS = 16
HEAD_DIM = 96
LATENTS = 64
LEN = 1024
KEY_BLOCK = 256

epsilon = 1e-05
BF16 = jnp.bfloat16


def cost(microseconds):
    return pl.CostEstimate(
        flops=int(microseconds * 1.1e9), transcendentals=0, bytes_accessed=int(microseconds * 3e6)
    )


F32 = jnp.float32


def normalize(row_values, norm_gain, norm_bias):
    row_mean = jnp.mean(row_values, axis=-1, keepdims=True)
    centred = row_values - row_mean
    variance = jnp.mean(centred * centred, axis=-1, keepdims=True)
    inverse = lax.rsqrt(variance + epsilon)
    scaled = centred * inverse
    return (scaled * norm_gain + norm_bias, scaled, inverse)


def normalize_back(incoming, scaled, inverse, norm_gain):
    weighted = incoming * norm_gain
    first_mean = jnp.mean(weighted, axis=-1, keepdims=True)
    second_mean = jnp.mean(weighted * scaled, axis=-1, keepdims=True)
    outgoing = inverse * (weighted - first_mean - scaled * second_mean)
    return (outgoing, jnp.sum(incoming * scaled, axis=0), jnp.sum(incoming, axis=0))


def product(left_side, right_side):
    return jnp.dot(left_side, right_side, preferred_element_type=F32)


def contract_rows(left_side, right_side):
    return lax.dot_general(
        left_side, right_side, (((0,), (0,)), ((), ())), preferred_element_type=F32
    )


def contract_cols(left_side, right_side):
    return lax.dot_general(
        left_side, right_side, (((1,), (1,)), ((), ())), preferred_element_type=F32
    )


def gelu_parts(inputs):
    normal_cdf = 0.5 * (1.0 + lax.erf(inputs * 0.7071067811865476))
    density = jnp.exp(-0.5 * inputs * inputs) * 0.3989422804014327
    return (inputs * normal_cdf, normal_cdf + inputs * density)


def block_diagonal(rows, heads):
    lane = lax.broadcasted_iota(jnp.int32, rows.shape, 1)
    parts = []
    for head in range(heads):
        inside = (lane >= head * HEAD_DIM) & (lane < (head + 1) * HEAD_DIM)
        parts.append(jnp.where(inside, rows, jnp.zeros_like(rows)))
    return jnp.concatenate(parts, axis=0)


def take_diagonal(wide, heads):
    lane = lax.broadcasted_iota(jnp.int32, (LATENTS, wide.shape[1]), 1)
    out = wide[:LATENTS]
    for head in range(1, heads):
        out = jnp.where(lane >= head * HEAD_DIM, wide[head * LATENTS : (head + 1) * LATENTS], out)
    return out


def start_loads(kv_hbm, kv_vmem, sems):
    copies = []
    at = 0
    for i, ref in enumerate(kv_hbm):
        size = ref.shape[0]
        copies.append(pltpu.make_async_copy(ref, kv_vmem.at[pl.ds(at, size), :], sems.at[i]))
        at += size
    for copy in copies:
        copy.start()
    return copies


WINDOWS = (256, 512)


def image_rows(image):
    return pl.ds(pl.multiple_of(image * LATENTS, LATENTS), LATENTS)


def window_start(lo, size):
    return jnp.minimum(lo // 16 * 16, LEN - size)


def list_images(here, low, high):
    images = here.shape[0]
    kind = len(WINDOWS) - sum(
        (high - window_start(low, size) <= size).astype(jnp.int32) for size in WINDOWS
    )
    kind = jnp.where(here, kind, len(WINDOWS) + 1)
    number = jnp.arange(images, dtype=jnp.int32)
    key = kind * images + number
    rank = jnp.sum((key[None, :] < key[:, None]).astype(jnp.int32), axis=1)
    listed = jnp.sum(jnp.where(rank[None, :] == number[:, None], number[None, :], 0), axis=1)
    ends = [jnp.sum((kind <= i).astype(jnp.int32)).reshape(1) for i in range(len(WINDOWS) + 1)]
    return jnp.concatenate([listed, *ends])


def each_image(listed_ref, images, short, long):
    begin = 0
    for i, size in enumerate(WINDOWS):
        end = listed_ref[images + i]

        def pair(index, _, size=size, begin=begin, end=end):
            at = begin + 2 * index
            short(size, [listed_ref[at], listed_ref[jnp.minimum(at + 1, end - 1)]])
            return 0

        lax.fori_loop(0, (end - begin + 1) // 2, pair, 0)
        begin = end

    def single(index, _):
        long(listed_ref[index])
        return 0

    lax.fori_loop(begin, listed_ref[images + len(WINDOWS)], single, 0)


def attention_forward(
    listed, slot, low, high, kv_slots, latent_qkv, offset=0, before=None, time=15.0
):
    images = slot.shape[0]
    count = len(kv_slots)
    keys = sum(kv.shape[0] for kv in kv_slots)
    width = latent_qkv.shape[1] // 3
    heads = width // HEAD_DIM
    rows = heads * LATENTS
    scale = HEAD_DIM ** (-0.5)
    given = () if before is None else tuple(before)
    whole_rows = latent_qkv.shape[0] == images * LATENTS

    def source_rows(image):
        return image_rows(image if whole_rows else image // 8 * 4 + image % 4)


    def body(listed_ref, slot_ref, low_ref, high_ref, *refs):
        kv_hbm = refs[:count]
        qkv_ref = refs[count]
        given_refs = refs[count + 1 : count + 1 + len(given)]
        out_ref, lse_ref, ent_ref, kv_vmem, scores, sems = refs[count + 1 + len(given) :]
        copies = start_loads(kv_hbm, kv_vmem, sems)
        if given:
            out_ref[...] = given_refs[0][...]
            lse_ref[...] = given_refs[1][...]
            ent_ref[...] = given_refs[2][...]
        for copy in copies:
            copy.wait()

        def short(size, pair):
            for image in pair:
                at = source_rows(image)
                lo = low_ref[image]
                hi = high_ref[image]
                start = window_start(lo, size)
                place = pl.multiple_of((slot_ref[image] - offset) * LEN + start, 16)
                query = block_diagonal(qkv_ref[at, :width], heads)
                own = contract_cols(qkv_ref[at, width : 2 * width], query) * scale
                part = contract_cols(kv_vmem[pl.ds(place, size), :width], query) * scale
                key = start + lax.broadcasted_iota(jnp.int32, part.shape, 0)
                part = jnp.where((key >= lo) & (key < hi), part, -1e30)
                peak = jnp.maximum(
                    jnp.max(own, axis=0, keepdims=True), jnp.max(part, axis=0, keepdims=True)
                )
                own = own - peak
                part = part - peak
                own_exp = jnp.exp(own)
                part_exp = jnp.exp(part)
                total = jnp.sum(own_exp, axis=0, keepdims=True) + jnp.sum(
                    part_exp, axis=0, keepdims=True
                )
                moment = jnp.sum(own_exp * own, axis=0, keepdims=True) + jnp.sum(
                    part_exp * part, axis=0, keepdims=True
                )
                inverse = 1.0 / total
                log_total = jnp.log(total)
                lse_ref[image] = peak + log_total
                ent_ref[image] = log_total - moment * inverse
                wide = contract_rows((own_exp * inverse).astype(BF16), qkv_ref[at, 2 * width :])
                wide = wide + contract_rows(
                    (part_exp * inverse).astype(BF16), kv_vmem[pl.ds(place, size), width:]
                )
                out_ref[image_rows(image), :] = take_diagonal(wide, heads).astype(BF16)

        def long(image):
            at = source_rows(image)
            base = (slot_ref[image] - offset) * LEN
            lo = low_ref[image]
            hi = high_ref[image]
            first = lo // KEY_BLOCK
            last = (hi + KEY_BLOCK - 1) // KEY_BLOCK
            query = block_diagonal(qkv_ref[at, :width], heads)
            own = contract_cols(qkv_ref[at, width : 2 * width], query) * scale
            peak = jnp.max(own, axis=0, keepdims=True)

            def first_pass(block, peak):
                row = pl.multiple_of(base + block * KEY_BLOCK, KEY_BLOCK)
                part = contract_cols(kv_vmem[pl.ds(row, KEY_BLOCK), :width], query) * scale
                key = block * KEY_BLOCK + lax.broadcasted_iota(jnp.int32, part.shape, 0)
                part = jnp.where((key >= lo) & (key < hi), part, -1e30)
                to = pl.multiple_of((block - first) * KEY_BLOCK, KEY_BLOCK)
                scores[pl.ds(to, KEY_BLOCK), :] = part
                return jnp.maximum(peak, jnp.max(part, axis=0, keepdims=True))

            peak = lax.fori_loop(first, last, first_pass, peak)
            own = own - peak
            own_exp = jnp.exp(own)
            total = jnp.sum(own_exp, axis=0, keepdims=True)
            moment = jnp.sum(own_exp * own, axis=0, keepdims=True)

            def second_pass(block, carry):
                total, moment = carry
                to = pl.multiple_of((block - first) * KEY_BLOCK, KEY_BLOCK)
                part = scores[pl.ds(to, KEY_BLOCK), :] - peak
                part_exp = jnp.exp(part)
                scores[pl.ds(to, KEY_BLOCK), :] = part_exp
                return (
                    total + jnp.sum(part_exp, axis=0, keepdims=True),
                    moment + jnp.sum(part_exp * part, axis=0, keepdims=True),
                )

            total, moment = lax.fori_loop(first, last, second_pass, (total, moment))
            inverse = 1.0 / total
            log_total = jnp.log(total)
            lse_ref[image] = peak + log_total
            ent_ref[image] = log_total - moment * inverse
            wide = contract_rows((own_exp * inverse).astype(BF16), qkv_ref[at, 2 * width :])

            def third_pass(block, wide):
                to = pl.multiple_of((block - first) * KEY_BLOCK, KEY_BLOCK)
                row = pl.multiple_of(base + block * KEY_BLOCK, KEY_BLOCK)
                low_prob = (scores[pl.ds(to, KEY_BLOCK), :] * inverse).astype(BF16)
                return wide + contract_rows(low_prob, kv_vmem[pl.ds(row, KEY_BLOCK), width:])

            wide = lax.fori_loop(first, last, third_pass, wide)
            out_ref[image_rows(image), :] = take_diagonal(wide, heads).astype(BF16)

        each_image(listed_ref, images, short, long)

    shapes = (
        jax.ShapeDtypeStruct((images * LATENTS, width), BF16),
        jax.ShapeDtypeStruct((images, 1, rows), F32),
        jax.ShapeDtypeStruct((images, 1, rows), F32),
    )
    scalar = pl.BlockSpec(memory_space=pltpu.SMEM)
    vmem = pl.BlockSpec(memory_space=pltpu.VMEM)
    return pl.pallas_call(
        body,
        out_shape=shapes,
        in_specs=[scalar] * 4
        + [pl.BlockSpec(memory_space=pl.ANY)] * count
        + [vmem] * (1 + len(given)),
        out_specs=(vmem,) * 3,
        scratch_shapes=[
            pltpu.VMEM((keys, 2 * width), BF16),
            pltpu.VMEM((LEN, rows), F32),
            pltpu.SemaphoreType.DMA((count,)),
        ],
        compiler_params=pltpu.CompilerParams(vmem_limit_bytes=48 << 20),
        cost_estimate=cost(time),
        name="attention_forward",
    )(listed, slot, low, high, *kv_slots, latent_qkv, *given)


def attention_backward(
    listed, slot, low, high, weight, kv_slots, latent_qkv, grad_out, lse, entropy
):
    images = slot.shape[0]
    count = len(kv_slots)
    keys = sum(kv.shape[0] for kv in kv_slots)
    width = latent_qkv.shape[1] // 3
    heads = width // HEAD_DIM
    rows = heads * LATENTS
    scale = HEAD_DIM ** (-0.5)

    def body(listed_ref, slot_ref, low_ref, high_ref, weight_ref, *refs):
        kv_hbm = refs[:count]
        qkv_ref, grad_ref, lse_ref, ent_ref = refs[count : count + 4]
        own_out, key_out, kv_vmem, probs, slopes, totals, sems = refs[count + 4 :]
        copies = start_loads(kv_hbm, kv_vmem, sems)
        totals[...] = jnp.zeros_like(totals)
        for copy in copies:
            copy.wait()

        def short(size, pair):
            for which, image in enumerate(pair):
                repeated = jnp.logical_and(which == 1, pair[0] == image)
                at = image_rows(image)
                lo = low_ref[image]
                hi = high_ref[image]
                pull = weight_ref[image]
                start = window_start(lo, size)
                place = pl.multiple_of(slot_ref[image] * LEN + start, 16)
                window = pl.ds(place, size)
                query = block_diagonal(qkv_ref[at, :width], heads)
                grad = block_diagonal(grad_ref[at, :], heads)
                log_total = lse_ref[image]
                ent = ent_ref[image]
                own_key = qkv_ref[at, width : 2 * width]
                own_log = contract_cols(own_key, query) * scale - log_total
                own_prob = jnp.exp(own_log)
                own_slope = contract_cols(qkv_ref[at, 2 * width :], grad)
                part = contract_cols(kv_vmem[window, :width], query) * scale
                key = start + lax.broadcasted_iota(jnp.int32, part.shape, 0)
                part = jnp.where((key >= lo) & (key < hi), part - log_total, -1e30)
                prob = jnp.exp(part)
                slope = contract_cols(kv_vmem[window, width:], grad)
                centre = jnp.sum(own_prob * own_slope, axis=0, keepdims=True)
                centre = centre + jnp.sum(prob * slope, axis=0, keepdims=True)
                own_low = own_prob * (own_slope - pull * (own_log + ent) - centre)
                own_low = own_low.astype(BF16)
                low_grad = (prob * (slope - pull * (part + ent) - centre)).astype(BF16)
                grad_query = contract_rows(own_low, own_key)
                grad_query = grad_query + contract_rows(low_grad, kv_vmem[window, :width])
                own_out[at, width : 2 * width] = (product(own_low, query) * scale).astype(BF16)
                own_out[at, 2 * width :] = product(own_prob.astype(BF16), grad).astype(BF16)
                once = jnp.where(repeated, 0.0, 1.0)
                totals[window, :width] += product(low_grad, query) * (scale * once)
                totals[window, width:] += product(prob.astype(BF16), grad) * once
                own_out[at, :width] = (take_diagonal(grad_query, heads) * scale).astype(BF16)

        def long(image):
            at = image_rows(image)
            base = slot_ref[image] * LEN
            lo = low_ref[image]
            hi = high_ref[image]
            pull = weight_ref[image]
            first = lo // KEY_BLOCK
            last = (hi + KEY_BLOCK - 1) // KEY_BLOCK
            query = block_diagonal(qkv_ref[at, :width], heads)
            grad = block_diagonal(grad_ref[at, :], heads)
            log_total = lse_ref[image]
            ent = ent_ref[image]
            own_key = qkv_ref[at, width : 2 * width]
            own_log = contract_cols(own_key, query) * scale - log_total
            own_prob = jnp.exp(own_log)
            own_slope = contract_cols(qkv_ref[at, 2 * width :], grad)
            centre = jnp.sum(own_prob * own_slope, axis=0, keepdims=True)
            own_slope = own_slope - pull * (own_log + ent)

            def first_pass(block, centre):
                row = pl.multiple_of(base + block * KEY_BLOCK, KEY_BLOCK)
                to = pl.multiple_of((block - first) * KEY_BLOCK, KEY_BLOCK)
                part = contract_cols(kv_vmem[pl.ds(row, KEY_BLOCK), :width], query) * scale
                key = block * KEY_BLOCK + lax.broadcasted_iota(jnp.int32, part.shape, 0)
                part = jnp.where((key >= lo) & (key < hi), part - log_total, -1e30)
                prob = jnp.exp(part)
                slope = contract_cols(kv_vmem[pl.ds(row, KEY_BLOCK), width:], grad)
                probs[pl.ds(to, KEY_BLOCK), :] = prob
                slopes[pl.ds(to, KEY_BLOCK), :] = slope - pull * (part + ent)
                return centre + jnp.sum(prob * slope, axis=0, keepdims=True)

            centre = lax.fori_loop(first, last, first_pass, centre)
            own_low = (own_prob * (own_slope - centre)).astype(BF16)
            grad_query = contract_rows(own_low, own_key)
            own_out[at, width : 2 * width] = (product(own_low, query) * scale).astype(BF16)
            own_out[at, 2 * width :] = product(own_prob.astype(BF16), grad).astype(BF16)

            def second_pass(block, grad_query):
                row = pl.multiple_of(base + block * KEY_BLOCK, KEY_BLOCK)
                to = pl.multiple_of((block - first) * KEY_BLOCK, KEY_BLOCK)
                prob = probs[pl.ds(to, KEY_BLOCK), :]
                low_grad = (prob * (slopes[pl.ds(to, KEY_BLOCK), :] - centre)).astype(BF16)
                totals[pl.ds(row, KEY_BLOCK), :width] += product(low_grad, query) * scale
                totals[pl.ds(row, KEY_BLOCK), width:] += product(prob.astype(BF16), grad)
                return grad_query + contract_rows(
                    low_grad, kv_vmem[pl.ds(row, KEY_BLOCK), :width]
                )

            grad_query = lax.fori_loop(first, last, second_pass, grad_query)
            own_out[at, :width] = (take_diagonal(grad_query, heads) * scale).astype(BF16)

        each_image(listed_ref, images, short, long)
        key_out[...] = totals[...].astype(BF16)

    scalar = pl.BlockSpec(memory_space=pltpu.SMEM)
    vmem = pl.BlockSpec(memory_space=pltpu.VMEM)
    return pl.pallas_call(
        body,
        out_shape=(
            jax.ShapeDtypeStruct((images * LATENTS, 3 * width), BF16),
            jax.ShapeDtypeStruct((keys, 2 * width), BF16),
        ),
        in_specs=[scalar] * 5 + [pl.BlockSpec(memory_space=pl.ANY)] * count + [vmem] * 4,
        out_specs=(vmem, vmem),
        scratch_shapes=[
            pltpu.VMEM((keys, 2 * width), BF16),
            pltpu.VMEM((LEN, rows), F32),
            pltpu.VMEM((LEN, rows), F32),
            pltpu.VMEM((keys, 2 * width), F32),
            pltpu.SemaphoreType.DMA((count,)),
        ],
        compiler_params=pltpu.CompilerParams(vmem_limit_bytes=56 << 20),
        cost_estimate=cost(0.5),
        name="attention_backward",
    )(listed, slot, low, high, weight, *kv_slots, latent_qkv, grad_out, lse, entropy)


ROW_BLOCK = 256


def call(body, grid, inputs, outputs, name, time=5.0, scratch=()):
    return pl.pallas_call(
        body,
        out_shape=tuple(jax.ShapeDtypeStruct(shape, dtype) for shape, dtype, _ in outputs),
        grid=(grid,),
        in_specs=[spec for _, spec in inputs],
        out_specs=tuple(spec for _, _, spec in outputs),
        scratch_shapes=list(scratch),
        compiler_params=pltpu.CompilerParams(
            dimension_semantics=("arbitrary",), vmem_limit_bytes=56 << 20
        ),
        cost_estimate=cost(time),
        name=name,
    )(*[value for value, _ in inputs])


def by_rows(width, move=lambda i: i, size=ROW_BLOCK):
    return pl.BlockSpec((size, width), lambda i: (move(i), 0))


def whole(value):
    return pl.BlockSpec(value.shape, lambda i: (0,) * value.ndim, pipeline_mode=pl.Buffered(1))


def stacked(values):
    steps = values[0].shape[0] // ROW_BLOCK
    return [
        (value, by_rows(value.shape[1], lambda i, k=k: jnp.clip(i - k * steps, 0, steps - 1)))
        for k, value in enumerate(values)
    ]


def stacked_rows(refs, values):
    steps = values[0].shape[0] // ROW_BLOCK
    rows = refs[0][...]
    for k in range(1, len(values)):
        rows = jnp.where(pl.program_id(0) >= k * steps, refs[k][...], rows)
    return rows


def low_half(i):
    return jnp.minimum(i, 1)


def high_half(i):
    return jnp.maximum(i - 2, 0)


def pair_inputs(pair, rest):
    return [(pair, by_rows(pair.shape[1], low_half)), (rest, by_rows(rest.shape[1], high_half))]


def pick(pair_ref, rest_ref):
    return jnp.where(pl.program_id(0) < 2, pair_ref[...], rest_ref[...])


def put_halves(low_ref, high_ref, value):
    @pl.when(pl.program_id(0) < 2)
    def _():
        low_ref[...] = value

    @pl.when(pl.program_id(0) >= 2)
    def _():
        high_ref[...] = value


def half_outputs(width):
    return [
        ((2 * ROW_BLOCK, width), BF16, by_rows(width, low_half)),
        ((2 * ROW_BLOCK, width), BF16, by_rows(width, high_half)),
    ]


def add_up(ref, value):
    total = jnp.sum(value, axis=0, keepdims=True)

    @pl.when(pl.program_id(0) == 0)
    def _():
        ref[...] = total

    @pl.when(pl.program_id(0) > 0)
    def _():
        ref[...] += total


def sum_output(width):
    return ((1, width), F32, pl.BlockSpec((1, width), lambda i: (0, 0)))


def norm_project(rows, gain, bias, weights, time=7.5, count=None):
    width, wide = rows[0].shape[1], weights.shape[1]
    count = count or sum(part.shape[0] for part in rows)

    def body(*refs):
        value = stacked_rows(refs, rows)
        gain_ref, bias_ref, weight_ref, out_ref, norm_ref = refs[len(rows) :]
        norm = normalize(value.astype(F32), gain_ref[...], bias_ref[...])[0].astype(BF16)
        norm_ref[...] = norm
        out_ref[...] = product(norm, weight_ref[...]).astype(BF16)

    return call(
        body,
        count // ROW_BLOCK,
        stacked(rows) + [(gain, whole(gain)), (bias, whole(bias)), (weights, whole(weights))],
        [((count, wide), BF16, by_rows(wide)), ((count, width), BF16, by_rows(width))],
        "norm_project",
        time,
    )


def cotangent_down(rows, weights):
    wide = weights.shape[0]

    def body(*refs):
        refs[-1][...] = contract_cols(stacked_rows(refs, rows), refs[-2][...])

    return call(
        body,
        4,
        stacked(rows) + [(weights, whole(weights))],
        [((4 * ROW_BLOCK, wide), F32, by_rows(wide))],
        "cotangent_down",
        10.0,
    )[0]


def feed_forward(attended, near_weights, far_weights, latent_rows, pulled, w_up, gain, bias):
    width = attended[0].shape[1]
    dim = w_up.shape[0]
    wide = w_up.shape[1]

    def body(*refs):
        own, near, across, beyond, first_ref, far_ref, far_rest, *lat_refs = refs[:11]
        pulled_ref, up_ref, gain_ref, bias_ref, middle_ref, ffn_ref, hidden_ref, grad_ref = refs[
            11:19
        ]
        low_ref, high_ref, second_ref = refs[19:]

        @pl.when(pl.program_id(0) == 0)
        def _():
            second_ref[:width, :] = far_ref[...]
            second_ref[width:, :] = far_rest[...]

        rows = stacked_rows(lat_refs, latent_rows).astype(F32)
        rows = rows + product(jnp.concatenate([own[...], near[...]], axis=1), first_ref[...])
        rows = rows + product(jnp.concatenate([across[...], beyond[...]], axis=1), second_ref[...])
        middle_ref[...] = rows
        norm = normalize(rows, gain_ref[...], bias_ref[...])[0].astype(BF16)
        ffn_ref[...] = norm
        step = wide // 3
        for i in range(3):
            at = slice(i * step, (i + 1) * step)
            activated, slope = gelu_parts(product(norm, up_ref[:, at]))
            hidden_ref[:, at] = activated.astype(BF16)
            grad_ref[:, at] = (pulled_ref[:, at] * slope).astype(BF16)
        back = contract_cols(grad_ref[...], up_ref[...]).astype(BF16)
        put_halves(low_ref, high_ref, back)

    count = 4 * ROW_BLOCK
    return call(
        body,
        4,
        [
            (attended[0], by_rows(width)),
            (attended[1], by_rows(width, lambda i: i ^ 2)),
            (attended[2], by_rows(width, lambda i: i ^ 1)),
            (attended[3], by_rows(width, lambda i: i ^ 3)),
            (near_weights, whole(near_weights)),
            (far_weights[0], whole(far_weights[0])),
            (far_weights[1], whole(far_weights[1])),
        ]
        + stacked(latent_rows)
        + [
            (pulled, by_rows(wide)),
            (w_up, whole(w_up)),
            (gain, whole(gain)),
            (bias, whole(bias)),
        ],
        [
            ((count, dim), F32, by_rows(dim)),
            ((count, dim), BF16, by_rows(dim)),
            ((count, wide), BF16, by_rows(wide)),
            ((count, wide), BF16, by_rows(wide)),
        ]
        + half_outputs(dim),
        "feed_forward",
        27.0,
        scratch=[pltpu.VMEM((2 * width, dim), BF16)],
    )


def part(value, rows=None, at=0, columns=slice(None)):
    return (value, value.shape[0] if rows is None else rows, at, columns)


def grad_halves(side, pairs, name):
    half = pairs[0][0].shape[1] // 2
    inputs = []
    for left, rights in pairs:
        inputs.append(
            (
                left,
                pl.BlockSpec(
                    (left.shape[0], half),
                    lambda i, x: (0, (i + 1 + x[0]) % 2),
                ),
            )
        )
        for value, rows, at, _ in rights:
            spec = pl.BlockSpec(
                (rows, value.shape[1]), lambda i, x, at=at: (at, 0), pipeline_mode=pl.Buffered(1)
            )
            inputs.append((value, spec))
    value, _, _, columns = pairs[0][1][0]
    wide = len(range(*columns.indices(value.shape[1])))

    def body(x_ref, *refs):
        total = None
        index = 0
        for left, rights in pairs:
            left_ref = refs[index]
            row = 0
            for i, (_, rows, _, columns) in enumerate(rights):
                value = contract_rows(
                    left_ref[row : row + rows, :], refs[index + 1 + i][:, columns]
                )
                row += rows
                total = value if total is None else total + value
            index += 1 + len(rights)
        put_sides(refs[-2], refs[-1], total.astype(BF16))

    return side_call(body, side, inputs, half, wide, name)


def put_sides(other_ref, mine_ref, value):
    @pl.when(pl.program_id(0) == 0)
    def _():
        other_ref[...] = value

    @pl.when(pl.program_id(0) == 1)
    def _():
        mine_ref[...] = value


def side_call(body, side, inputs, half, wide, name):
    out = pl.BlockSpec((half, wide), lambda i, x: (0, 0))
    return pl.pallas_call(
        body,
        out_shape=(jax.ShapeDtypeStruct((half, wide), BF16),) * 2,
        grid_spec=pltpu.PrefetchScalarGridSpec(
            num_scalar_prefetch=1,
            grid=(2,),
            in_specs=[spec for _, spec in inputs],
            out_specs=(out, out),
        ),
        compiler_params=pltpu.CompilerParams(
            dimension_semantics=("arbitrary",), vmem_limit_bytes=56 << 20
        ),
        cost_estimate=cost(0.5),
        name=name,
    )(side, *[value for value, _ in inputs])


def late_grads(side, latent_back, early_low, late_low, attended, grad_branch):
    width = attended.shape[1]
    wide = grad_branch.shape[1]

    def body(x_ref, back_ref, early_ref, late_ref, attended_ref, branch_ref, other_ref, mine_ref):
        size = early_low.shape[0] // 2
        which = (pl.program_id(0) + 1 + x_ref[0]) % 2

        @pl.when(which == 0)
        def _():
            value = jnp.zeros((width, wide), F32)
            for i, low_ref in enumerate((early_ref, late_ref, early_ref, late_ref)):
                value = value + contract_rows(
                    back_ref[i * size : (i + 1) * size, :],
                    low_ref[i // 2 * size : (i // 2 + 1) * size, :],
                )
            put_sides(other_ref, mine_ref, value.astype(BF16))

        @pl.when(which == 1)
        def _():
            value = contract_rows(attended_ref[...], branch_ref[...]).astype(BF16)
            put_sides(other_ref, mine_ref, value)

    inputs = [
        (
            value,
            pl.BlockSpec(
                (value.shape[0], min(value.shape[1], size)),
                lambda i, x: (0, 0),
                pipeline_mode=pl.Buffered(1),
            ),
        )
        for value, size in (
            (latent_back, width),
            (early_low, wide),
            (late_low, wide),
            (attended, width),
            (grad_branch, wide),
        )
    ]
    return side_call(body, side, inputs, width, wide, "late_grads")


def join_rows(place, parts, splits):
    size = parts[0].shape[0]
    count = len(parts)

    def body(place_ref, *refs):
        step = pl.program_id(0)
        for i in range(count):

            @pl.when(step == i)
            def _():
                for (first, last), out_ref in zip(splits, refs[count:]):
                    out_ref[...] = refs[i][:, first:last].astype(F32)

    inputs = [
        pl.BlockSpec(value.shape, lambda i, p: (0, 0), pipeline_mode=pl.Buffered(1))
        for value in parts
    ]
    return pl.pallas_call(
        body,
        out_shape=tuple(
            jax.ShapeDtypeStruct((count * size, last - first), F32) for first, last in splits
        ),
        grid_spec=pltpu.PrefetchScalarGridSpec(
            num_scalar_prefetch=1,
            grid=(count,),
            in_specs=inputs,
            out_specs=tuple(
                pl.BlockSpec((size, last - first), lambda i, p: (i ^ p[0], 0))
                for first, last in splits
            ),
        ),
        compiler_params=pltpu.CompilerParams(
            dimension_semantics=("arbitrary",), vmem_limit_bytes=56 << 20
        ),
        cost_estimate=cost(0.5),
        name="join_rows",
    )(place, *parts)


def join_late(place, parts):
    size, dim = parts[0].shape

    def body(place_ref, own_ref, pair_ref, side_ref, last_ref, query_ref, out_ref):
        odd = place_ref[0] % 2 == 1
        first = place_ref[0] < 2

        def rows(low_ref, high_ref):
            low, high = low_ref[...], high_ref[...]
            return jnp.concatenate(
                [jnp.where(odd, high, low), jnp.where(odd, low, high)], axis=0
            ).astype(F32)

        mine, other = rows(own_ref, pair_ref), rows(side_ref, last_ref)
        query_ref[...] = jnp.where(first, mine, other).T
        out_ref[...] = jnp.where(first, other, mine)

    spec = pl.BlockSpec((size, 384), lambda i, p: (0, i))
    return pl.pallas_call(
        body,
        out_shape=(
            jax.ShapeDtypeStruct((dim, 2 * size), F32),
            jax.ShapeDtypeStruct((2 * size, dim), F32),
        ),
        grid_spec=pltpu.PrefetchScalarGridSpec(
            num_scalar_prefetch=1,
            grid=(dim // 384,),
            in_specs=[spec] * 4,
            out_specs=(
                pl.BlockSpec((384, 2 * size), lambda i, p: (i, 0)),
                pl.BlockSpec((2 * size, 384), lambda i, p: (0, i)),
            ),
        ),
        compiler_params=pltpu.CompilerParams(dimension_semantics=("arbitrary",)),
        cost_estimate=cost(0.5),
        name="join_late",
    )(place, *parts)


def project_halves(rows, weights, transposed, name):
    wide = weights.shape[0] if transposed else weights.shape[1]

    def body(rows_ref, weight_ref, low_ref, high_ref):
        if transposed:
            out = contract_cols(rows_ref[...], weight_ref[...])
        else:
            out = product(rows_ref[...], weight_ref[...])
        put_halves(low_ref, high_ref, out.astype(BF16))

    return call(
        body,
        4,
        [(rows, by_rows(rows.shape[1])), (weights, whole(weights))],
        half_outputs(wide),
        name,
        0.5,
    )


def project_slot(rows, slot, weights, added=()):
    wide = weights.shape[0]
    blocks_in = LEN // ROW_BLOCK

    def body(rows_ref, weight_ref, *refs):
        out = contract_cols(rows_ref[...], weight_ref[...])
        if added:
            out = out + stacked_rows(refs, added).astype(F32)
        refs[-1][...] = out.astype(BF16)

    return call(
        body,
        blocks_in,
        [
            (rows, by_rows(rows.shape[1], lambda i: i + slot * blocks_in)),
            (weights, whole(weights)),
        ]
        + (stacked(added) if added else []),
        [((LEN, wide), BF16, by_rows(wide))],
        "project_slot",
        0.5,
    )[0]


def middle_back(grads, middle, cotangents, gain, bias, w_out):
    dim = middle.shape[1]
    width = w_out.shape[0]

    def body(*refs):
        grad_ref, third_ref, fourth_ref, middle_ref, *cot_refs = refs[:8]
        gain_ref, bias_ref, out_ref, branch_ref, own_ref, attended_ref, gain_sum, bias_sum = refs[8:]
        step = pl.program_id(0)
        grad = jnp.where(step == 2, third_ref[...], fourth_ref[...])
        grad = jnp.where(step < 2, grad_ref[...], grad).astype(F32)
        _, hat, inv = normalize(middle_ref[...], gain_ref[...], bias_ref[...])
        weighted = grad * gain_ref[...]
        moved = grad * hat
        first_mean = jnp.mean(weighted, axis=-1, keepdims=True)
        second_mean = jnp.mean(weighted * hat, axis=-1, keepdims=True)
        value = stacked_rows(cot_refs, cotangents).astype(F32) + inv * (
            weighted - first_mean - hat * second_mean
        )
        low = value.astype(BF16)
        branch_ref[...] = low
        attended_ref[...] = contract_cols(low, out_ref[...]).astype(BF16)
        add_up(gain_sum, moved)
        add_up(bias_sum, grad)

        @pl.when(pl.program_id(0) == 0)
        def _():
            own_ref[...] = value

    count = 4 * ROW_BLOCK
    return call(
        body,
        4,
        [(grads[0], by_rows(dim, low_half))]
        + [(grad, whole(grad)) for grad in grads[1:]]
        + [(middle, by_rows(dim))]
        + stacked(cotangents)
        + [(gain, whole(gain)), (bias, whole(bias)), (w_out, whole(w_out))],
        [
            ((count, dim), BF16, by_rows(dim)),
            ((ROW_BLOCK, dim), F32, by_rows(dim, lambda i: 0)),
            ((count, width), BF16, by_rows(width)),
            sum_output(dim),
            sum_output(dim),
        ],
        "middle_back",
        0.5,
    )


def norm_back(near, far, rows, gain, bias, added=None):
    dim = rows.shape[1]
    extra = [] if added is None else [(added, by_rows(dim))]

    def body(*refs):
        near_ref, far_ref, rows_ref, gain_ref, bias_ref = refs[:5]
        out_ref, gain_sum, bias_sum = refs[-3:]
        grad = near_ref[...].astype(F32) + far_ref[...].astype(F32)
        _, hat, inv = normalize(rows_ref[...].astype(F32), gain_ref[...], bias_ref[...])
        weighted = grad * gain_ref[...]
        first_mean = jnp.mean(weighted, axis=-1, keepdims=True)
        second_mean = jnp.mean(weighted * hat, axis=-1, keepdims=True)
        value = inv * (weighted - first_mean - hat * second_mean)
        if extra:
            value = refs[5][...] + value
        out_ref[...] = value.astype(BF16)
        add_up(gain_sum, grad * hat)
        add_up(bias_sum, grad)

    return call(
        body,
        rows.shape[0] // ROW_BLOCK,
        [(near, by_rows(dim)), (far, by_rows(dim)), (rows, by_rows(dim))]
        + [(gain, whole(gain)), (bias, whole(bias))]
        + extra,
        [(rows.shape, BF16, by_rows(dim)), sum_output(dim), sum_output(dim)],
        "norm_back",
        0.5,
    )


def swap_head(value, bit):
    size = lax.axis_size("head")
    return lax.ppermute(value, "head", [(i, i ^ bit) for i in range(size)])


def swap_seq(value, bit):
    size = lax.axis_size("seq")
    return lax.ppermute(value, "seq", [(i, i ^ bit) for i in range(size)])


def sum_seq(value):
    size = lax.axis_size("seq")
    bit = 1
    while bit < size:
        value = value + swap_seq(value, bit)
        bit *= 2
    return value


def sum_head(value):
    size = lax.axis_size("head")
    bit = 1
    while bit < size:
        value = value + swap_head(value, bit)
        bit *= 2
    return value


OVER_Z = (False, False, True, False)


class Values:
    pass


class Order:
    def __init__(self):
        self.last = None

    def __call__(self, step, *values):
        if self.last is not None:
            *values, _ = lax.optimization_barrier((*values, self.last))
        out = step(*values)
        self.last = tuple(out) if isinstance(out, (tuple, list)) else out
        return out

    def gate(self, value):
        return lax.optimization_barrier((value, self.last))[0]

    def pin(self, value):
        self.last = self.gate(value)
        return self.last


class SeqSum:
    def __init__(self, order, halves, over_z):
        other, self.mine = halves
        self.order = order
        self.over_z = over_z
        self.moving = swap_seq(other, 1)

    def split(self):
        odd = lax.axis_index("seq") // 2 % 2
        quarter = self.mine.shape[0] // 2

        def run(mine, moving):
            total = mine + moving
            return [
                lax.dynamic_slice_in_dim(total, which * quarter, quarter, axis=0)
                for which in (1 - odd, odd)
            ]

        other, self.mine = self.order(run, self.mine, self.moving)
        self.moving = swap_seq(other, 2)

    def across(self):
        self.mine = self.order(lambda v, r: v + r, self.mine, self.moving)
        self.moving = swap_seq(self.mine, 4)

    def spread(self):
        self.mine = self.order(lambda v, r: v + r, self.mine, self.moving)
        self.side = swap_seq(self.mine, 1)
        self.pair = swap_seq(self.mine, 2)

    def corner(self):
        if self.over_z:
            self.side = self.order.pin(self.side)
            self.last = swap_seq(self.side, 2)
        else:
            self.pair = self.order.pin(self.pair)
            self.last = swap_seq(self.pair, 1)

    def pieces(self):
        return [self.mine, self.pair, self.side, self.last]


def blocks(value, count):
    size = value.shape[0] // count
    return [value[i * size : (i + 1) * size] for i in range(count)]


def shards_quad(
    media,
    media_ids,
    image_seq,
    image_valid,
    latents,
    w_query,
    w_key,
    w_value,
    w_out,
    w_up,
    w_down,
    media_gain,
    media_bias,
    latent_gain,
    latent_bias,
    ffn_gain,
    ffn_bias,
    cotangent,
):
    seq_index = lax.axis_index("seq")
    head_index = lax.axis_index("head")
    seq_size = lax.axis_size("seq")
    images = image_seq.shape[0]
    sequences = media_ids.shape[0] // LEN
    own_rows = latents.shape[0]
    width = w_query.shape[1]
    dim = media.shape[1]
    order = Order()
    media_gain, media_bias, latent_gain, latent_bias, ffn_gain, ffn_bias = (
        value.reshape(1, dim)
        for value in (media_gain, media_bias, latent_gain, latent_bias, ffn_gain, ffn_bias)
    )

    slots = jnp.array([0, 2, 1, 3], jnp.int32)
    per_device = images // 4
    which = ((slots ^ head_index)[:, None] * per_device + jnp.arange(per_device)[None, :]).reshape(-1)
    owners = seq_index * images + which
    local_seq = jnp.take(image_seq, which) - seq_index * sequences
    valid_float = jnp.take(image_valid, which).astype(F32)
    matches = media_ids[None, :] == owners[:, None]
    place = jnp.arange(media_ids.shape[0], dtype=jnp.int32)[None, :]
    run = jnp.sum(matches.astype(jnp.int32), axis=1)
    start = jnp.min(jnp.where(matches, place, media_ids.shape[0]), axis=1)
    low = jnp.where(run > 0, start - local_seq * LEN, 0)
    high = low + run
    slot = local_seq ^ head_index

    share = width // seq_size
    raw_across = swap_head(media, 2)
    out_piece = lax.dynamic_slice_in_dim(w_out, seq_index * share, share, axis=0)
    out_piece = swap_head(out_piece, 2)
    raw_near = swap_head(media, 1)
    latents_near = swap_head(latents, 1)
    out_near = swap_head(w_out, 1)

    cotangent_near = swap_head(cotangent, 1)
    w_kv = jnp.concatenate([w_key, w_value], axis=1)
    w_qkv = jnp.concatenate([w_query, w_kv], axis=1)

    def media_step(rows, weights):
        return norm_project([rows], media_gain, media_bias, weights, 0.3, LEN)

    def stack(*values):
        return jnp.concatenate(values, axis=0)

    def add(left, right):
        return left + right

    def latent_step(own, other, weights):
        return norm_project([own, other], latent_gain, latent_bias, weights, 0.3)

    def forward(lists, kv_slots, latent_qkv, offset, before):
        count = len(kv_slots)
        return order(
            lambda *v: attention_forward(
                *v[:4], v[4 : 4 + count], v[4 + count], offset, v[5 + count :] or None, time=1.0
            ),
            lists,
            slot,
            low,
            high,
            *kv_slots,
            latent_qkv,
            *before,
        )

    count = order(
        lambda v: jnp.broadcast_to(jnp.sum(v).reshape(1, 1), (8, 128)), valid_float
    )
    count_moved = swap_seq(count, 1)
    kv_own, norm_own = order(media_step, media, w_kv)
    count = order(add, count, count_moved)
    count_moved = swap_seq(count, 2)
    latents_across = swap_head(order.gate(latents), 2)
    early_qkv, early_low = order(latent_step, latents, latents_near, w_qkv)
    count = order(add, count, count_moved)
    count_moved = swap_seq(count, 4)
    early = jnp.arange(images) // per_device % 2 == 0
    near_list, rest_list, full_list = order(
        lambda s, a, b: (
            list_images(early & (s < 2), a, b),
            list_images(jnp.logical_not(early & (s < 2)), a, b),
            list_images(s >= 0, a, b),
        ),
        slot,
        low,
        high,
    )
    kv_near, norm_near = order(media_step, raw_near, w_kv)
    outcome = forward(near_list, (kv_own, kv_near), early_qkv, 0, ())
    cotangent_across = swap_head(order.gate(cotangent), 2)
    out_first = order(stack, w_out, out_near)
    count = order(add, count, count_moved)
    penalty_weight, pen_scale = order(
        lambda v, c: (v * (4.0 * images * seq_size / c[0, 0]), 1.0 / (HEADS * LATENTS * c[0, 0])),
        valid_float,
        count,
    )
    raw_across = order.pin(raw_across)
    raw_beyond = swap_head(raw_across, 1)
    kv_across, norm_across = order(media_step, raw_across, w_kv)
    kv_beyond, norm_beyond = order(media_step, raw_beyond, w_kv)
    out_piece = order.pin(out_piece)
    out_far = lax.all_gather(out_piece, "seq", axis=0, tiled=True)
    kv_far = (kv_across, kv_beyond)
    latents_across = order.pin(latents_across)
    latents_beyond = swap_head(latents_across, 1)
    late_qkv, late_low = order(latent_step, latents_across, latents_beyond, w_qkv)

    def interleave(first, second):
        first, second = blocks(first, 2), blocks(second, 2)
        return stack(first[0], second[0], first[1], second[1])

    latent_qkv = order(interleave, early_qkv, late_qkv)
    attended, lse, entropy = forward(
        rest_list, (kv_own, kv_near, *kv_far), latent_qkv, 0, outcome
    )
    attended_across = swap_head(attended, 2)
    attended_near = swap_head(attended, 1)
    cotangent_across = order.pin(cotangent_across)
    cotangent_beyond = swap_head(cotangent_across, 1)
    cotangents = (cotangent, cotangent_across, cotangent_near, cotangent_beyond)
    pulled = order(lambda *v: cotangent_down(v[:4], v[4]), *cotangents, w_down)
    out_far = order.pin(out_far)
    out_beyond = swap_head(out_far, 1)
    attended_across = order.gate(attended_across)
    attended_beyond = swap_head(attended_across, 1)
    middle, ffn_low, hidden, grad_before, lower, upper = order(
        lambda *v: feed_forward(v[:4], v[4], v[5:7], v[7:11], *v[11:], ffn_gain, ffn_bias),
        attended,
        attended_near,
        attended_across,
        attended_beyond,
        out_first,
        out_far,
        out_beyond,
        latents,
        latents_across,
        latents_near,
        latents_beyond,
        pulled,
        w_up,
    )
    side = (seq_index % 2).reshape(1)
    place = (seq_index % 2 * 2 + seq_index // 2 % 2).reshape(1)
    v = Values()
    v.upper = swap_head(upper, 1)

    def lowadd():
        v.lower = order(add, lower, v.upper)
        v.Y = swap_head(v.lower, 2)

    def sum_steps(grads, over_z):
        made = []

        def start():
            made.append(SeqSum(order, grads(), over_z))

        return (
            start,
            lambda: made[0].split(),
            lambda: made[0].across(),
            lambda: made[0].spread(),
            lambda: made[0].corner(),
            lambda: made[0].pieces(),
        )

    def down_grads():
        return order(
            lambda x, h, *g: grad_halves(x, [(h, [part(one) for one in g])], "down_grad"),
            side,
            hidden,
            *cotangents,
        )

    def up_grads():
        return order(
            lambda x, h, g: grad_halves(x, [(h, [part(g)])], "up_grad"),
            side,
            ffn_low,
            grad_before,
        )

    norms = (norm_own, norm_near, norm_across, norm_beyond)

    def key_pairs(
        x, own, near, across, beyond, back, early_rows, late_rows, latent_part
    ):
        pairs = [
            (rows, [part(back, LEN, i)]) for i, rows in enumerate((own, near, across, beyond))
        ]
        for rows, at in ((early_rows, 0), (late_rows, 1)):
            pairs.append(
                (
                    rows,
                    [
                        part(latent_part, own_rows, at + 2 * i, slice(width, None))
                        for i in range(2)
                    ],
                )
            )
        return grad_halves(x, pairs, "key_grad")

    def key_grads():
        return order(
            key_pairs, side, *norms, v.kv_back, early_low, late_low, v.latent_back
        )

    d, d_1, d_2, d_3, d_4, down_parts = sum_steps(down_grads, OVER_Z[0])
    u, u_1, u_2, u_3, u_4, up_parts = sum_steps(up_grads, OVER_Z[1])
    k, k_1, k_2, k_3, k_4, key_parts = sum_steps(key_grads, OVER_Z[2])
    l, l_1, l_2, l_3, l_4, late_parts = sum_steps(
        lambda: order(
            late_grads, side, v.latent_back, early_low, late_low, attended, v.grad_branch
        ),
        OVER_Z[3],
    )

    def branch():
        v.branch, v.branch_upper = order(
            lambda h, w: project_halves(h, w, False, "branch"), hidden, w_down
        )
        v.BC = swap_head(v.branch_upper, 1)

    def bradd():
        v.branch = order(add, v.branch, v.BC)
        v.BY = swap_head(v.branch[own_rows:], 2)

    def res():
        v.result = order(
            lambda m, b, r: (m[:own_rows] + b[:own_rows].astype(F32) + r.astype(F32)).astype(BF16),
            middle,
            v.branch,
            v.BY,
        )

    def gpair():
        v.pair = order(
            lambda a, r: a + jnp.concatenate(blocks(r, 2)[::-1], axis=0), v.lower, v.Y
        )
        v.G = [swap_head(piece, 1) for piece in blocks(v.pair, 2)]

    def mback():
        out = order(
            lambda *a: middle_back(a[:3], a[3], a[4:8], ffn_gain, ffn_bias, a[8]),
            v.pair,
            *v.G,
            middle,
            *cotangents,
            w_out,
        )
        v.grad_branch, v.grad_middle, v.grad_attended = out[:3]
        v.ffn_sums = out[3:]

    def attb():
        v.latent_back, v.kv_back = order(
            lambda *a: attention_backward(*a[:5], a[5:9], *a[9:]),
            full_list,
            slot,
            low,
            high,
            penalty_weight,
            kv_own,
            kv_near,
            *kv_far,
            latent_qkv,
            v.grad_attended,
            lse,
            entropy,
        )

    def swap_pieces(value):
        return [swap_head(piece, 1) for piece in blocks(value, 2)]

    def pb():
        v.K1 = swap_pieces(order(lambda a, w: project_slot(a, 3, w), v.kv_back, w_kv))

    def pa():
        v.MF = swap_head(
            order(lambda a, w, *r: project_slot(a, 2, w, r), v.kv_back, w_kv, *v.K1), 2
        )

    def pn():
        v.K2 = swap_pieces(order(lambda a, w: project_slot(a, 1, w), v.kv_back, w_kv))

    def po():
        v.media_near = order(
            lambda a, w, *r: project_slot(a, 0, w, r), v.kv_back, w_kv, *v.K2
        )

    def lb():
        v.latent_lower, upper = order(
            lambda a, w: project_halves(a, w, True, "latent_back"), v.latent_back, w_qkv
        )
        v.LC = swap_head(upper, 1)

    def ladd():
        v.latent_lower = order(add, v.latent_lower, v.LC)
        v.LY = swap_head(v.latent_lower[own_rows:], 2)

    def nbm():
        v.media_grad, *v.media_sums = order(
            lambda *a: norm_back(*a, media_gain, media_bias), v.media_near, v.MF, media
        )

    def nbl():
        v.latents_grad, *v.latent_sums = order(
            lambda *a: norm_back(*a[:3], latent_gain, latent_bias, a[3]),
            v.latent_lower,
            v.LY,
            latents,
            v.grad_middle,
        )

    def s0():
        entropy_local = jnp.sum(entropy.reshape(images, -1) * valid_float[:, None])
        part_of = 1.0 / lax.axis_size("head")
        v.sums = order(
            stack,
            *v.media_sums,
            *v.latent_sums,
            *[value * part_of for value in v.ffn_sums],
            jnp.broadcast_to(entropy_local, (2, dim)),
        )
        v.moved = swap_head(v.sums, 1)

    def add_moved():
        v.sums = order(add, v.sums, v.moved)

    def s1():
        add_moved()
        v.moved = swap_head(v.sums, 2)

    def s2():
        add_moved()
        v.moved = swap_seq(v.sums, 1)

    def s3():
        add_moved()
        v.moved = swap_seq(v.sums, 2)

    def s4():
        add_moved()
        v.moved = swap_seq(v.sums, 4)

    s5 = add_moved

    def d_5():
        parts = down_parts()
        v.down = order(lambda p, *a: join_rows(p, a, ((0, dim),))[0], place, *parts)

    def u_5():
        parts = up_parts()
        v.up = order(lambda p, *a: join_rows(p, a, ((0, dim),))[0], place, *parts)

    def k_5():
        parts = key_parts()
        v.key, v.value = order(
            lambda p, *a: join_rows(p, a, ((0, width), (width, 2 * width))), place, *parts
        )

    def l_5():
        v.query, v.out = order(lambda p, *a: join_late(p, a), place, *late_parts())

    steps = (
        d, lowadd, u, gpair, mback, d_1, attb, d_2, lb, pb, u_1, l, k, d_3, u_2, l_1, ladd,
        pa, k_1, d_4, branch, nbl, pn, u_3, l_2, d_5, k_2, bradd, po, u_4, nbm, s0, l_3, s1,
        k_3, s2, u_5, l_4, s3, k_4, k_5, s4, res, l_5, s5,
    )
    for step in steps:
        step()
    sums = v.sums
    return (
        v.result,
        sums[6, 0] * pen_scale,
        v.media_grad,
        v.latents_grad,
        v.query,
        v.key,
        v.value,
        v.out,
        v.up,
        v.down,
        sums[0],
        sums[1],
        sums[2],
        sums[3],
        sums[4],
        sums[5],
    )


def shards_any(
    media,
    media_ids,
    image_seq,
    image_valid,
    latents,
    w_query,
    w_key,
    w_value,
    w_out,
    w_up,
    w_down,
    media_gain,
    media_bias,
    latent_gain,
    latent_bias,
    ffn_gain,
    ffn_bias,
    cotangent,
):
    seq_index = lax.axis_index("seq")
    head_index = lax.axis_index("head")
    images = image_seq.shape[0]
    sequences = media_ids.shape[0] // LEN
    own_rows = latents.shape[0]
    inner_width = w_query.shape[1]
    seq_size = lax.axis_size("seq")
    valid_float = image_valid.astype(F32)

    media_norm, media_hat, media_inv = normalize(media.astype(F32), media_gain, media_bias)
    latent_rows = lax.all_gather(latents, "head", axis=0, tiled=True)
    media_all = lax.all_gather(media_norm.astype(BF16), "head", axis=0, tiled=True)
    grad_all = lax.all_gather(cotangent, "head", axis=0, tiled=True)
    latent_float = latent_rows.astype(F32)
    latent_norm, latent_hat, latent_inv = normalize(latent_float, latent_gain, latent_bias)
    latent_low = latent_norm.astype(BF16)

    count_all = jnp.sum(valid_float).reshape(1, 1)
    count_all = sum_seq(jnp.broadcast_to(count_all, (8, 128)))[0, 0]
    pen_scale = 1.0 / (HEADS * LATENTS * count_all)
    weighted_scale = 4.0 * images * seq_size / count_all

    owners = seq_index * images + jnp.arange(images, dtype=jnp.int32)
    local_seq = image_seq - seq_index * sequences
    matches = media_ids[None, :] == owners[:, None]
    place = jnp.arange(media_ids.shape[0], dtype=jnp.int32)[None, :]
    run = jnp.sum(matches.astype(jnp.int32), axis=1)
    start = jnp.min(jnp.where(matches, place, media_ids.shape[0]), axis=1)
    low = jnp.where(run > 0, start - local_seq * LEN, 0)
    high = low + run
    slot = local_seq
    listed = list_images(jnp.full((images,), True), low, high)

    w_kv = jnp.concatenate([w_key, w_value], axis=1)
    w_qkv = jnp.concatenate([w_query, w_kv], axis=1)
    latent_qkv = product(latent_low, w_qkv).astype(BF16)
    kv_slots = [product(media_all, w_kv).astype(BF16)]
    attended, lse, entropy = attention_forward(listed, slot, low, high, kv_slots, latent_qkv)

    branch = lax.psum(product(attended, w_out).astype(BF16), "head").astype(F32)
    middle = latent_float + branch
    ffn_norm, ffn_hat, ffn_inv = normalize(middle, ffn_gain, ffn_bias)
    ffn_low = ffn_norm.astype(BF16)
    before_gelu = product(ffn_low, w_up)
    activated, gelu_slope = gelu_parts(before_gelu)
    hidden = activated.astype(BF16)
    grad_before = (contract_cols(grad_all, w_down) * gelu_slope).astype(BF16)
    grad_ffn_part = contract_cols(grad_before, w_up).astype(BF16)
    grad_ffn = lax.psum(grad_ffn_part, "head").astype(F32)
    down_grad = contract_rows(hidden, grad_all).astype(BF16)
    up_grad = contract_rows(ffn_low, grad_before).astype(BF16)
    up_grad, down_grad = lax.psum((up_grad, down_grad), "seq")

    ffn_branch = product(hidden, w_down).astype(BF16)
    ffn_branch = lax.psum_scatter(ffn_branch, "head", scatter_dimension=0, tiled=True)

    def own(value):
        return lax.dynamic_slice_in_dim(value, head_index * own_rows, own_rows, axis=0)

    result = (own(middle) + ffn_branch.astype(F32)).astype(BF16)

    middle_part, ffn_gain_part, ffn_bias_part = normalize_back(
        grad_ffn, ffn_hat, ffn_inv, ffn_gain
    )
    grad_middle = grad_all.astype(F32) + middle_part
    grad_branch = grad_middle.astype(BF16)
    grad_attended = contract_cols(grad_branch, w_out).astype(BF16)
    out_grad = contract_rows(attended, grad_branch)
    back = attention_backward(
        listed,
        slot,
        low,
        high,
        valid_float * weighted_scale,
        kv_slots,
        latent_qkv,
        grad_attended,
        lse,
        entropy,
    )
    latent_back, kv_back = back
    grad_media_norm = lax.psum_scatter(
        contract_cols(kv_back, w_kv).astype(BF16), "head", scatter_dimension=0, tiled=True
    ).astype(F32)
    grad_latent_part = contract_cols(latent_back, w_qkv).astype(BF16)
    grad_latent_norm = lax.psum_scatter(
        grad_latent_part, "head", scatter_dimension=0, tiled=True
    ).astype(F32)
    latent_grads = contract_rows(latent_low, latent_back)
    kv_grads = latent_grads[:, inner_width:] + contract_rows(media_all, kv_back)
    late = (
        latent_grads[:, :inner_width].astype(BF16),
        kv_grads.astype(BF16),
        out_grad.astype(BF16),
    )
    up_grad, down_grad, *late = lax.optimization_barrier((up_grad, down_grad) + late)
    query_grad, kv_grads, out_grad = lax.psum(tuple(late), "seq")

    media_rows_grad, media_gain_part, media_bias_part = normalize_back(
        grad_media_norm, media_hat, media_inv, media_gain
    )
    latent_part, latent_gain_part, latent_bias_part = normalize_back(
        grad_latent_norm, own(latent_hat), own(latent_inv), latent_gain
    )
    latents_grad = (own(grad_middle) + latent_part).astype(BF16)
    entropy_local = jnp.sum(entropy.reshape(images, -1) * valid_float[:, None])
    share = 1.0 / lax.axis_size("head")
    sums = jnp.stack(
        [
            media_gain_part,
            media_bias_part,
            latent_gain_part,
            latent_bias_part,
            ffn_gain_part * share,
            ffn_bias_part * share,
            jnp.broadcast_to(entropy_local, media_gain.shape),
            jnp.zeros_like(media_gain),
        ]
    )
    sums = sum_seq(sum_head(sums))
    return (
        result,
        sums[6, 0] * pen_scale,
        media_rows_grad.astype(BF16),
        latents_grad,
        query_grad.astype(F32),
        kv_grads[:, :inner_width].astype(F32),
        kv_grads[:, inner_width:].astype(F32),
        out_grad.astype(F32),
        up_grad.astype(F32),
        down_grad.astype(F32),
        sums[0],
        sums[1],
        sums[2],
        sums[3],
        sums[4],
        sums[5],
    )


def solution(mesh):
    rows = P(("seq", "head"), None)
    columns = P(None, "head")
    lines = P("head", None)
    quad = mesh.shape["head"] == 4 and mesh.shape["seq"] == 8
    return jax.shard_map(
        shards_quad if quad else shards_any,
        mesh=mesh,
        in_specs=(
            (rows, P("seq"), P("seq"), P("seq"), rows)
            + (columns, columns, columns, lines, columns, lines)
            + (P(),) * 6
            + (rows,)
        ),
        out_specs=(
            (rows, P(), rows, rows)
            + (columns, columns, columns, lines, columns, lines)
            + (P(),) * 6
        ),
        check_vma=False,
    )
```

```python
import jax
import jax.numpy as jnp
from jax import lax
from jax.experimental import pallas as pl
from jax.experimental.pallas import tpu as pltpu
from jax.sharding import PartitionSpec as P

HEADS = 16
HEAD_DIM = 96
LATENTS = 64
LEN = 1024
KEY_BLOCK = 256

epsilon = 1e-05
BF16 = jnp.bfloat16


def cost(microseconds):
    return pl.CostEstimate(
        flops=int(microseconds * 1.1e9), transcendentals=0, bytes_accessed=int(microseconds * 3e6)
    )


F32 = jnp.float32


def normalize(row_values, norm_gain, norm_bias):
    row_mean = jnp.mean(row_values, axis=-1, keepdims=True)
    centred = row_values - row_mean
    variance = jnp.mean(centred * centred, axis=-1, keepdims=True)
    inverse = lax.rsqrt(variance + epsilon)
    scaled = centred * inverse
    return (scaled * norm_gain + norm_bias, scaled, inverse)


def normalize_back(incoming, scaled, inverse, norm_gain):
    weighted = incoming * norm_gain
    first_mean = jnp.mean(weighted, axis=-1, keepdims=True)
    second_mean = jnp.mean(weighted * scaled, axis=-1, keepdims=True)
    outgoing = inverse * (weighted - first_mean - scaled * second_mean)
    return (outgoing, jnp.sum(incoming * scaled, axis=0), jnp.sum(incoming, axis=0))


def product(left_side, right_side):
    return jnp.dot(left_side, right_side, preferred_element_type=F32)


def contract_rows(left_side, right_side):
    return lax.dot_general(
        left_side, right_side, (((0,), (0,)), ((), ())), preferred_element_type=F32
    )


def contract_cols(left_side, right_side):
    return lax.dot_general(
        left_side, right_side, (((1,), (1,)), ((), ())), preferred_element_type=F32
    )


def gelu_parts(inputs):
    normal_cdf = 0.5 * (1.0 + lax.erf(inputs * 0.7071067811865476))
    density = jnp.exp(-0.5 * inputs * inputs) * 0.3989422804014327
    return (inputs * normal_cdf, normal_cdf + inputs * density)


def block_diagonal(rows, heads):
    lane = lax.broadcasted_iota(jnp.int32, rows.shape, 1)
    parts = []
    for head in range(heads):
        inside = (lane >= head * HEAD_DIM) & (lane < (head + 1) * HEAD_DIM)
        parts.append(jnp.where(inside, rows, jnp.zeros_like(rows)))
    return jnp.concatenate(parts, axis=0)


def take_diagonal(wide, heads):
    lane = lax.broadcasted_iota(jnp.int32, (LATENTS, wide.shape[1]), 1)
    out = wide[:LATENTS]
    for head in range(1, heads):
        out = jnp.where(lane >= head * HEAD_DIM, wide[head * LATENTS : (head + 1) * LATENTS], out)
    return out


def start_loads(kv_hbm, kv_vmem, sems):
    copies = []
    at = 0
    for i, ref in enumerate(kv_hbm):
        size = ref.shape[0]
        copies.append(pltpu.make_async_copy(ref, kv_vmem.at[pl.ds(at, size), :], sems.at[i]))
        at += size
    for copy in copies:
        copy.start()
    return copies


WINDOWS = (256, 512)


def image_rows(image):
    return pl.ds(pl.multiple_of(image * LATENTS, LATENTS), LATENTS)


def window_start(lo, size):
    return jnp.minimum(lo // 16 * 16, LEN - size)


def list_images(here, low, high):
    images = here.shape[0]
    kind = len(WINDOWS) - sum(
        (high - window_start(low, size) <= size).astype(jnp.int32) for size in WINDOWS
    )
    kind = jnp.where(here, kind, len(WINDOWS) + 1)
    number = jnp.arange(images, dtype=jnp.int32)
    key = kind * images + number
    rank = jnp.sum((key[None, :] < key[:, None]).astype(jnp.int32), axis=1)
    listed = jnp.sum(jnp.where(rank[None, :] == number[:, None], number[None, :], 0), axis=1)
    ends = [jnp.sum((kind <= i).astype(jnp.int32)).reshape(1) for i in range(len(WINDOWS) + 1)]
    return jnp.concatenate([listed, *ends])


def each_image(listed_ref, images, short, long):
    begin = 0
    for i, size in enumerate(WINDOWS):
        end = listed_ref[images + i]

        def pair(index, _, size=size, begin=begin, end=end):
            at = begin + 2 * index
            short(size, [listed_ref[at], listed_ref[jnp.minimum(at + 1, end - 1)]])
            return 0

        lax.fori_loop(0, (end - begin + 1) // 2, pair, 0)
        begin = end

    def single(index, _):
        long(listed_ref[index])
        return 0

    lax.fori_loop(begin, listed_ref[images + len(WINDOWS)], single, 0)


def attention_forward(
    listed, slot, low, high, kv_slots, latent_qkv, offset=0, before=None, time=15.0
):
    images = slot.shape[0]
    count = len(kv_slots)
    keys = sum(kv.shape[0] for kv in kv_slots)
    width = latent_qkv.shape[1] // 3
    heads = width // HEAD_DIM
    rows = heads * LATENTS
    scale = HEAD_DIM ** (-0.5)
    given = () if before is None else tuple(before)
    whole_rows = latent_qkv.shape[0] == images * LATENTS

    def source_rows(image):
        return image_rows(image if whole_rows else image // 8 * 4 + image % 4)


    def body(listed_ref, slot_ref, low_ref, high_ref, *refs):
        kv_hbm = refs[:count]
        qkv_ref = refs[count]
        given_refs = refs[count + 1 : count + 1 + len(given)]
        out_ref, lse_ref, ent_ref, kv_vmem, scores, sems = refs[count + 1 + len(given) :]
        copies = start_loads(kv_hbm, kv_vmem, sems)
        if given:
            out_ref[...] = given_refs[0][...]
            lse_ref[...] = given_refs[1][...]
            ent_ref[...] = given_refs[2][...]
        for copy in copies:
            copy.wait()

        def short(size, pair):
            for image in pair:
                at = source_rows(image)
                lo = low_ref[image]
                hi = high_ref[image]
                start = window_start(lo, size)
                place = pl.multiple_of((slot_ref[image] - offset) * LEN + start, 16)
                query = block_diagonal(qkv_ref[at, :width], heads)
                own = contract_cols(qkv_ref[at, width : 2 * width], query) * scale
                part = contract_cols(kv_vmem[pl.ds(place, size), :width], query) * scale
                key = start + lax.broadcasted_iota(jnp.int32, part.shape, 0)
                part = jnp.where((key >= lo) & (key < hi), part, -1e30)
                peak = jnp.maximum(
                    jnp.max(own, axis=0, keepdims=True), jnp.max(part, axis=0, keepdims=True)
                )
                own = own - peak
                part = part - peak
                own_exp = jnp.exp(own)
                part_exp = jnp.exp(part)
                total = jnp.sum(own_exp, axis=0, keepdims=True) + jnp.sum(
                    part_exp, axis=0, keepdims=True
                )
                moment = jnp.sum(own_exp * own, axis=0, keepdims=True) + jnp.sum(
                    part_exp * part, axis=0, keepdims=True
                )
                inverse = 1.0 / total
                log_total = jnp.log(total)
                lse_ref[image] = peak + log_total
                ent_ref[image] = log_total - moment * inverse
                wide = contract_rows((own_exp * inverse).astype(BF16), qkv_ref[at, 2 * width :])
                wide = wide + contract_rows(
                    (part_exp * inverse).astype(BF16), kv_vmem[pl.ds(place, size), width:]
                )
                out_ref[image_rows(image), :] = take_diagonal(wide, heads).astype(BF16)

        def long(image):
            at = source_rows(image)
            base = (slot_ref[image] - offset) * LEN
            lo = low_ref[image]
            hi = high_ref[image]
            first = lo // KEY_BLOCK
            last = (hi + KEY_BLOCK - 1) // KEY_BLOCK
            query = block_diagonal(qkv_ref[at, :width], heads)
            own = contract_cols(qkv_ref[at, width : 2 * width], query) * scale
            peak = jnp.max(own, axis=0, keepdims=True)

            def first_pass(block, peak):
                row = pl.multiple_of(base + block * KEY_BLOCK, KEY_BLOCK)
                part = contract_cols(kv_vmem[pl.ds(row, KEY_BLOCK), :width], query) * scale
                key = block * KEY_BLOCK + lax.broadcasted_iota(jnp.int32, part.shape, 0)
                part = jnp.where((key >= lo) & (key < hi), part, -1e30)
                to = pl.multiple_of((block - first) * KEY_BLOCK, KEY_BLOCK)
                scores[pl.ds(to, KEY_BLOCK), :] = part
                return jnp.maximum(peak, jnp.max(part, axis=0, keepdims=True))

            peak = lax.fori_loop(first, last, first_pass, peak)
            own = own - peak
            own_exp = jnp.exp(own)
            total = jnp.sum(own_exp, axis=0, keepdims=True)
            moment = jnp.sum(own_exp * own, axis=0, keepdims=True)

            def second_pass(block, carry):
                total, moment = carry
                to = pl.multiple_of((block - first) * KEY_BLOCK, KEY_BLOCK)
                part = scores[pl.ds(to, KEY_BLOCK), :] - peak
                part_exp = jnp.exp(part)
                scores[pl.ds(to, KEY_BLOCK), :] = part_exp
                return (
                    total + jnp.sum(part_exp, axis=0, keepdims=True),
                    moment + jnp.sum(part_exp * part, axis=0, keepdims=True),
                )

            total, moment = lax.fori_loop(first, last, second_pass, (total, moment))
            inverse = 1.0 / total
            log_total = jnp.log(total)
            lse_ref[image] = peak + log_total
            ent_ref[image] = log_total - moment * inverse
            wide = contract_rows((own_exp * inverse).astype(BF16), qkv_ref[at, 2 * width :])

            def third_pass(block, wide):
                to = pl.multiple_of((block - first) * KEY_BLOCK, KEY_BLOCK)
                row = pl.multiple_of(base + block * KEY_BLOCK, KEY_BLOCK)
                low_prob = (scores[pl.ds(to, KEY_BLOCK), :] * inverse).astype(BF16)
                return wide + contract_rows(low_prob, kv_vmem[pl.ds(row, KEY_BLOCK), width:])

            wide = lax.fori_loop(first, last, third_pass, wide)
            out_ref[image_rows(image), :] = take_diagonal(wide, heads).astype(BF16)

        each_image(listed_ref, images, short, long)

    shapes = (
        jax.ShapeDtypeStruct((images * LATENTS, width), BF16),
        jax.ShapeDtypeStruct((images, 1, rows), F32),
        jax.ShapeDtypeStruct((images, 1, rows), F32),
    )
    scalar = pl.BlockSpec(memory_space=pltpu.SMEM)
    vmem = pl.BlockSpec(memory_space=pltpu.VMEM)
    return pl.pallas_call(
        body,
        out_shape=shapes,
        in_specs=[scalar] * 4
        + [pl.BlockSpec(memory_space=pl.ANY)] * count
        + [vmem] * (1 + len(given)),
        out_specs=(vmem,) * 3,
        scratch_shapes=[
            pltpu.VMEM((keys, 2 * width), BF16),
            pltpu.VMEM((LEN, rows), F32),
            pltpu.SemaphoreType.DMA((count,)),
        ],
        compiler_params=pltpu.CompilerParams(vmem_limit_bytes=48 << 20),
        cost_estimate=cost(time),
        name="attention_forward",
    )(listed, slot, low, high, *kv_slots, latent_qkv, *given)


def attention_backward(
    listed, slot, low, high, weight, kv_slots, latent_qkv, grad_out, lse, entropy
):
    images = slot.shape[0]
    count = len(kv_slots)
    keys = sum(kv.shape[0] for kv in kv_slots)
    width = latent_qkv.shape[1] // 3
    heads = width // HEAD_DIM
    rows = heads * LATENTS
    scale = HEAD_DIM ** (-0.5)

    def body(listed_ref, slot_ref, low_ref, high_ref, weight_ref, *refs):
        kv_hbm = refs[:count]
        qkv_ref, grad_ref, lse_ref, ent_ref = refs[count : count + 4]
        own_out, key_out, kv_vmem, probs, slopes, totals, sems = refs[count + 4 :]
        copies = start_loads(kv_hbm, kv_vmem, sems)
        totals[...] = jnp.zeros_like(totals)
        for copy in copies:
            copy.wait()

        def short(size, pair):
            for which, image in enumerate(pair):
                repeated = jnp.logical_and(which == 1, pair[0] == image)
                at = image_rows(image)
                lo = low_ref[image]
                hi = high_ref[image]
                pull = weight_ref[image]
                start = window_start(lo, size)
                place = pl.multiple_of(slot_ref[image] * LEN + start, 16)
                window = pl.ds(place, size)
                query = block_diagonal(qkv_ref[at, :width], heads)
                grad = block_diagonal(grad_ref[at, :], heads)
                log_total = lse_ref[image]
                ent = ent_ref[image]
                own_key = qkv_ref[at, width : 2 * width]
                own_log = contract_cols(own_key, query) * scale - log_total
                own_prob = jnp.exp(own_log)
                own_slope = contract_cols(qkv_ref[at, 2 * width :], grad)
                part = contract_cols(kv_vmem[window, :width], query) * scale
                key = start + lax.broadcasted_iota(jnp.int32, part.shape, 0)
                part = jnp.where((key >= lo) & (key < hi), part - log_total, -1e30)
                prob = jnp.exp(part)
                slope = contract_cols(kv_vmem[window, width:], grad)
                centre = jnp.sum(own_prob * own_slope, axis=0, keepdims=True)
                centre = centre + jnp.sum(prob * slope, axis=0, keepdims=True)
                own_low = own_prob * (own_slope - pull * (own_log + ent) - centre)
                own_low = own_low.astype(BF16)
                low_grad = (prob * (slope - pull * (part + ent) - centre)).astype(BF16)
                grad_query = contract_rows(own_low, own_key)
                grad_query = grad_query + contract_rows(low_grad, kv_vmem[window, :width])
                own_out[at, width : 2 * width] = (product(own_low, query) * scale).astype(BF16)
                own_out[at, 2 * width :] = product(own_prob.astype(BF16), grad).astype(BF16)
                once = jnp.where(repeated, 0.0, 1.0)
                totals[window, :width] += product(low_grad, query) * (scale * once)
                totals[window, width:] += product(prob.astype(BF16), grad) * once
                own_out[at, :width] = (take_diagonal(grad_query, heads) * scale).astype(BF16)

        def long(image):
            at = image_rows(image)
            base = slot_ref[image] * LEN
            lo = low_ref[image]
            hi = high_ref[image]
            pull = weight_ref[image]
            first = lo // KEY_BLOCK
            last = (hi + KEY_BLOCK - 1) // KEY_BLOCK
            query = block_diagonal(qkv_ref[at, :width], heads)
            grad = block_diagonal(grad_ref[at, :], heads)
            log_total = lse_ref[image]
            ent = ent_ref[image]
            own_key = qkv_ref[at, width : 2 * width]
            own_log = contract_cols(own_key, query) * scale - log_total
            own_prob = jnp.exp(own_log)
            own_slope = contract_cols(qkv_ref[at, 2 * width :], grad)
            centre = jnp.sum(own_prob * own_slope, axis=0, keepdims=True)
            own_slope = own_slope - pull * (own_log + ent)

            def first_pass(block, centre):
                row = pl.multiple_of(base + block * KEY_BLOCK, KEY_BLOCK)
                to = pl.multiple_of((block - first) * KEY_BLOCK, KEY_BLOCK)
                part = contract_cols(kv_vmem[pl.ds(row, KEY_BLOCK), :width], query) * scale
                key = block * KEY_BLOCK + lax.broadcasted_iota(jnp.int32, part.shape, 0)
                part = jnp.where((key >= lo) & (key < hi), part - log_total, -1e30)
                prob = jnp.exp(part)
                slope = contract_cols(kv_vmem[pl.ds(row, KEY_BLOCK), width:], grad)
                probs[pl.ds(to, KEY_BLOCK), :] = prob
                slopes[pl.ds(to, KEY_BLOCK), :] = slope - pull * (part + ent)
                return centre + jnp.sum(prob * slope, axis=0, keepdims=True)

            centre = lax.fori_loop(first, last, first_pass, centre)
            own_low = (own_prob * (own_slope - centre)).astype(BF16)
            grad_query = contract_rows(own_low, own_key)
            own_out[at, width : 2 * width] = (product(own_low, query) * scale).astype(BF16)
            own_out[at, 2 * width :] = product(own_prob.astype(BF16), grad).astype(BF16)

            def second_pass(block, grad_query):
                row = pl.multiple_of(base + block * KEY_BLOCK, KEY_BLOCK)
                to = pl.multiple_of((block - first) * KEY_BLOCK, KEY_BLOCK)
                prob = probs[pl.ds(to, KEY_BLOCK), :]
                low_grad = (prob * (slopes[pl.ds(to, KEY_BLOCK), :] - centre)).astype(BF16)
                totals[pl.ds(row, KEY_BLOCK), :width] += product(low_grad, query) * scale
                totals[pl.ds(row, KEY_BLOCK), width:] += product(prob.astype(BF16), grad)
                return grad_query + contract_rows(
                    low_grad, kv_vmem[pl.ds(row, KEY_BLOCK), :width]
                )

            grad_query = lax.fori_loop(first, last, second_pass, grad_query)
            own_out[at, :width] = (take_diagonal(grad_query, heads) * scale).astype(BF16)

        each_image(listed_ref, images, short, long)
        key_out[...] = totals[...].astype(BF16)

    scalar = pl.BlockSpec(memory_space=pltpu.SMEM)
    vmem = pl.BlockSpec(memory_space=pltpu.VMEM)
    return pl.pallas_call(
        body,
        out_shape=(
            jax.ShapeDtypeStruct((images * LATENTS, 3 * width), BF16),
            jax.ShapeDtypeStruct((keys, 2 * width), BF16),
        ),
        in_specs=[scalar] * 5 + [pl.BlockSpec(memory_space=pl.ANY)] * count + [vmem] * 4,
        out_specs=(vmem, vmem),
        scratch_shapes=[
            pltpu.VMEM((keys, 2 * width), BF16),
            pltpu.VMEM((LEN, rows), F32),
            pltpu.VMEM((LEN, rows), F32),
            pltpu.VMEM((keys, 2 * width), F32),
            pltpu.SemaphoreType.DMA((count,)),
        ],
        compiler_params=pltpu.CompilerParams(vmem_limit_bytes=56 << 20),
        cost_estimate=cost(0.5),
        name="attention_backward",
    )(listed, slot, low, high, weight, *kv_slots, latent_qkv, grad_out, lse, entropy)


ROW_BLOCK = 256


def call(body, grid, inputs, outputs, name, time=5.0, scratch=()):
    return pl.pallas_call(
        body,
        out_shape=tuple(jax.ShapeDtypeStruct(shape, dtype) for shape, dtype, _ in outputs),
        grid=(grid,),
        in_specs=[spec for _, spec in inputs],
        out_specs=tuple(spec for _, _, spec in outputs),
        scratch_shapes=list(scratch),
        compiler_params=pltpu.CompilerParams(
            dimension_semantics=("arbitrary",), vmem_limit_bytes=56 << 20
        ),
        cost_estimate=cost(time),
        name=name,
    )(*[value for value, _ in inputs])


def by_rows(width, move=lambda i: i, size=ROW_BLOCK):
    return pl.BlockSpec((size, width), lambda i: (move(i), 0))


def whole(value):
    return pl.BlockSpec(value.shape, lambda i: (0,) * value.ndim, pipeline_mode=pl.Buffered(1))


def stacked(values):
    steps = values[0].shape[0] // ROW_BLOCK
    return [
        (value, by_rows(value.shape[1], lambda i, k=k: jnp.clip(i - k * steps, 0, steps - 1)))
        for k, value in enumerate(values)
    ]


def stacked_rows(refs, values):
    steps = values[0].shape[0] // ROW_BLOCK
    rows = refs[0][...]
    for k in range(1, len(values)):
        rows = jnp.where(pl.program_id(0) >= k * steps, refs[k][...], rows)
    return rows


def low_half(i):
    return jnp.minimum(i, 1)


def high_half(i):
    return jnp.maximum(i - 2, 0)


def pair_inputs(pair, rest):
    return [(pair, by_rows(pair.shape[1], low_half)), (rest, by_rows(rest.shape[1], high_half))]


def pick(pair_ref, rest_ref):
    return jnp.where(pl.program_id(0) < 2, pair_ref[...], rest_ref[...])


def put_halves(low_ref, high_ref, value):
    @pl.when(pl.program_id(0) < 2)
    def _():
        low_ref[...] = value

    @pl.when(pl.program_id(0) >= 2)
    def _():
        high_ref[...] = value


def half_outputs(width):
    return [
        ((2 * ROW_BLOCK, width), BF16, by_rows(width, low_half)),
        ((2 * ROW_BLOCK, width), BF16, by_rows(width, high_half)),
    ]


def add_up(ref, value):
    total = jnp.sum(value, axis=0, keepdims=True)

    @pl.when(pl.program_id(0) == 0)
    def _():
        ref[...] = total

    @pl.when(pl.program_id(0) > 0)
    def _():
        ref[...] += total


def sum_output(width):
    return ((1, width), F32, pl.BlockSpec((1, width), lambda i: (0, 0)))


def norm_project(rows, gain, bias, weights, time=7.5, count=None):
    width, wide = rows[0].shape[1], weights.shape[1]
    count = count or sum(part.shape[0] for part in rows)

    def body(*refs):
        value = stacked_rows(refs, rows)
        gain_ref, bias_ref, weight_ref, out_ref, norm_ref = refs[len(rows) :]
        norm = normalize(value.astype(F32), gain_ref[...], bias_ref[...])[0].astype(BF16)
        norm_ref[...] = norm
        out_ref[...] = product(norm, weight_ref[...]).astype(BF16)

    return call(
        body,
        count // ROW_BLOCK,
        stacked(rows) + [(gain, whole(gain)), (bias, whole(bias)), (weights, whole(weights))],
        [((count, wide), BF16, by_rows(wide)), ((count, width), BF16, by_rows(width))],
        "norm_project",
        time,
    )


def cotangent_down(rows, weights):
    wide = weights.shape[0]

    def body(*refs):
        refs[-1][...] = contract_cols(stacked_rows(refs, rows), refs[-2][...])

    return call(
        body,
        4,
        stacked(rows) + [(weights, whole(weights))],
        [((4 * ROW_BLOCK, wide), F32, by_rows(wide))],
        "cotangent_down",
        10.0,
    )[0]


def feed_forward(attended, near_weights, far_weights, latent_rows, pulled, w_up, gain, bias):
    width = attended[0].shape[1]
    dim = w_up.shape[0]
    wide = w_up.shape[1]

    def body(*refs):
        own, near, across, beyond, first_ref, far_ref, far_rest, *lat_refs = refs[:11]
        pulled_ref, up_ref, gain_ref, bias_ref, middle_ref, hat_ref, inv_ref = refs[11:18]
        ffn_ref, hidden_ref, grad_ref, low_ref, high_ref, second_ref = refs[18:]

        @pl.when(pl.program_id(0) == 0)
        def _():
            second_ref[:width, :] = far_ref[...]
            second_ref[width:, :] = far_rest[...]

        rows = stacked_rows(lat_refs, latent_rows).astype(F32)
        rows = rows + product(jnp.concatenate([own[...], near[...]], axis=1), first_ref[...])
        rows = rows + product(jnp.concatenate([across[...], beyond[...]], axis=1), second_ref[...])

        @pl.when(pl.program_id(0) == 0)
        def _():
            middle_ref[...] = rows

        norm, hat_ref[...], inv_ref[...] = normalize(rows, gain_ref[...], bias_ref[...])
        norm = norm.astype(BF16)
        ffn_ref[...] = norm
        step = wide // 3
        for i in range(3):
            at = slice(i * step, (i + 1) * step)
            activated, slope = gelu_parts(product(norm, up_ref[:, at]))
            hidden_ref[:, at] = activated.astype(BF16)
            grad_ref[:, at] = (pulled_ref[:, at] * slope).astype(BF16)
        back = contract_cols(grad_ref[...], up_ref[...]).astype(BF16)
        put_halves(low_ref, high_ref, back)

    count = 4 * ROW_BLOCK
    return call(
        body,
        4,
        [
            (attended[0], by_rows(width)),
            (attended[1], by_rows(width, lambda i: i ^ 2)),
            (attended[2], by_rows(width, lambda i: i ^ 1)),
            (attended[3], by_rows(width, lambda i: i ^ 3)),
            (near_weights, whole(near_weights)),
            (far_weights[0], whole(far_weights[0])),
            (far_weights[1], whole(far_weights[1])),
        ]
        + stacked(latent_rows)
        + [
            (pulled, by_rows(wide)),
            (w_up, whole(w_up)),
            (gain, whole(gain)),
            (bias, whole(bias)),
        ],
        [
            ((ROW_BLOCK, dim), F32, by_rows(dim, lambda i: 0)),
            ((count, dim), F32, by_rows(dim)),
            ((count, 1), F32, by_rows(1)),
            ((count, dim), BF16, by_rows(dim)),
            ((count, wide), BF16, by_rows(wide)),
            ((count, wide), BF16, by_rows(wide)),
        ]
        + half_outputs(dim),
        "feed_forward",
        27.0,
        scratch=[pltpu.VMEM((2 * width, dim), BF16)],
    )


def part(value, rows=None, at=0, columns=slice(None)):
    return (value, value.shape[0] if rows is None else rows, at, columns)


def grad_halves(side, pairs, name):
    half = pairs[0][0].shape[1] // 2
    inputs = []
    for left, rights in pairs:
        inputs.append(
            (
                left,
                pl.BlockSpec(
                    (left.shape[0], half),
                    lambda i, x: (0, (i + 1 + x[0]) % 2),
                ),
            )
        )
        for value, rows, at, _ in rights:
            spec = pl.BlockSpec(
                (rows, value.shape[1]), lambda i, x, at=at: (at, 0), pipeline_mode=pl.Buffered(1)
            )
            inputs.append((value, spec))
    value, _, _, columns = pairs[0][1][0]
    wide = len(range(*columns.indices(value.shape[1])))

    def body(x_ref, *refs):
        total = None
        index = 0
        for left, rights in pairs:
            left_ref = refs[index]
            row = 0
            for i, (_, rows, _, columns) in enumerate(rights):
                value = contract_rows(
                    left_ref[row : row + rows, :], refs[index + 1 + i][:, columns]
                )
                row += rows
                total = value if total is None else total + value
            index += 1 + len(rights)
        put_sides(refs[-2], refs[-1], total.astype(BF16))

    return side_call(body, side, inputs, half, wide, name)


def put_sides(other_ref, mine_ref, value):
    @pl.when(pl.program_id(0) == 0)
    def _():
        other_ref[...] = value

    @pl.when(pl.program_id(0) == 1)
    def _():
        mine_ref[...] = value


def side_call(body, side, inputs, half, wide, name):
    out = pl.BlockSpec((half, wide), lambda i, x: (0, 0))
    return pl.pallas_call(
        body,
        out_shape=(jax.ShapeDtypeStruct((half, wide), BF16),) * 2,
        grid_spec=pltpu.PrefetchScalarGridSpec(
            num_scalar_prefetch=1,
            grid=(2,),
            in_specs=[spec for _, spec in inputs],
            out_specs=(out, out),
        ),
        compiler_params=pltpu.CompilerParams(
            dimension_semantics=("arbitrary",), vmem_limit_bytes=56 << 20
        ),
        cost_estimate=cost(0.5),
        name=name,
    )(side, *[value for value, _ in inputs])


def late_grads(side, latent_back, early_low, late_low, attended, grad_branch):
    width = attended.shape[1]
    wide = grad_branch.shape[1]

    def body(x_ref, back_ref, early_ref, late_ref, attended_ref, branch_ref, other_ref, mine_ref):
        size = early_low.shape[0] // 2
        which = (pl.program_id(0) + 1 + x_ref[0]) % 2

        @pl.when(which == 0)
        def _():
            value = jnp.zeros((width, wide), F32)
            for i, low_ref in enumerate((early_ref, late_ref, early_ref, late_ref)):
                value = value + contract_rows(
                    back_ref[i * size : (i + 1) * size, :],
                    low_ref[i // 2 * size : (i // 2 + 1) * size, :],
                )
            put_sides(other_ref, mine_ref, value.astype(BF16))

        @pl.when(which == 1)
        def _():
            value = contract_rows(attended_ref[...], branch_ref[...]).astype(BF16)
            put_sides(other_ref, mine_ref, value)

    inputs = [
        (
            value,
            pl.BlockSpec(
                (value.shape[0], min(value.shape[1], size)),
                lambda i, x: (0, 0),
                pipeline_mode=pl.Buffered(1),
            ),
        )
        for value, size in (
            (latent_back, width),
            (early_low, wide),
            (late_low, wide),
            (attended, width),
            (grad_branch, wide),
        )
    ]
    return side_call(body, side, inputs, width, wide, "late_grads")


def join_rows(place, parts, splits):
    size = parts[0].shape[0]
    count = len(parts)

    def body(place_ref, *refs):
        step = pl.program_id(0)
        for i in range(count):

            @pl.when(step == i)
            def _():
                for (first, last), out_ref in zip(splits, refs[count:]):
                    out_ref[...] = refs[i][:, first:last].astype(F32)

    inputs = [
        pl.BlockSpec(value.shape, lambda i, p: (0, 0), pipeline_mode=pl.Buffered(1))
        for value in parts
    ]
    return pl.pallas_call(
        body,
        out_shape=tuple(
            jax.ShapeDtypeStruct((count * size, last - first), F32) for first, last in splits
        ),
        grid_spec=pltpu.PrefetchScalarGridSpec(
            num_scalar_prefetch=1,
            grid=(count,),
            in_specs=inputs,
            out_specs=tuple(
                pl.BlockSpec((size, last - first), lambda i, p: (i ^ p[0], 0))
                for first, last in splits
            ),
        ),
        compiler_params=pltpu.CompilerParams(
            dimension_semantics=("arbitrary",), vmem_limit_bytes=56 << 20
        ),
        cost_estimate=cost(0.5),
        name="join_rows",
    )(place, *parts)


def join_late(place, parts):
    size, dim = parts[0].shape

    def body(place_ref, own_ref, pair_ref, side_ref, last_ref, query_ref, out_ref):
        odd = place_ref[0] % 2 == 1
        first = place_ref[0] < 2

        def rows(low_ref, high_ref):
            low, high = low_ref[...], high_ref[...]
            return jnp.concatenate(
                [jnp.where(odd, high, low), jnp.where(odd, low, high)], axis=0
            ).astype(F32)

        mine, other = rows(own_ref, pair_ref), rows(side_ref, last_ref)
        query_ref[...] = jnp.where(first, mine, other).T
        out_ref[...] = jnp.where(first, other, mine)

    spec = pl.BlockSpec((size, 384), lambda i, p: (0, i))
    return pl.pallas_call(
        body,
        out_shape=(
            jax.ShapeDtypeStruct((dim, 2 * size), F32),
            jax.ShapeDtypeStruct((2 * size, dim), F32),
        ),
        grid_spec=pltpu.PrefetchScalarGridSpec(
            num_scalar_prefetch=1,
            grid=(dim // 384,),
            in_specs=[spec] * 4,
            out_specs=(
                pl.BlockSpec((384, 2 * size), lambda i, p: (i, 0)),
                pl.BlockSpec((2 * size, 384), lambda i, p: (0, i)),
            ),
        ),
        compiler_params=pltpu.CompilerParams(dimension_semantics=("arbitrary",)),
        cost_estimate=cost(0.5),
        name="join_late",
    )(place, *parts)


def project_halves(rows, weights, transposed, name):
    wide = weights.shape[0] if transposed else weights.shape[1]

    def body(rows_ref, weight_ref, low_ref, high_ref):
        if transposed:
            out = contract_cols(rows_ref[...], weight_ref[...])
        else:
            out = product(rows_ref[...], weight_ref[...])
        put_halves(low_ref, high_ref, out.astype(BF16))

    return call(
        body,
        4,
        [(rows, by_rows(rows.shape[1])), (weights, whole(weights))],
        half_outputs(wide),
        name,
        0.5,
    )


def project_slot(rows, slot, weights, added=()):
    wide = weights.shape[0]
    blocks_in = LEN // ROW_BLOCK

    def body(rows_ref, weight_ref, *refs):
        out = contract_cols(rows_ref[...], weight_ref[...])
        if added:
            out = out + stacked_rows(refs, added).astype(F32)
        refs[-1][...] = out.astype(BF16)

    return call(
        body,
        blocks_in,
        [
            (rows, by_rows(rows.shape[1], lambda i: i + slot * blocks_in)),
            (weights, whole(weights)),
        ]
        + (stacked(added) if added else []),
        [((LEN, wide), BF16, by_rows(wide))],
        "project_slot",
        0.5,
    )[0]


def middle_back(grads, hat, inv, cotangents, gain, w_out):
    dim = hat.shape[1]
    width = w_out.shape[0]

    def body(*refs):
        grad_ref, third_ref, fourth_ref, hat_ref, inv_ref, *cot_refs = refs[:9]
        gain_ref, out_ref, branch_ref, own_ref, attended_ref, gain_sum, bias_sum = refs[9:]
        step = pl.program_id(0)
        grad = jnp.where(step == 2, third_ref[...], fourth_ref[...])
        grad = jnp.where(step < 2, grad_ref[...], grad).astype(F32)
        hat, inv = hat_ref[...], inv_ref[...]
        weighted = grad * gain_ref[...]
        moved = grad * hat
        first_mean = jnp.mean(weighted, axis=-1, keepdims=True)
        second_mean = jnp.mean(weighted * hat, axis=-1, keepdims=True)
        value = stacked_rows(cot_refs, cotangents).astype(F32) + inv * (
            weighted - first_mean - hat * second_mean
        )
        low = value.astype(BF16)
        branch_ref[...] = low
        attended_ref[...] = contract_cols(low, out_ref[...]).astype(BF16)
        add_up(gain_sum, moved)
        add_up(bias_sum, grad)

        @pl.when(pl.program_id(0) == 0)
        def _():
            own_ref[...] = value

    count = 4 * ROW_BLOCK
    return call(
        body,
        4,
        [(grads[0], by_rows(dim, low_half))]
        + [(grad, whole(grad)) for grad in grads[1:]]
        + [(hat, by_rows(dim)), (inv, by_rows(1))]
        + stacked(cotangents)
        + [(gain, whole(gain)), (w_out, whole(w_out))],
        [
            ((count, dim), BF16, by_rows(dim)),
            ((ROW_BLOCK, dim), F32, by_rows(dim, lambda i: 0)),
            ((count, width), BF16, by_rows(width)),
            sum_output(dim),
            sum_output(dim),
        ],
        "middle_back",
        0.5,
    )


def norm_back(near, far, rows, gain, bias, added=None):
    dim = rows.shape[1]
    extra = [] if added is None else [(added, by_rows(dim))]

    def body(*refs):
        near_ref, far_ref, rows_ref, gain_ref, bias_ref = refs[:5]
        out_ref, gain_sum, bias_sum = refs[-3:]
        grad = near_ref[...].astype(F32) + far_ref[...].astype(F32)
        _, hat, inv = normalize(rows_ref[...].astype(F32), gain_ref[...], bias_ref[...])
        weighted = grad * gain_ref[...]
        first_mean = jnp.mean(weighted, axis=-1, keepdims=True)
        second_mean = jnp.mean(weighted * hat, axis=-1, keepdims=True)
        value = inv * (weighted - first_mean - hat * second_mean)
        if extra:
            value = refs[5][...] + value
        out_ref[...] = value.astype(BF16)
        add_up(gain_sum, grad * hat)
        add_up(bias_sum, grad)

    return call(
        body,
        rows.shape[0] // ROW_BLOCK,
        [(near, by_rows(dim)), (far, by_rows(dim)), (rows, by_rows(dim))]
        + [(gain, whole(gain)), (bias, whole(bias))]
        + extra,
        [(rows.shape, BF16, by_rows(dim)), sum_output(dim), sum_output(dim)],
        "norm_back",
        0.5,
    )


def swap_head(value, bit):
    size = lax.axis_size("head")
    return lax.ppermute(value, "head", [(i, i ^ bit) for i in range(size)])


def swap_seq(value, bit):
    size = lax.axis_size("seq")
    return lax.ppermute(value, "seq", [(i, i ^ bit) for i in range(size)])


def sum_seq(value):
    size = lax.axis_size("seq")
    bit = 1
    while bit < size:
        value = value + swap_seq(value, bit)
        bit *= 2
    return value


def sum_head(value):
    size = lax.axis_size("head")
    bit = 1
    while bit < size:
        value = value + swap_head(value, bit)
        bit *= 2
    return value


OVER_Z = (False, False, True, False)


class Values:
    pass


class Order:
    def __init__(self):
        self.last = None

    def __call__(self, step, *values):
        if self.last is not None:
            *values, _ = lax.optimization_barrier((*values, self.last))
        out = step(*values)
        self.last = tuple(out) if isinstance(out, (tuple, list)) else out
        return out

    def gate(self, value):
        return lax.optimization_barrier((value, self.last))[0]

    def pin(self, value):
        self.last = self.gate(value)
        return self.last


class SeqSum:
    def __init__(self, order, halves, over_z):
        other, self.mine = halves
        self.order = order
        self.over_z = over_z
        self.moving = swap_seq(other, 1)

    def split(self):
        odd = lax.axis_index("seq") // 2 % 2
        quarter = self.mine.shape[0] // 2

        def run(mine, moving):
            total = mine + moving
            return [
                lax.dynamic_slice_in_dim(total, which * quarter, quarter, axis=0)
                for which in (1 - odd, odd)
            ]

        other, self.mine = self.order(run, self.mine, self.moving)
        self.moving = swap_seq(other, 2)

    def across(self):
        self.mine = self.order(lambda v, r: v + r, self.mine, self.moving)
        self.moving = swap_seq(self.mine, 4)

    def spread(self):
        self.mine = self.order(lambda v, r: v + r, self.mine, self.moving)
        self.side = swap_seq(self.mine, 1)
        self.pair = swap_seq(self.mine, 2)

    def corner(self):
        if self.over_z:
            self.side = self.order.pin(self.side)
            self.last = swap_seq(self.side, 2)
        else:
            self.pair = self.order.pin(self.pair)
            self.last = swap_seq(self.pair, 1)

    def pieces(self):
        return [self.mine, self.pair, self.side, self.last]


def blocks(value, count):
    size = value.shape[0] // count
    return [value[i * size : (i + 1) * size] for i in range(count)]


def shards_quad(
    media,
    media_ids,
    image_seq,
    image_valid,
    latents,
    w_query,
    w_key,
    w_value,
    w_out,
    w_up,
    w_down,
    media_gain,
    media_bias,
    latent_gain,
    latent_bias,
    ffn_gain,
    ffn_bias,
    cotangent,
):
    seq_index = lax.axis_index("seq")
    head_index = lax.axis_index("head")
    seq_size = lax.axis_size("seq")
    images = image_seq.shape[0]
    sequences = media_ids.shape[0] // LEN
    own_rows = latents.shape[0]
    width = w_query.shape[1]
    dim = media.shape[1]
    order = Order()
    media_gain, media_bias, latent_gain, latent_bias, ffn_gain, ffn_bias = (
        value.reshape(1, dim)
        for value in (media_gain, media_bias, latent_gain, latent_bias, ffn_gain, ffn_bias)
    )

    slots = jnp.array([0, 2, 1, 3], jnp.int32)
    per_device = images // 4
    which = ((slots ^ head_index)[:, None] * per_device + jnp.arange(per_device)[None, :]).reshape(-1)
    owners = seq_index * images + which
    local_seq = jnp.take(image_seq, which) - seq_index * sequences
    valid_float = jnp.take(image_valid, which).astype(F32)
    matches = media_ids[None, :] == owners[:, None]
    place = jnp.arange(media_ids.shape[0], dtype=jnp.int32)[None, :]
    run = jnp.sum(matches.astype(jnp.int32), axis=1)
    start = jnp.min(jnp.where(matches, place, media_ids.shape[0]), axis=1)
    low = jnp.where(run > 0, start - local_seq * LEN, 0)
    high = low + run
    slot = local_seq ^ head_index

    share = width // seq_size
    raw_across = swap_head(media, 2)
    out_piece = lax.dynamic_slice_in_dim(w_out, seq_index * share, share, axis=0)
    out_piece = swap_head(out_piece, 2)
    raw_near = swap_head(media, 1)
    latents_near = swap_head(latents, 1)
    out_near = swap_head(w_out, 1)

    cotangent_near = swap_head(cotangent, 1)
    w_kv = jnp.concatenate([w_key, w_value], axis=1)
    w_qkv = jnp.concatenate([w_query, w_kv], axis=1)

    def media_step(rows, weights):
        return norm_project([rows], media_gain, media_bias, weights, 0.3, LEN)

    def stack(*values):
        return jnp.concatenate(values, axis=0)

    def add(left, right):
        return left + right

    def latent_step(own, other, weights):
        return norm_project([own, other], latent_gain, latent_bias, weights, 0.3)

    def forward(lists, kv_slots, latent_qkv, offset, before):
        count = len(kv_slots)
        return order(
            lambda *v: attention_forward(
                *v[:4], v[4 : 4 + count], v[4 + count], offset, v[5 + count :] or None, time=1.0
            ),
            lists,
            slot,
            low,
            high,
            *kv_slots,
            latent_qkv,
            *before,
        )

    count = order(
        lambda v: jnp.broadcast_to(jnp.sum(v).reshape(1, 1), (8, 128)), valid_float
    )
    count_moved = swap_seq(count, 1)
    kv_own, norm_own = order(media_step, media, w_kv)
    count = order(add, count, count_moved)
    count_moved = swap_seq(count, 2)
    latents_across = swap_head(order.gate(latents), 2)
    early_qkv, early_low = order(latent_step, latents, latents_near, w_qkv)
    count = order(add, count, count_moved)
    count_moved = swap_seq(count, 4)
    early = jnp.arange(images) // per_device % 2 == 0
    near_list, rest_list, full_list = order(
        lambda s, a, b: (
            list_images(early & (s < 2), a, b),
            list_images(jnp.logical_not(early & (s < 2)), a, b),
            list_images(s >= 0, a, b),
        ),
        slot,
        low,
        high,
    )
    kv_near, norm_near = order(media_step, raw_near, w_kv)
    outcome = forward(near_list, (kv_own, kv_near), early_qkv, 0, ())
    cotangent_across = swap_head(order.gate(cotangent), 2)
    out_first = order(stack, w_out, out_near)
    count = order(add, count, count_moved)
    penalty_weight, pen_scale = order(
        lambda v, c: (v * (4.0 * images * seq_size / c[0, 0]), 1.0 / (HEADS * LATENTS * c[0, 0])),
        valid_float,
        count,
    )
    raw_across = order.pin(raw_across)
    raw_beyond = swap_head(raw_across, 1)
    kv_across, norm_across = order(media_step, raw_across, w_kv)
    kv_beyond, norm_beyond = order(media_step, raw_beyond, w_kv)
    out_piece = order.pin(out_piece)
    out_far = lax.all_gather(out_piece, "seq", axis=0, tiled=True)
    kv_far = (kv_across, kv_beyond)
    latents_across = order.pin(latents_across)
    latents_beyond = swap_head(latents_across, 1)
    late_qkv, late_low = order(latent_step, latents_across, latents_beyond, w_qkv)

    def interleave(first, second):
        first, second = blocks(first, 2), blocks(second, 2)
        return stack(first[0], second[0], first[1], second[1])

    latent_qkv = order(interleave, early_qkv, late_qkv)
    attended, lse, entropy = forward(
        rest_list, (kv_own, kv_near, *kv_far), latent_qkv, 0, outcome
    )
    attended_across = swap_head(attended, 2)
    attended_near = swap_head(attended, 1)
    cotangent_across = order.pin(cotangent_across)
    cotangent_beyond = swap_head(cotangent_across, 1)
    cotangents = (cotangent, cotangent_across, cotangent_near, cotangent_beyond)
    pulled = order(lambda *v: cotangent_down(v[:4], v[4]), *cotangents, w_down)
    out_far = order.pin(out_far)
    out_beyond = swap_head(out_far, 1)
    attended_across = order.gate(attended_across)
    attended_beyond = swap_head(attended_across, 1)
    middle, ffn_hat, ffn_inv, ffn_low, hidden, grad_before, lower, upper = order(
        lambda *v: feed_forward(v[:4], v[4], v[5:7], v[7:11], *v[11:], ffn_gain, ffn_bias),
        attended,
        attended_near,
        attended_across,
        attended_beyond,
        out_first,
        out_far,
        out_beyond,
        latents,
        latents_across,
        latents_near,
        latents_beyond,
        pulled,
        w_up,
    )
    side = (seq_index % 2).reshape(1)
    place = (seq_index % 2 * 2 + seq_index // 2 % 2).reshape(1)
    v = Values()
    v.upper = swap_head(upper, 1)

    def lowadd():
        v.lower = order(add, lower, v.upper)
        v.Y = swap_head(v.lower, 2)

    def sum_steps(grads, over_z):
        made = []

        def start():
            made.append(SeqSum(order, grads(), over_z))

        return (
            start,
            lambda: made[0].split(),
            lambda: made[0].across(),
            lambda: made[0].spread(),
            lambda: made[0].corner(),
            lambda: made[0].pieces(),
        )

    def down_grads():
        return order(
            lambda x, h, *g: grad_halves(x, [(h, [part(one) for one in g])], "down_grad"),
            side,
            hidden,
            *cotangents,
        )

    def up_grads():
        return order(
            lambda x, h, g: grad_halves(x, [(h, [part(g)])], "up_grad"),
            side,
            ffn_low,
            grad_before,
        )

    norms = (norm_own, norm_near, norm_across, norm_beyond)

    def key_pairs(
        x, own, near, across, beyond, back, early_rows, late_rows, latent_part
    ):
        pairs = [
            (rows, [part(back, LEN, i)]) for i, rows in enumerate((own, near, across, beyond))
        ]
        for rows, at in ((early_rows, 0), (late_rows, 1)):
            pairs.append(
                (
                    rows,
                    [
                        part(latent_part, own_rows, at + 2 * i, slice(width, None))
                        for i in range(2)
                    ],
                )
            )
        return grad_halves(x, pairs, "key_grad")

    def key_grads():
        return order(
            key_pairs, side, *norms, v.kv_back, early_low, late_low, v.latent_back
        )

    d, d_1, d_2, d_3, d_4, down_parts = sum_steps(down_grads, OVER_Z[0])
    u, u_1, u_2, u_3, u_4, up_parts = sum_steps(up_grads, OVER_Z[1])
    k, k_1, k_2, k_3, k_4, key_parts = sum_steps(key_grads, OVER_Z[2])
    l, l_1, l_2, l_3, l_4, late_parts = sum_steps(
        lambda: order(
            late_grads, side, v.latent_back, early_low, late_low, attended, v.grad_branch
        ),
        OVER_Z[3],
    )

    def branch():
        v.branch, v.branch_upper = order(
            lambda h, w: project_halves(h, w, False, "branch"), hidden, w_down
        )
        v.BC = swap_head(v.branch_upper, 1)

    def bradd():
        v.branch = order(add, v.branch, v.BC)
        v.BY = swap_head(v.branch[own_rows:], 2)

    def res():
        v.result = order(
            lambda m, b, r: (m + b[:own_rows].astype(F32) + r.astype(F32)).astype(BF16),
            middle,
            v.branch,
            v.BY,
        )

    def gpair():
        v.pair = order(
            lambda a, r: a + jnp.concatenate(blocks(r, 2)[::-1], axis=0), v.lower, v.Y
        )
        v.G = [swap_head(piece, 1) for piece in blocks(v.pair, 2)]

    def mback():
        out = order(
            lambda *a: middle_back(a[:3], a[3], a[4], a[5:9], ffn_gain, a[9]),
            v.pair,
            *v.G,
            ffn_hat,
            ffn_inv,
            *cotangents,
            w_out,
        )
        v.grad_branch, v.grad_middle, v.grad_attended = out[:3]
        v.ffn_sums = out[3:]

    def attb():
        v.latent_back, v.kv_back = order(
            lambda *a: attention_backward(*a[:5], a[5:9], *a[9:]),
            full_list,
            slot,
            low,
            high,
            penalty_weight,
            kv_own,
            kv_near,
            *kv_far,
            latent_qkv,
            v.grad_attended,
            lse,
            entropy,
        )

    def swap_pieces(value):
        return [swap_head(piece, 1) for piece in blocks(value, 2)]

    def pb():
        v.K1 = swap_pieces(order(lambda a, w: project_slot(a, 3, w), v.kv_back, w_kv))

    def pa():
        v.MF = swap_head(
            order(lambda a, w, *r: project_slot(a, 2, w, r), v.kv_back, w_kv, *v.K1), 2
        )

    def pn():
        v.K2 = swap_pieces(order(lambda a, w: project_slot(a, 1, w), v.kv_back, w_kv))

    def po():
        v.media_near = order(
            lambda a, w, *r: project_slot(a, 0, w, r), v.kv_back, w_kv, *v.K2
        )

    def lb():
        v.latent_lower, upper = order(
            lambda a, w: project_halves(a, w, True, "latent_back"), v.latent_back, w_qkv
        )
        v.LC = swap_head(upper, 1)

    def ladd():
        v.latent_lower = order(add, v.latent_lower, v.LC)
        v.LY = swap_head(v.latent_lower[own_rows:], 2)

    def nbm():
        v.media_grad, *v.media_sums = order(
            lambda *a: norm_back(*a, media_gain, media_bias), v.media_near, v.MF, media
        )

    def nbl():
        v.latents_grad, *v.latent_sums = order(
            lambda *a: norm_back(*a[:3], latent_gain, latent_bias, a[3]),
            v.latent_lower,
            v.LY,
            latents,
            v.grad_middle,
        )

    def s0():
        entropy_local = jnp.sum(entropy.reshape(images, -1) * valid_float[:, None])
        part_of = 1.0 / lax.axis_size("head")
        v.sums = order(
            stack,
            *v.media_sums,
            *v.latent_sums,
            *[value * part_of for value in v.ffn_sums],
            jnp.broadcast_to(entropy_local, (2, dim)),
        )
        v.moved = swap_head(v.sums, 1)

    def add_moved():
        v.sums = order(add, v.sums, v.moved)

    def s1():
        add_moved()
        v.moved = swap_head(v.sums, 2)

    def s2():
        add_moved()
        v.moved = swap_seq(v.sums, 1)

    def s3():
        add_moved()
        v.moved = swap_seq(v.sums, 2)

    def s4():
        add_moved()
        v.moved = swap_seq(v.sums, 4)

    s5 = add_moved

    def d_5():
        parts = down_parts()
        v.down = order(lambda p, *a: join_rows(p, a, ((0, dim),))[0], place, *parts)

    def u_5():
        parts = up_parts()
        v.up = order(lambda p, *a: join_rows(p, a, ((0, dim),))[0], place, *parts)

    def k_5():
        parts = key_parts()
        v.key, v.value = order(
            lambda p, *a: join_rows(p, a, ((0, width), (width, 2 * width))), place, *parts
        )

    def l_5():
        v.query, v.out = order(lambda p, *a: join_late(p, a), place, *late_parts())

    steps = (
        d, lowadd, u, gpair, mback, d_1, attb, d_2, lb, pb, u_1, l, k, d_3, u_2, l_1, ladd,
        pa, k_1, d_4, branch, nbl, pn, u_3, l_2, d_5, k_2, bradd, po, u_4, nbm, s0, l_3, s1,
        k_3, s2, u_5, l_4, s3, k_4, k_5, s4, res, l_5, s5,
    )
    for step in steps:
        step()
    sums = v.sums
    return (
        v.result,
        sums[6, 0] * pen_scale,
        v.media_grad,
        v.latents_grad,
        v.query,
        v.key,
        v.value,
        v.out,
        v.up,
        v.down,
        sums[0],
        sums[1],
        sums[2],
        sums[3],
        sums[4],
        sums[5],
    )


def shards_any(
    media,
    media_ids,
    image_seq,
    image_valid,
    latents,
    w_query,
    w_key,
    w_value,
    w_out,
    w_up,
    w_down,
    media_gain,
    media_bias,
    latent_gain,
    latent_bias,
    ffn_gain,
    ffn_bias,
    cotangent,
):
    seq_index = lax.axis_index("seq")
    head_index = lax.axis_index("head")
    images = image_seq.shape[0]
    sequences = media_ids.shape[0] // LEN
    own_rows = latents.shape[0]
    inner_width = w_query.shape[1]
    seq_size = lax.axis_size("seq")
    valid_float = image_valid.astype(F32)

    media_norm, media_hat, media_inv = normalize(media.astype(F32), media_gain, media_bias)
    latent_rows = lax.all_gather(latents, "head", axis=0, tiled=True)
    media_all = lax.all_gather(media_norm.astype(BF16), "head", axis=0, tiled=True)
    grad_all = lax.all_gather(cotangent, "head", axis=0, tiled=True)
    latent_float = latent_rows.astype(F32)
    latent_norm, latent_hat, latent_inv = normalize(latent_float, latent_gain, latent_bias)
    latent_low = latent_norm.astype(BF16)

    count_all = jnp.sum(valid_float).reshape(1, 1)
    count_all = sum_seq(jnp.broadcast_to(count_all, (8, 128)))[0, 0]
    pen_scale = 1.0 / (HEADS * LATENTS * count_all)
    weighted_scale = 4.0 * images * seq_size / count_all

    owners = seq_index * images + jnp.arange(images, dtype=jnp.int32)
    local_seq = image_seq - seq_index * sequences
    matches = media_ids[None, :] == owners[:, None]
    place = jnp.arange(media_ids.shape[0], dtype=jnp.int32)[None, :]
    run = jnp.sum(matches.astype(jnp.int32), axis=1)
    start = jnp.min(jnp.where(matches, place, media_ids.shape[0]), axis=1)
    low = jnp.where(run > 0, start - local_seq * LEN, 0)
    high = low + run
    slot = local_seq
    listed = list_images(jnp.full((images,), True), low, high)

    w_kv = jnp.concatenate([w_key, w_value], axis=1)
    w_qkv = jnp.concatenate([w_query, w_kv], axis=1)
    latent_qkv = product(latent_low, w_qkv).astype(BF16)
    kv_slots = [product(media_all, w_kv).astype(BF16)]
    attended, lse, entropy = attention_forward(listed, slot, low, high, kv_slots, latent_qkv)

    branch = lax.psum(product(attended, w_out).astype(BF16), "head").astype(F32)
    middle = latent_float + branch
    ffn_norm, ffn_hat, ffn_inv = normalize(middle, ffn_gain, ffn_bias)
    ffn_low = ffn_norm.astype(BF16)
    before_gelu = product(ffn_low, w_up)
    activated, gelu_slope = gelu_parts(before_gelu)
    hidden = activated.astype(BF16)
    grad_before = (contract_cols(grad_all, w_down) * gelu_slope).astype(BF16)
    grad_ffn_part = contract_cols(grad_before, w_up).astype(BF16)
    grad_ffn = lax.psum(grad_ffn_part, "head").astype(F32)
    down_grad = contract_rows(hidden, grad_all).astype(BF16)
    up_grad = contract_rows(ffn_low, grad_before).astype(BF16)
    up_grad, down_grad = lax.psum((up_grad, down_grad), "seq")

    ffn_branch = product(hidden, w_down).astype(BF16)
    ffn_branch = lax.psum_scatter(ffn_branch, "head", scatter_dimension=0, tiled=True)

    def own(value):
        return lax.dynamic_slice_in_dim(value, head_index * own_rows, own_rows, axis=0)

    result = (own(middle) + ffn_branch.astype(F32)).astype(BF16)

    middle_part, ffn_gain_part, ffn_bias_part = normalize_back(
        grad_ffn, ffn_hat, ffn_inv, ffn_gain
    )
    grad_middle = grad_all.astype(F32) + middle_part
    grad_branch = grad_middle.astype(BF16)
    grad_attended = contract_cols(grad_branch, w_out).astype(BF16)
    out_grad = contract_rows(attended, grad_branch)
    back = attention_backward(
        listed,
        slot,
        low,
        high,
        valid_float * weighted_scale,
        kv_slots,
        latent_qkv,
        grad_attended,
        lse,
        entropy,
    )
    latent_back, kv_back = back
    grad_media_norm = lax.psum_scatter(
        contract_cols(kv_back, w_kv).astype(BF16), "head", scatter_dimension=0, tiled=True
    ).astype(F32)
    grad_latent_part = contract_cols(latent_back, w_qkv).astype(BF16)
    grad_latent_norm = lax.psum_scatter(
        grad_latent_part, "head", scatter_dimension=0, tiled=True
    ).astype(F32)
    latent_grads = contract_rows(latent_low, latent_back)
    kv_grads = latent_grads[:, inner_width:] + contract_rows(media_all, kv_back)
    late = (
        latent_grads[:, :inner_width].astype(BF16),
        kv_grads.astype(BF16),
        out_grad.astype(BF16),
    )
    up_grad, down_grad, *late = lax.optimization_barrier((up_grad, down_grad) + late)
    query_grad, kv_grads, out_grad = lax.psum(tuple(late), "seq")

    media_rows_grad, media_gain_part, media_bias_part = normalize_back(
        grad_media_norm, media_hat, media_inv, media_gain
    )
    latent_part, latent_gain_part, latent_bias_part = normalize_back(
        grad_latent_norm, own(latent_hat), own(latent_inv), latent_gain
    )
    latents_grad = (own(grad_middle) + latent_part).astype(BF16)
    entropy_local = jnp.sum(entropy.reshape(images, -1) * valid_float[:, None])
    share = 1.0 / lax.axis_size("head")
    sums = jnp.stack(
        [
            media_gain_part,
            media_bias_part,
            latent_gain_part,
            latent_bias_part,
            ffn_gain_part * share,
            ffn_bias_part * share,
            jnp.broadcast_to(entropy_local, media_gain.shape),
            jnp.zeros_like(media_gain),
        ]
    )
    sums = sum_seq(sum_head(sums))
    return (
        result,
        sums[6, 0] * pen_scale,
        media_rows_grad.astype(BF16),
        latents_grad,
        query_grad.astype(F32),
        kv_grads[:, :inner_width].astype(F32),
        kv_grads[:, inner_width:].astype(F32),
        out_grad.astype(F32),
        up_grad.astype(F32),
        down_grad.astype(F32),
        sums[0],
        sums[1],
        sums[2],
        sums[3],
        sums[4],
        sums[5],
    )


def solution(mesh):
    rows = P(("seq", "head"), None)
    columns = P(None, "head")
    lines = P("head", None)
    quad = mesh.shape["head"] == 4 and mesh.shape["seq"] == 8
    return jax.shard_map(
        shards_quad if quad else shards_any,
        mesh=mesh,
        in_specs=(
            (rows, P("seq"), P("seq"), P("seq"), rows)
            + (columns, columns, columns, lines, columns, lines)
            + (P(),) * 6
            + (rows,)
        ),
        out_specs=(
            (rows, P(), rows, rows)
            + (columns, columns, columns, lines, columns, lines)
            + (P(),) * 6
        ),
        check_vma=False,
    )
```
